128 devices in a mesh: seq: 8 (over x, core), tp: 16 (over z, y).
Axes of the slice: x: 4, y: 4, z: 4, core: 2. Of those that a mesh axis runs over, the one named last changes fastest.
Arguments:
- tokens: bfloat16 [2048, 4096], P('seq', 'tp'), may hold values from -12 to 12
- norm_gain: float32 [2, 4096], replicated, may hold values from 0.5 to 1.5
- w_in: bfloat16 [2, 4096, 2, 8192], P(None, None, None, 'tp'), may hold values from -0.09375 to 0.09375
- w_low: bfloat16 [2, 4096, 288], P(None, 'tp'), may hold values from -0.09375 to 0.09375
- w_dt: bfloat16 [2, 256, 8192], P(None, None, 'tp'), may hold values from -0.75 to 0.75
- a_rate: float32 [2, 16, 8192], P(None, None, 'tp'), may hold values from 0.00024414062 to 0.2
- dt_bias: float32 [2, 8192], P(None, 'tp'), may hold values from -5 to -1
- skip_gain: float32 [2, 8192], P(None, 'tp'), may hold values from 0.5 to 1.5
- threshold: float32 [2, 8192], P(None, 'tp'), may hold values from 0.1 to 0.8
- w_out: bfloat16 [2, 8192, 4096], P(None, 'tp'), may hold values from -0.09375 to 0.09375
Outputs:
- hidden: bfloat16 [2048, 4096], P('seq', 'tp')
The draws below stay inside these ranges and needn't reach their ends.
All inputs are finite; a program needn't handle non-finite values.
Results may differ from the reference program's by a relative error of at most 0.019.
Values may be sent and summed in bfloat16 or wider, within the bound.
A program may use at most 128 MiB of HBM per device.

```python
import math
import jax
import jax.numpy as jnp
from jax import lax

D = 4096
CHANNELS = 8192
STATE = 16
RANK = 256
GROUP = 128
LAYERS = 2
TOK_DEV = 256
TOKENS = 2048
CH_DEV = 512
N_TP = 16


def draw_tokens(key, part):
    key_noise = jax.random.fold_in(key, 11)
    key_amp = jax.random.fold_in(key, 12)
    key_dir = jax.random.fold_in(key, 13)
    block_count = TOKENS // TOK_DEV
    noise = jnp.clip(jax.random.normal(key_noise, (TOKENS, D), jnp.float32), -4.0, 4.0)
    amp = jax.random.uniform(key_amp, (block_count, 1), jnp.float32, -2.5, 2.5)
    dir_vec = jnp.clip(jax.random.normal(key_dir, (1, D), jnp.float32), -3.0, 3.0)
    offset = jnp.repeat(amp, TOK_DEV, axis=0) * dir_vec
    return jnp.clip(noise + offset, -12.0, 12.0).astype(jnp.bfloat16)


def spiked(values, own_key, source, target, parts, factor):
    owner, partner = [(jnp.arange(values.shape[dim]) // (values.shape[dim] // parts)).reshape([-1 if axis == dim else 1 for axis in range(values.ndim)]) for dim in (source, target)]
    chosen = jax.random.permutation(own_key, parts)[partner]
    strong = (owner == chosen) | (owner == (partner + parts // 2) % parts)
    return jnp.where(strong, factor * values, values)


def block_scale(key, shape, split, low, top_value):
    def one(position, parts):
        steps = jax.random.uniform(jax.random.fold_in(jax.random.fold_in(key, 6), position), (parts,), jnp.float32, low / len(split), top_value / len(split))
        return jnp.repeat(jnp.exp(steps), shape[position] // parts).reshape((-1,) + (1,) * (len(shape) - position - 1))

    loudness = one(*split[0])
    for cut in split[1:]:
        loudness = loudness * one(*cut)
    return loudness


def normal_values(stream_key, shape, deviation, most, shards=(), dtype=jnp.bfloat16):
    drawn = jax.random.normal(stream_key, shape, jnp.float32) * deviation
    if len(shards) > 0:
        drawn = block_scale(stream_key, shape, shards, -0.22, 0.18) * drawn
    return jnp.clip(drawn, min=-most, max=most).astype(dtype)


def noise_with(own_key, shape, spread, limit, pieces, heavy, held_as=jnp.bfloat16):
    result = spread * jax.random.normal(own_key, shape, jnp.float32)
    if pieces:
        result = result * block_scale(own_key, shape, pieces, -0.22, 0.18)
    return jnp.clip(spiked(result, jax.random.fold_in(own_key, 3), *heavy), -limit, limit).astype(held_as)


def setup_inputs(seed: int = 0) -> dict:
    arg_keys = jax.random.split(jax.random.key(seed), 11)
    return {
        "tokens": draw_tokens(jax.random.fold_in(arg_keys[10], 71), 0),
        "norm_gain": jnp.clip(1.0 + 0.1 * jax.random.normal(arg_keys[1], (LAYERS, D), jnp.float32), 0.5, 1.5),
        "w_in": normal_values(arg_keys[2], (LAYERS, D, 2, CHANNELS), D ** -0.5, 0.09375, ((3, 16),)),
        "w_low": normal_values(arg_keys[3], (LAYERS, D, RANK + 2 * STATE), D ** -0.5, 0.09375, ((1, 16),)),
        "w_dt": normal_values(arg_keys[4], (LAYERS, RANK, CHANNELS), (RANK // 4) ** -0.5, 0.75, ((2, 16),)),
        "a_rate": jnp.clip(jnp.exp(math.log(0.2) - 6.7083283 * jax.random.uniform(arg_keys[5], (LAYERS, STATE, CHANNELS), jnp.float32) ** block_scale(arg_keys[5], (LAYERS, STATE, CHANNELS), ((2, 16),), -0.2, 0.2)), 0.00024414062, 0.2),
        "dt_bias": jnp.clip(-5.0 + 4.0 * jax.random.uniform(arg_keys[6], (LAYERS, CHANNELS), jnp.float32) ** block_scale(arg_keys[6], (LAYERS, CHANNELS), ((1, 16),), -0.2, 0.2), -5.0, -1.0),
        "skip_gain": jnp.clip(0.5 + 1.0 * jax.random.uniform(arg_keys[7], (LAYERS, CHANNELS), jnp.float32) ** block_scale(arg_keys[7], (LAYERS, CHANNELS), ((1, 16),), -0.2, 0.2), 0.5, 1.5),
        "threshold": jnp.clip(0.1 + 0.7 * jax.random.uniform(arg_keys[8], (LAYERS, CHANNELS), jnp.float32) ** block_scale(arg_keys[8], (LAYERS, CHANNELS), ((1, 16),), -0.2, 0.2), 0.1, 0.8),
        "w_out": noise_with(arg_keys[9], (LAYERS, CHANNELS, D), CHANNELS ** -0.5, 0.09375, ((1, 16),), (1, 2, 16, 2.0)),
    }


def rms_rows(values_in, gain_row):
    values = values_in.astype(jnp.float32)
    factor = lax.rsqrt(lax.optimization_barrier(jnp.mean(values * values, axis=-1, keepdims=True)) + 1e-05)
    return (values * factor * gain_row).astype(jnp.bfloat16)

def shrink_gate(mixed_out, gate_pre, thresh_row):
    row_count, chan_width = mixed_out.shape
    grouped = mixed_out.reshape(row_count, chan_width // GROUP, GROUP)
    factor = lax.rsqrt(lax.optimization_barrier(jnp.mean(grouped * grouped, axis=-1, keepdims=True)) + 1e-05)
    normal_out = (grouped * factor).reshape(row_count, chan_width)
    shrunk = jax.nn.relu(normal_out - thresh_row) - jax.nn.relu(-normal_out - thresh_row)
    return (shrunk * jax.nn.silu(gate_pre)).astype(jnp.bfloat16)

def ref_layer(hidden, gain_row, w_in_l, w_low_l, w_dt_l, rates, bias_row, skip_row, thresh_row, w_out_l):
    normed = rms_rows(hidden, gain_row)
    projected = jnp.dot(normed, w_in_l.reshape(D, 2 * CHANNELS), preferred_element_type=jnp.float32)
    current = projected[:, :CHANNELS]
    gate_pre = projected[:, CHANNELS:]
    selectors = jnp.dot(normed, w_low_l, preferred_element_type=jnp.float32)
    rank_part = selectors[:, :RANK].astype(jnp.bfloat16)
    in_sel = selectors[:, RANK:RANK + STATE]
    out_sel = selectors[:, RANK + STATE:]
    step_size = jax.nn.softplus(jnp.dot(rank_part, w_dt_l, preferred_element_type=jnp.float32) + bias_row)
    drive_in = step_size * current

    def advance(state_now, inputs):
        step_row, drive_row, in_row, out_row = inputs
        state_now = jnp.exp(-step_row[None, :] * rates) * state_now + in_row[:, None] * drive_row[None, :]
        return (state_now, lax.optimization_barrier(jnp.sum(out_row[:, None] * state_now, axis=0)))
    final_state, mixed_out = lax.scan(advance, jnp.zeros((STATE, CHANNELS), jnp.float32), (step_size, drive_in, in_sel, out_sel))
    mixed_out = mixed_out + skip_row * current
    gated_out = shrink_gate(mixed_out, gate_pre, thresh_row)
    slabs_gate = gated_out.reshape(TOKENS, N_TP, CH_DEV).transpose(1, 0, 2)
    slabs_weight = w_out_l.reshape(N_TP, CH_DEV, D)

    def add_slab(running, pair):
        term = jnp.dot(pair[0], pair[1], preferred_element_type=jnp.float32)
        rounded = lax.optimization_barrier(term.astype(jnp.bfloat16)).astype(jnp.float32)
        return (running + rounded, None)
    summed, unused = lax.scan(add_slab, jnp.zeros((TOKENS, D), jnp.float32), (slabs_gate, slabs_weight))
    return (hidden.astype(jnp.float32) + summed).astype(jnp.bfloat16)

def reference(tokens, norm_gain, w_in, w_low, w_dt, a_rate, dt_bias, skip_gain, threshold, w_out):
    hidden = tokens
    for layer_index in range(LAYERS):
        hidden = ref_layer(hidden, norm_gain[layer_index], w_in[layer_index], w_low[layer_index], w_dt[layer_index], a_rate[layer_index], dt_bias[layer_index], skip_gain[layer_index], threshold[layer_index], w_out[layer_index])
    return hidden
```

```python
import functools
import math

import jax
import jax.numpy as jnp
from jax import lax
from jax.experimental import pallas as pl
from jax.experimental.pallas import tpu as pltpu
from jax.sharding import PartitionSpec as P

MESH = pl.DeviceIdType.MESH
F32 = jnp.float32
BF16 = jnp.bfloat16
SUB = 8
LANE = 128
SIDE = 4
LOG2E = math.log2(math.e)
OFFS = (0, -1, 1, 2)


def kernel_body(
    dims,
    tok_ref,
    gain_ref,
    w_in_hbm,
    w_low_hbm,
    w_dt_hbm,
    a_ref,
    bias_ref,
    skip_ref,
    thresh_ref,
    w_out_hbm,
    out_ref,
    w_in_v,
    w_low_v,
    w_dt_v,
    w_out_v,
    hid,
    agbuf,
    selp,
    arrecv,
    arres,
    expand_b,
    expand_c,
    bx,
    cx,
    step,
    cum,
    proj,
    yv,
    pin,
    ein,
    hdev,
    esend_f,
    esend,
    erecv,
    tsend,
    trecv,
    gated,
    pbuf,
    x1,
    x2,
    s2,
    x3,
    x4,
    wsem,
    ag_s,
    ag_r,
    ar1_s,
    ar1_r,
    ar2_s,
    ar2_r,
    t_s,
    t_r,
    e_s,
    e_r,
    rs_s,
    rs_r,
):
    layers, n_seq, toks, feat, chans, states, rank = dims
    n_tp = SIDE * SIDE
    half = toks // 2
    quart = toks // 4
    steps = toks // SUB
    arow = toks // n_tp
    ncb = chans // LANE
    seqi = lax.axis_index("seq")
    tpi = lax.axis_index("tp")
    zc = tpi // SIDE
    yc = lax.rem(tpi, SIDE)

    def wrap(v):
        return lax.rem(v + 2 * SIDE, SIDE)

    pos = ((yc, zc), (zc, yc))

    def blk(h, c1, c2):
        return c2 * SIDE + c1 if h == 0 else c1 * SIDE + c2

    def nb(h, axis, d):
        p1, p2 = pos[h]
        if axis == 1:
            return {"tp": blk(h, wrap(p1 + d), p2)}
        return {"tp": blk(h, p1, wrap(p2 + d))}

    def rcopy(src, dst, ssem, rsem, dev):
        return pltpu.make_async_remote_copy(
            src_ref=src, dst_ref=dst, send_sem=ssem, recv_sem=rsem,
            device_id=dev, device_id_type=MESH,
        )

    def wcopies(l):
        return (
            pltpu.make_async_copy(w_low_hbm.at[l], w_low_v.at[l, : rank + 2 * states], wsem.at[l, 0]),
            pltpu.make_async_copy(w_dt_hbm.at[l], w_dt_v.at[l], wsem.at[l, 1]),
            pltpu.make_async_copy(w_in_hbm.at[l], w_in_v.at[l], wsem.at[l, 2]),
            pltpu.make_async_copy(w_out_hbm.at[l], w_out_v.at[l], wsem.at[l, 3]),
        )

    for l in range(layers):
        for c in wcopies(l):
            c.start()

    barrier = pltpu.get_barrier_semaphore()
    for d in range(1, n_tp):
        pl.semaphore_signal(barrier, inc=1, device_id={"tp": lax.rem(tpi + d, n_tp)}, device_id_type=MESH)
    for d in range(1, n_seq):
        pl.semaphore_signal(barrier, inc=1, device_id={"seq": lax.rem(seqi + d, n_seq)}, device_id_type=MESH)
    pl.semaphore_wait(barrier, n_tp + n_seq - 2)

    ri = lax.broadcasted_iota(jnp.int32, (toks, toks), 0)
    ci = lax.broadcasted_iota(jnp.int32, (toks, toks), 1)
    perm = jnp.where(ci == lax.rem(ri, SUB) * steps + ri // SUB, 1.0, 0.0).astype(BF16)
    hid[...] = jnp.dot(perm, tok_ref[...], preferred_element_type=F32).astype(BF16)

    ei = lax.broadcasted_iota(jnp.int32, (LANE, states * LANE), 0)
    ej = lax.broadcasted_iota(jnp.int32, (LANE, states * LANE), 1) // LANE
    expand_b[...] = jnp.where(ei == ej, 1.0, 0.0).astype(BF16)
    expand_c[...] = jnp.where(ei == ej + states, 1.0, 0.0).astype(BF16)
    sel_w = rank + LANE
    pad_from = rank + 2 * states
    for l in range(layers):
        w_low_v[l, pad_from:, :] = jnp.zeros((sel_w - pad_from, feat), BF16)

    def ag_info(h, k):
        p1, p2 = pos[h]
        r0 = h * half
        full = pl.ds(r0, half)
        lo = pl.ds(r0, quart)
        hi = pl.ds(r0 + quart, quart)
        if k < 4:
            m = k
            ax = 1

            def at(d):
                return blk(h, wrap(p1 + d), p2)
        else:
            m = (k - 4) % 4
            o = OFFS[(k - 4) // 4]
            ax = 2

            def at(d):
                return blk(h, wrap(p1 + o), wrap(p2 + d))

        src_d, dst_d, rows, to = (
            (0, -1, full, 1),
            (0, 1, full, -1),
            (-1, -2, lo, 1),
            (1, 2, hi, -1),
        )[m]
        return at(src_d), at(dst_d), rows, nb(h, ax, to)

    def ag_send(h, k):
        src, _, rows, dev = ag_info(h, k)
        ref = agbuf.at[src, rows]
        return rcopy(ref, ref, ag_s.at[h, k], ag_r.at[h, k], dev)

    def ag_start(*ks):
        for k in ks:
            for h in range(2):
                ag_send(h, k).start()

    def ag_wait(*ks):
        for k in ks:
            for h in range(2):
                _, dst, rows, dev = ag_info(h, k)
                ref = agbuf.at[dst, rows]
                rcopy(ref, ref, ag_s.at[h, k], ag_r.at[h, k], dev).wait_recv()

    def layer(l, unused):
        low_c, dt_c, in_c, out_c = wcopies(l)
        own = hid[...].astype(F32)
        gain_row = gain_ref[pl.ds(l, 1), pl.ds(pl.multiple_of(tpi * feat, feat), feat)]
        agbuf[tpi] = (own * gain_row).astype(BF16)
        sq = jnp.sum(own * own, axis=1, keepdims=True)
        ag_start(0, 1, 4, 5)

        low_c.wait()
        selv = lax.dot_general(
            agbuf[tpi], w_low_v[l], (((1,), (1,)), ((), ())), preferred_element_type=F32
        )
        sq_hi = sq.astype(BF16).astype(F32)
        lane = lax.broadcasted_iota(jnp.int32, (toks, sel_w), 1)
        selv = jnp.where(lane == pad_from, sq_hi, selv)
        selv = jnp.where(lane == pad_from + 1, sq - sq_hi, selv)
        selp[...] = selv.astype(BF16)
        arrecv[tpi] = selp[pl.ds(pl.multiple_of(tpi * arow, arow), arow), :]

        def ar1(d, sending):
            to = lax.rem(tpi + d, n_tp)
            fr = lax.rem(tpi + n_tp - d, n_tp)
            rows = pl.ds(pl.multiple_of(to * arow, arow), arow)
            dst = arrecv.at[tpi] if sending else arrecv.at[fr]
            return rcopy(selp.at[rows], dst, ar1_s.at[d], ar1_r.at[d], {"tp": to})

        for d in range(1, n_tp):
            ar1(d, True).start()

        ag_wait(0, 1)
        ag_start(2, 3, 8, 9, 12, 13)

        for d in range(1, n_tp):
            ar1(d, False).wait_recv()
        tot = jnp.zeros((arow, sel_w), F32)
        for i in range(n_tp):
            tot = tot + arrecv[i].astype(F32)
        lane = lax.broadcasted_iota(jnp.int32, (arow, sel_w), 1)
        is_sq = (lane == pad_from) | (lane == pad_from + 1)
        ssum = jnp.sum(jnp.where(is_sq, tot, 0.0), axis=1, keepdims=True)
        factor = lax.rsqrt(ssum / (n_tp * feat) + 1e-05)
        f_hi = factor.astype(BF16).astype(F32)
        tot = jnp.where(lane == pad_from, f_hi, jnp.where(lane == pad_from + 1, factor - f_hi, tot * factor))
        mine = pl.ds(pl.multiple_of(tpi * arow, arow), arow)
        arres[mine, :] = tot.astype(BF16)

        def ar2(d, sending):
            to = lax.rem(tpi + d, n_tp)
            fr = lax.rem(tpi + n_tp - d, n_tp)
            base = tpi if sending else fr
            rows = pl.ds(pl.multiple_of(base * arow, arow), arow)
            return rcopy(arres.at[rows], arres.at[rows], ar2_s.at[d], ar2_r.at[d], {"tp": to})

        for d in range(1, n_tp):
            ar2(d, True).start()

        ag_wait(4, 5)
        ag_start(6, 7)
        ag_wait(2, 3)
        ag_start(16, 17)

        for d in range(1, n_tp):
            ar2(d, False).wait_recv()
        tail = arres[:, rank:]
        tl = lax.broadcasted_iota(jnp.int32, (toks, LANE), 1)
        in_f = (tl == 2 * states) | (tl == 2 * states + 1)
        fac = jnp.sum(jnp.where(in_f, tail.astype(F32), 0.0), axis=1, keepdims=True)
        dt_c.wait()
        pre = jnp.dot(arres[:, :rank], w_dt_v[l], preferred_element_type=F32) + bias_ref[pl.ds(l, 1), :]
        step[...] = jnp.maximum(pre, 0.0) + jnp.log1p(jnp.exp(-jnp.abs(pre)))
        bx[...] = jnp.dot(tail, expand_b[...], preferred_element_type=F32)
        cx[...] = jnp.dot(tail, expand_c[...], preferred_element_type=F32)

        def accum(t, run):
            rows = pl.ds(pl.multiple_of(t * SUB, SUB), SUB)
            run = run + step[rows, :]
            cum[rows, :] = run
            return run

        ctot = lax.fori_loop(0, steps, accum, jnp.zeros((SUB, chans), F32))
        tsend[l] = jnp.broadcast_to(jnp.sum(ctot, axis=0, keepdims=True), (SUB, chans))

        def seq_copy(src, dst, ss, rs, q, sending):
            slot = seqi if sending else q
            return rcopy(src, dst.at[l, slot], ss.at[l, q], rs.at[l, slot], {"seq": q})

        for q in range(1, n_seq):
            @pl.when(q > seqi)
            def _():
                seq_copy(tsend.at[l], trecv, t_s, t_r, q, True).start()

        ag_wait(8, 9)
        ag_start(10, 11)
        ag_wait(12, 13)
        ag_start(14, 15)

        in_c.wait()

        def mm(first, pairs):
            for i, (dz, dy) in enumerate(pairs):
                b = wrap(zc + dz) * SIDE + wrap(yc + dy)
                rows = pl.ds(pl.multiple_of(b * feat, feat), feat)
                val = jnp.dot(agbuf[b], w_in_v[l, rows, :], preferred_element_type=F32)
                if first and i == 0:
                    proj[...] = val
                else:
                    proj[...] += val

        mm(True, ((0, 0), (0, 1), (0, -1), (1, 0), (-1, 0), (1, 1), (1, -1), (-1, 1), (-1, -1)))
        ag_wait(16, 17)
        ag_start(18, 19)
        ag_wait(6, 7, 10, 11, 14, 15, 18, 19)
        mm(False, ((2, 0), (2, 1), (2, 2), (2, 3), (0, 2), (1, 2), (3, 2)))
        proj[...] = proj[...] * fac
        for k in range(20):
            for h in range(2):
                ag_send(h, k).wait_send()
        for d in range(1, n_tp):
            ar1(d, True).wait_send()
            ar2(d, True).wait_send()

        skip_row = skip_ref[pl.ds(l, 1), :]
        th_row = thresh_ref[pl.ds(l, 1), :]
        for cb in range(ncb):
            cs = pl.ds(cb * LANE, LANE)
            na = [
                jnp.broadcast_to(a_ref[l, s : s + 1, cs] * (-LOG2E), (SUB, LANE)) for s in range(states)
            ]
            skip = skip_row[:, cb * LANE : (cb + 1) * LANE]

            def scan_step(t, hs):
                rows = pl.ds(pl.multiple_of(t * SUB, SUB), SUB)
                st = step[rows, cs]
                cur = proj[rows, cs]
                dr = st * cur
                acc = skip * cur
                new = []
                for s in range(states):
                    ls = pl.ds(s * LANE, LANE)
                    hn = jnp.exp2(st * na[s]) * hs[s] + bx[rows, ls] * dr
                    acc = acc + cx[rows, ls] * hn
                    new.append(hn)
                yv[rows, cs] = acc
                return tuple(new)

            hs = lax.fori_loop(
                0, steps, scan_step, tuple(jnp.zeros((SUB, LANE), F32) for _ in range(states))
            )
            sub = lax.broadcasted_iota(jnp.int32, (SUB, LANE), 0)
            ct = cum[pl.ds((steps - 1) * SUB, SUB), cs]
            for s in range(states):
                e = hs[s]
                p = jnp.exp2(ct * na[s])
                for d in (1, 2, 4):
                    ok = sub >= d
                    e = e + jnp.where(ok, p * pltpu.roll(e, d, 0), 0.0)
                    p = p * jnp.where(ok, pltpu.roll(p, d, 0), 1.0)
                esend_f[s : s + 1, cs] = e[SUB - 1 : SUB, :]
                ein[s, :, cs] = jnp.where(sub >= 1, pltpu.roll(e, 1, 0), 0.0)
                pin[s, :, cs] = jnp.where(sub >= 1, pltpu.roll(p, 1, 0), 1.0)

        esend[l] = esend_f[...].astype(BF16)
        for q in range(1, n_seq):
            @pl.when(q > seqi)
            def _():
                seq_copy(esend.at[l], erecv, e_s, e_r, q, True).start()

        hdev[...] = jnp.zeros_like(hdev)
        for q in range(n_seq - 1):
            @pl.when(q < seqi)
            def _():
                seq_copy(tsend.at[l], trecv, t_s, t_r, q, False).wait_recv()
                seq_copy(esend.at[l], erecv, e_s, e_r, q, False).wait_recv()
                dec = jnp.exp2(a_ref[l] * (-LOG2E) * trecv[l, q, 0:1, :])
                hdev[...] = dec * hdev[...] + erecv[l, q].astype(F32)

        for cb in range(ncb):
            cs = pl.ds(cb * LANE, LANE)
            na = [
                jnp.broadcast_to(a_ref[l, s : s + 1, cs] * (-LOG2E), (SUB, LANE)) for s in range(states)
            ]
            hin = [ein[s, :, cs] + pin[s, :, cs] * hdev[s : s + 1, cs] for s in range(states)]
            th = th_row[:, cb * LANE : (cb + 1) * LANE]

            def fold(t, unused):
                rows = pl.ds(pl.multiple_of(t * SUB, SUB), SUB)
                ct = cum[rows, cs]
                acc = yv[rows, cs]
                for s in range(states):
                    ls = pl.ds(s * LANE, LANE)
                    acc = acc + cx[rows, ls] * (jnp.exp2(ct * na[s]) * hin[s])
                yv[rows, cs] = acc
                return unused

            lax.fori_loop(0, steps, fold, 0)

            mixed = yv[:, cs]
            fct = lax.rsqrt(jnp.mean(mixed * mixed, axis=1, keepdims=True) + 1e-05)
            normal = mixed * fct
            shrunk = jnp.maximum(normal - th, 0.0) - jnp.maximum(-normal - th, 0.0)
            gate = proj[:, pl.ds(chans + cb * LANE, LANE)]
            gated[:, cs] = (shrunk * (gate / (1.0 + jnp.exp(-gate)))).astype(BF16)

        for q in range(1, n_seq):
            @pl.when(q > seqi)
            def _():
                seq_copy(tsend.at[l], trecv, t_s, t_r, q, True).wait_send()
                seq_copy(esend.at[l], erecv, e_s, e_r, q, True).wait_send()

        out_c.wait()
        lo = pl.ds(0, quart)
        hi = pl.ds(quart, quart)

        def rpos(h):
            p2, p1 = pos[h]
            return p1, p2

        def rnb(h, axis, d):
            return nb(h, 3 - axis, d)

        def omm(h, c1):
            lhs = gated[h * half : (h + 1) * half, :]
            for c2 in range(SIDE):
                b = c1 * SIDE + c2 if h == 0 else c2 * SIDE + c1
                cols = pl.ds(pl.multiple_of(b * feat, feat), feat)
                pbuf[h, c1, c2] = jnp.dot(
                    lhs, w_out_v[l, :, cols], preferred_element_type=F32
                ).astype(BF16)

        def rs_copy(h, k):
            p1, p2 = rpos(h)
            src, dst, dev = (
                lambda: (pbuf.at[h, wrap(p1 + 2), :, lo], x1.at[h, 0], rnb(h, 1, 1)),
                lambda: (pbuf.at[h, wrap(p1 + 2), :, hi], x1.at[h, 1], rnb(h, 1, -1)),
                lambda: (pbuf.at[h, wrap(p1 + 1)], x2.at[h, 0], rnb(h, 1, 1)),
                lambda: (pbuf.at[h, wrap(p1 - 1)], x2.at[h, 1], rnb(h, 1, -1)),
                lambda: (s2.at[h, wrap(p2 + 2), lo], x3.at[h, 0], rnb(h, 2, 1)),
                lambda: (s2.at[h, wrap(p2 + 2), hi], x3.at[h, 1], rnb(h, 2, -1)),
                lambda: (s2.at[h, wrap(p2 + 1)], x4.at[h, 0], rnb(h, 2, 1)),
                lambda: (s2.at[h, wrap(p2 - 1)], x4.at[h, 1], rnb(h, 2, -1)),
            )[k]()
            return rcopy(src, dst, rs_s.at[h, k], rs_r.at[h, k], dev)

        for h in range(2):
            omm(h, wrap(rpos(h)[0] + 2))
            rs_copy(h, 0).start()
            rs_copy(h, 1).start()
        for h in range(2):
            omm(h, wrap(rpos(h)[0] + 1))
            omm(h, wrap(rpos(h)[0] - 1))
        for h in range(2):
            p1, _ = rpos(h)
            up = wrap(p1 + 1)
            dn = wrap(p1 - 1)
            rs_copy(h, 0).wait_recv()
            pbuf[h, up, :, lo] = (pbuf[h, up, :, lo].astype(F32) + x1[h, 0].astype(F32)).astype(BF16)
            rs_copy(h, 2).start()
            rs_copy(h, 1).wait_recv()
            pbuf[h, dn, :, hi] = (pbuf[h, dn, :, hi].astype(F32) + x1[h, 1].astype(F32)).astype(BF16)
            rs_copy(h, 3).start()
        for h in range(2):
            omm(h, rpos(h)[0])
        for h in range(2):
            p1, p2 = rpos(h)
            rs_copy(h, 2).wait_recv()
            rs_copy(h, 3).wait_recv()

            def sum3(c2):
                return pbuf[h, p1, c2].astype(F32) + x2[h, 0, c2].astype(F32) + x2[h, 1, c2].astype(F32)

            far = wrap(p2 + 2)
            s2[h, far] = sum3(far).astype(BF16)
            rs_copy(h, 4).start()
            rs_copy(h, 5).start()
            for d in (1, -1):
                c2 = wrap(p2 + d)
                s2[h, c2] = sum3(c2).astype(BF16)
        for h in range(2):
            p1, p2 = rpos(h)
            up = wrap(p2 + 1)
            dn = wrap(p2 - 1)
            rs_copy(h, 4).wait_recv()
            s2[h, up, lo] = (s2[h, up, lo].astype(F32) + x3[h, 0].astype(F32)).astype(BF16)
            rs_copy(h, 6).start()
            rs_copy(h, 5).wait_recv()
            s2[h, dn, hi] = (s2[h, dn, hi].astype(F32) + x3[h, 1].astype(F32)).astype(BF16)
            rs_copy(h, 7).start()
        for h in range(2):
            p1, p2 = rpos(h)
            rs_copy(h, 6).wait_recv()
            rs_copy(h, 7).wait_recv()
            total = pbuf[h, p1, p2].astype(F32) + x2[h, 0, p2].astype(F32) + x2[h, 1, p2].astype(F32)
            total = total + x4[h, 0].astype(F32) + x4[h, 1].astype(F32)
            rows = pl.ds(h * half, half)
            hid[rows, :] = (hid[rows, :].astype(F32) + total).astype(BF16)
        for h in range(2):
            for k in range(8):
                rs_copy(h, k).wait_send()
        return unused

    lax.fori_loop(0, layers, layer, 0)
    out_ref[...] = lax.dot_general(
        perm, hid[...], (((0,), (0,)), ((), ())), preferred_element_type=F32
    ).astype(BF16)


def per_device(n_seq, tokens, norm_gain, w_in, w_low, w_dt, a_rate, dt_bias, skip_gain, threshold, w_out):
    toks, feat = tokens.shape
    layers, model, _, chans = w_in.shape
    states = a_rate.shape[1]
    rank = w_dt.shape[1]
    n_tp = SIDE * SIDE
    half, quart = toks // 2, toks // 4
    sel_w = rank + LANE
    dims = (layers, n_seq, toks, feat, chans, states, rank)
    vm = pl.BlockSpec(memory_space=pltpu.VMEM)
    hb = pl.BlockSpec(memory_space=pl.ANY)
    dma = pltpu.SemaphoreType.DMA
    V = pltpu.VMEM
    return pl.pallas_call(
        functools.partial(kernel_body, dims),
        out_shape=jax.ShapeDtypeStruct((toks, feat), BF16),
        in_specs=[vm, vm, hb, hb, hb, vm, vm, vm, vm, hb],
        out_specs=vm,
        scratch_shapes=[
            V((layers, model, 2 * chans), BF16),
            V((layers, sel_w, feat), BF16),
            V((layers, rank, chans), BF16),
            V((layers, chans, model), BF16),
            V((toks, feat), BF16),
            V((n_tp, toks, feat), BF16),
            V((toks, sel_w), BF16),
            V((n_tp, toks // n_tp, sel_w), BF16),
            V((toks, sel_w), BF16),
            V((LANE, states * LANE), BF16),
            V((LANE, states * LANE), BF16),
            V((toks, states * LANE), F32),
            V((toks, states * LANE), F32),
            V((toks, chans), F32),
            V((toks, chans), F32),
            V((toks, 2 * chans), F32),
            V((toks, chans), F32),
            V((states, SUB, chans), F32),
            V((states, SUB, chans), F32),
            V((states, chans), F32),
            V((states, chans), F32),
            V((layers, states, chans), BF16),
            V((layers, n_seq, states, chans), BF16),
            V((layers, SUB, chans), F32),
            V((layers, n_seq, SUB, chans), F32),
            V((toks, chans), BF16),
            V((2, SIDE, SIDE, half, feat), BF16),
            V((2, 2, SIDE, quart, feat), BF16),
            V((2, 2, SIDE, half, feat), BF16),
            V((2, SIDE, half, feat), BF16),
            V((2, 2, quart, feat), BF16),
            V((2, 2, half, feat), BF16),
            dma((layers, 4)),
            dma((2, 20)),
            dma((2, 20)),
            dma((n_tp,)),
            dma((n_tp,)),
            dma((n_tp,)),
            dma((n_tp,)),
            dma((layers, n_seq)),
            dma((layers, n_seq)),
            dma((layers, n_seq)),
            dma((layers, n_seq)),
            dma((2, 8)),
            dma((2, 8)),
        ],
        compiler_params=pltpu.CompilerParams(
            collective_id=0, has_side_effects=True, vmem_limit_bytes=60 * 1024 * 1024
        ),
    )(
        tokens,
        norm_gain,
        w_in.reshape(layers, model, 2 * chans),
        jnp.swapaxes(w_low, 1, 2),
        w_dt,
        a_rate,
        dt_bias,
        skip_gain,
        threshold,
        w_out,
    )


def solution(mesh):
    in_specs = (
        P("seq", "tp"),
        P(),
        P(None, None, None, "tp"),
        P(None, "tp", None),
        P(None, None, "tp"),
        P(None, None, "tp"),
        P(None, "tp"),
        P(None, "tp"),
        P(None, "tp"),
        P(None, "tp", None),
    )
    return jax.shard_map(
        functools.partial(per_device, mesh.shape["seq"]),
        mesh=mesh,
        in_specs=in_specs,
        out_specs=P("seq", "tp"),
        check_vma=False,
    )
```

```python
import functools
import math

import jax
import jax.numpy as jnp
from jax import lax
from jax.experimental import pallas as pl
from jax.experimental.pallas import tpu as pltpu
from jax.sharding import PartitionSpec as P

MESH = pl.DeviceIdType.MESH
F32 = jnp.float32
BF16 = jnp.bfloat16
SUB = 8
LANE = 128
SIDE = 4
LOG2E = math.log2(math.e)
OFFS = (0, -1, 1, 2)


def kernel_body(
    dims,
    tok_ref,
    gain_ref,
    w_in_hbm,
    w_low_hbm,
    w_dt_hbm,
    a_ref,
    bias_ref,
    skip_ref,
    thresh_ref,
    w_out_hbm,
    out_ref,
    raw,
    seld,
    w_in_v,
    w_low_v,
    w_dt_v,
    w_out_v,
    hid,
    agbuf,
    sqv,
    selp,
    arrecv,
    arres,
    expand_b,
    expand_c,
    bx,
    cx,
    step,
    cum,
    proj,
    yv,
    pin,
    ein,
    hst,
    hdev,
    hdec,
    esend_f,
    esend,
    erecv,
    tsend,
    trecv,
    gated,
    pbuf,
    x1,
    x2,
    s2,
    x3,
    x4,
    wsem,
    ag_s,
    ag_r,
    ar1_s,
    ar1_r,
    ar2_s,
    ar2_r,
    t_s,
    t_r,
    e_s,
    e_r,
    rs_s,
    rs_r,
):
    layers, n_seq, toks, feat, chans, states, rank = dims
    n_tp = SIDE * SIDE
    half = toks // 2
    quart = toks // 4
    eighth = toks // 8
    per_d = 2 * chans // LANE
    steps = toks // SUB
    arow = toks // n_tp
    ncb = chans // LANE
    seqi = lax.axis_index("seq")
    tpi = lax.axis_index("tp")
    zc = tpi // SIDE
    yc = lax.rem(tpi, SIDE)

    def wrap(v):
        return lax.rem(v + 2 * SIDE, SIDE)

    pos = ((yc, zc), (zc, yc))

    def blk(h, c1, c2):
        return c2 * SIDE + c1 if h == 0 else c1 * SIDE + c2

    def nb(h, axis, d):
        p1, p2 = pos[h]
        if axis == 1:
            return {"tp": blk(h, wrap(p1 + d), p2)}
        return {"tp": blk(h, p1, wrap(p2 + d))}

    def rcopy(src, dst, ssem, rsem, dev):
        return pltpu.make_async_remote_copy(
            src_ref=src, dst_ref=dst, send_sem=ssem, recv_sem=rsem,
            device_id=dev, device_id_type=MESH,
        )

    def wcopies(l):
        return (
            pltpu.make_async_copy(w_low_hbm.at[l], w_low_v.at[l, : rank + 2 * states], wsem.at[l, 0]),
            pltpu.make_async_copy(w_dt_hbm.at[l], w_dt_v.at[l], wsem.at[l, 1]),
            pltpu.make_async_copy(w_in_hbm.at[l], raw, wsem.at[l, 2]),
            pltpu.make_async_copy(w_out_hbm.at[l], w_out_v.at[l], wsem.at[l, 3]),
        )

    first_copies = wcopies(0)
    later_copies = wcopies(1)
    for c in (first_copies[0], first_copies[2], first_copies[1], first_copies[3],
              later_copies[0], later_copies[1], later_copies[3]):
        c.start()

    barrier = pltpu.get_barrier_semaphore()
    for d in range(1, n_tp):
        pl.semaphore_signal(barrier, inc=1, device_id={"tp": lax.rem(tpi + d, n_tp)}, device_id_type=MESH)
    for d in range(1, n_seq):
        pl.semaphore_signal(barrier, inc=1, device_id={"seq": lax.rem(seqi + d, n_seq)}, device_id_type=MESH)
    pl.semaphore_wait(barrier, n_tp + n_seq - 2)

    ri = lax.broadcasted_iota(jnp.int32, (toks, toks), 0)
    ci = lax.broadcasted_iota(jnp.int32, (toks, toks), 1)
    perm = jnp.where(ci == lax.rem(ri, SUB) * steps + ri // SUB, 1.0, 0.0).astype(BF16)
    hid[...] = jnp.dot(perm, tok_ref[...], preferred_element_type=F32).astype(BF16)

    def ag_info(u, h, k):
        p1, p2 = pos[h]
        r0 = u * half + h * quart
        full = pl.ds(r0, quart)
        lo = pl.ds(r0, eighth)
        hi = pl.ds(r0 + eighth, eighth)
        if k < 4:
            m = k
            ax = 1

            def at(d):
                return blk(h, wrap(p1 + d), p2)
        else:
            m = (k - 4) % 4
            o = OFFS[(k - 4) // 4]
            ax = 2

            def at(d):
                return blk(h, wrap(p1 + o), wrap(p2 + d))

        src_d, dst_d, rows, to = (
            (0, -1, full, 1),
            (0, 1, full, -1),
            (-1, -2, lo, 1),
            (1, 2, hi, -1),
        )[m]
        return at(src_d), at(dst_d), rows, nb(h, ax, to)

    def ag_send(u, h, k):
        src, _, rows, dev = ag_info(u, h, k)
        ref = agbuf.at[src, rows]
        return rcopy(ref, ref, ag_s.at[u, h, k], ag_r.at[u, h, k], dev)

    def ag_start(u, *ks):
        for k in ks:
            for h in range(2):
                ag_send(u, h, k).start()

    def ag_wait(u, *ks):
        for k in ks:
            for h in range(2):
                _, dst, rows, dev = ag_info(u, h, k)
                ref = agbuf.at[dst, rows]
                rcopy(ref, ref, ag_s.at[u, h, k], ag_r.at[u, h, k], dev).wait_recv()

    def publish(l, u):
        rows = pl.ds(u * half, half)
        own = hid[rows, :].astype(F32)
        gain_row = gain_ref[pl.ds(l, 1), pl.ds(pl.multiple_of(tpi * feat, feat), feat)]
        agbuf[tpi, rows] = (own * gain_row).astype(BF16)
        sqv[rows, :] = jnp.broadcast_to(jnp.sum(own * own, axis=1, keepdims=True), (half, LANE))
        ag_start(u, 0, 1, 4, 5)

    publish(0, 0)

    ei = lax.broadcasted_iota(jnp.int32, (LANE, states * LANE), 0)
    ej = lax.broadcasted_iota(jnp.int32, (LANE, states * LANE), 1) // LANE
    expand_b[...] = jnp.where(ei == ej, 1.0, 0.0).astype(BF16)
    expand_c[...] = jnp.where(ei == ej + states, 1.0, 0.0).astype(BF16)
    grp = 2 * LANE // per_d
    gi = lax.broadcasted_iota(jnp.int32, (2 * LANE, 2 * LANE), 0)
    gj = lax.broadcasted_iota(jnp.int32, (2 * LANE, 2 * LANE), 1)
    seld[...] = jnp.where(gj == lax.rem(gi, grp) * per_d + gi // grp, 1.0, 0.0).astype(BF16)
    sel_w = rank + LANE
    pad_from = rank + 2 * states
    for l in range(layers):
        w_low_v[l, pad_from:, :] = jnp.zeros((sel_w - pad_from, feat), BF16)

    def regroup(b0, b1):
        def one(i, unused):
            r = pl.multiple_of(i * 4 * LANE, 4 * LANE)
            two = jnp.concatenate(
                [raw[pl.ds(r, 2 * LANE), :], raw[pl.ds(r + 2 * LANE, 2 * LANE), :]], axis=1
            )
            got = jnp.dot(seld[...], two, preferred_element_type=F32).astype(BF16)
            d0 = pl.multiple_of(i * 2 * grp, 2 * grp)
            for q in range(per_d):
                cols = pl.ds((q % 2) * chans + (q // 2) * LANE, LANE)
                for v in range(2):
                    w_in_v[pl.ds(d0 + v * grp, grp), cols] = got[
                        q * grp : (q + 1) * grp, v * LANE : (v + 1) * LANE
                    ]
            return unused

        lax.fori_loop(b0, b1, one, 0)

    nreg = n_tp * feat // (2 * grp)

    def seq_copy(l, src, dst, ss, rs, q, sending):
        slot = seqi if sending else q
        return rcopy(src, dst.at[l, slot], ss.at[l, q], rs.at[l, slot], {"seq": q})

    def t_copy(l, q, sending):
        return seq_copy(l, tsend.at[l], trecv, t_s, t_r, q, sending)

    def e_copy(l, q, sending):
        return seq_copy(l, esend.at[l], erecv, e_s, e_r, q, sending)

    lo = pl.ds(0, eighth)
    hi = pl.ds(eighth, eighth)

    def rpos(h):
        p2, p1 = pos[h]
        return p1, p2

    def rnb(h, axis, d):
        return nb(h, 3 - axis, d)

    def rs_copy(u, h, k):
        p1, p2 = rpos(h)
        src, dst, dev = (
            lambda: (pbuf.at[u, h, wrap(p1 + 2), :, lo], x1.at[u, h, 0], rnb(h, 1, 1)),
            lambda: (pbuf.at[u, h, wrap(p1 + 2), :, hi], x1.at[u, h, 1], rnb(h, 1, -1)),
            lambda: (pbuf.at[u, h, wrap(p1 + 1)], x2.at[u, h, 0], rnb(h, 1, 1)),
            lambda: (pbuf.at[u, h, wrap(p1 - 1)], x2.at[u, h, 1], rnb(h, 1, -1)),
            lambda: (s2.at[u, h, wrap(p2 + 2), lo], x3.at[u, h, 0], rnb(h, 2, 1)),
            lambda: (s2.at[u, h, wrap(p2 + 2), hi], x3.at[u, h, 1], rnb(h, 2, -1)),
            lambda: (s2.at[u, h, wrap(p2 + 1)], x4.at[u, h, 0], rnb(h, 2, 1)),
            lambda: (s2.at[u, h, wrap(p2 - 1)], x4.at[u, h, 1], rnb(h, 2, -1)),
        )[k]()
        return rcopy(src, dst, rs_s.at[u, h, k], rs_r.at[u, h, k], dev)

    def omm(l, u, pairs):
        lhs = gated[u * half : (u + 1) * half, :]
        for dz, dy in pairs:
            z, y = wrap(zc + dz), wrap(yc + dy)
            cols = pl.ds(pl.multiple_of((z * SIDE + y) * feat, feat), feat)
            val = jnp.dot(lhs, w_out_v[l, :, cols], preferred_element_type=F32).astype(BF16)
            pbuf[u, 0, z, y] = val[:quart]
            pbuf[u, 1, y, z] = val[quart:]

    def rs1(l, u):
        omm(l, u, ((2, 0), (2, 1), (2, 2), (2, 3), (0, 2), (1, 2), (3, 2)))
        for h in range(2):
            rs_copy(u, h, 0).start()
            rs_copy(u, h, 1).start()

    def rs2(u):
        for h in range(2):
            p1, _ = rpos(h)
            up = wrap(p1 + 1)
            dn = wrap(p1 - 1)
            rs_copy(u, h, 0).wait_recv()
            pbuf[u, h, up, :, lo] = (
                pbuf[u, h, up, :, lo].astype(F32) + x1[u, h, 0].astype(F32)
            ).astype(BF16)
            rs_copy(u, h, 2).start()
            rs_copy(u, h, 1).wait_recv()
            pbuf[u, h, dn, :, hi] = (
                pbuf[u, h, dn, :, hi].astype(F32) + x1[u, h, 1].astype(F32)
            ).astype(BF16)
            rs_copy(u, h, 3).start()

    def sum3(u, h, p1, c2):
        return (
            pbuf[u, h, p1, c2].astype(F32) + x2[u, h, 0, c2].astype(F32) + x2[u, h, 1, c2].astype(F32)
        )

    def rs3(u):
        for h in range(2):
            p1, p2 = rpos(h)
            rs_copy(u, h, 2).wait_recv()
            rs_copy(u, h, 3).wait_recv()
            far = wrap(p2 + 2)
            s2[u, h, far] = sum3(u, h, p1, far).astype(BF16)
            rs_copy(u, h, 4).start()
            rs_copy(u, h, 5).start()
            for d in (1, -1):
                c2 = wrap(p2 + d)
                s2[u, h, c2] = sum3(u, h, p1, c2).astype(BF16)

    def rs4(u):
        for h in range(2):
            _, p2 = rpos(h)
            up = wrap(p2 + 1)
            dn = wrap(p2 - 1)
            rs_copy(u, h, 4).wait_recv()
            s2[u, h, up, lo] = (s2[u, h, up, lo].astype(F32) + x3[u, h, 0].astype(F32)).astype(BF16)
            rs_copy(u, h, 6).start()
            rs_copy(u, h, 5).wait_recv()
            s2[u, h, dn, hi] = (s2[u, h, dn, hi].astype(F32) + x3[u, h, 1].astype(F32)).astype(BF16)
            rs_copy(u, h, 7).start()

    def rs5(u):
        for h in range(2):
            p1, p2 = rpos(h)
            rs_copy(u, h, 6).wait_recv()
            rs_copy(u, h, 7).wait_recv()
            total = sum3(u, h, p1, p2) + x4[u, h, 0].astype(F32) + x4[u, h, 1].astype(F32)
            rows = pl.ds(u * half + h * quart, quart)
            hid[rows, :] = (hid[rows, :].astype(F32) + total).astype(BF16)

    def layer(l, unused):
        low_c, dt_c, in_c, out_c = wcopies(l)
        publish(l, 1)

        low_c.wait()
        selv = lax.dot_general(
            agbuf[tpi], w_low_v[l], (((1,), (1,)), ((), ())), preferred_element_type=F32
        )
        sq = sqv[:, 0:1]
        sq_hi = sq.astype(BF16).astype(F32)
        lane = lax.broadcasted_iota(jnp.int32, (toks, sel_w), 1)
        selv = jnp.where(lane == pad_from, sq_hi, selv)
        selv = jnp.where(lane == pad_from + 1, sq - sq_hi, selv)
        selp[...] = selv.astype(BF16)
        arrecv[tpi] = selp[pl.ds(pl.multiple_of(tpi * arow, arow), arow), :]

        def ar1(d, sending):
            to = lax.rem(tpi + d, n_tp)
            fr = lax.rem(tpi + n_tp - d, n_tp)
            rows = pl.ds(pl.multiple_of(to * arow, arow), arow)
            dst = arrecv.at[tpi] if sending else arrecv.at[fr]
            return rcopy(selp.at[rows], dst, ar1_s.at[d], ar1_r.at[d], {"tp": to})

        for d in range(1, n_tp):
            ar1(d, True).start()

        in_c.wait()
        ag_wait(0, 0, 1)
        ag_start(0, 2, 3, 8, 9, 12, 13)
        ag_wait(0, 4, 5)
        ag_start(0, 6, 7)
        regroup(0, nreg // 4)
        ag_wait(1, 0, 1)
        ag_start(1, 2, 3, 8, 9, 12, 13)
        ag_wait(0, 2, 3)
        ag_start(0, 16, 17)
        ag_wait(0, 8, 9)
        ag_start(0, 10, 11)
        ag_wait(0, 12, 13)
        ag_start(0, 14, 15)
        ag_wait(1, 4, 5)
        ag_start(1, 6, 7)

        for d in range(1, n_tp):
            ar1(d, False).wait_recv()
        tot = jnp.zeros((arow, sel_w), F32)
        for i in range(n_tp):
            tot = tot + arrecv[i].astype(F32)
        lane = lax.broadcasted_iota(jnp.int32, (arow, sel_w), 1)
        is_sq = (lane == pad_from) | (lane == pad_from + 1)
        ssum = jnp.sum(jnp.where(is_sq, tot, 0.0), axis=1, keepdims=True)
        factor = lax.rsqrt(ssum / (n_tp * feat) + 1e-05)
        f_hi = factor.astype(BF16).astype(F32)
        tot = jnp.where(lane == pad_from, f_hi, jnp.where(lane == pad_from + 1, factor - f_hi, tot * factor))
        mine = pl.ds(pl.multiple_of(tpi * arow, arow), arow)
        arres[mine, :] = tot.astype(BF16)

        def ar2(d, sending):
            to = lax.rem(tpi + d, n_tp)
            fr = lax.rem(tpi + n_tp - d, n_tp)
            base = tpi if sending else fr
            rows = pl.ds(pl.multiple_of(base * arow, arow), arow)
            return rcopy(arres.at[rows], arres.at[rows], ar2_s.at[d], ar2_r.at[d], {"tp": to})

        for d in range(1, n_tp):
            ar2(d, True).start()

        regroup(nreg // 4, nreg // 2)
        ag_wait(1, 2, 3)
        ag_start(1, 16, 17)
        ag_wait(0, 16, 17)
        ag_start(0, 18, 19)
        ag_wait(1, 8, 9)
        ag_start(1, 10, 11)
        ag_wait(1, 12, 13)
        ag_start(1, 14, 15)
        regroup(nreg // 2, nreg)

        @pl.when(l + 1 < layers)
        def _():
            later_copies[2].start()

        for d in range(1, n_tp):
            ar2(d, False).wait_recv()
        tail = arres[:, rank:]
        tl = lax.broadcasted_iota(jnp.int32, (toks, LANE), 1)
        in_f = (tl == 2 * states) | (tl == 2 * states + 1)
        fac = jnp.sum(jnp.where(in_f, tail.astype(F32), 0.0), axis=1, keepdims=True)
        dt_c.wait()
        pre = jnp.dot(arres[:, :rank], w_dt_v[l], preferred_element_type=F32) + bias_ref[pl.ds(l, 1), :]
        step[...] = jnp.maximum(pre, 0.0) + jnp.log1p(jnp.exp(-jnp.abs(pre)))
        bx[...] = jnp.dot(tail, expand_b[...], preferred_element_type=F32)
        cx[...] = jnp.dot(tail, expand_c[...], preferred_element_type=F32)

        def accum(t, run):
            rows = pl.ds(pl.multiple_of(t * SUB, SUB), SUB)
            run = run + step[rows, :]
            cum[rows, :] = run
            return run

        ctot = lax.fori_loop(0, steps, accum, jnp.zeros((SUB, chans), F32))
        tsend[l] = jnp.broadcast_to(jnp.sum(ctot, axis=0, keepdims=True), (SUB, chans))
        for q in range(1, n_seq):
            @pl.when(q > seqi)
            def _():
                t_copy(l, q, True).start()

        skip_row = skip_ref[pl.ds(l, 1), :]
        th_row = thresh_ref[pl.ds(l, 1), :]

        def mm(u, first, pairs):
            rs = pl.ds(u * half, half)
            for i, (dz, dy) in enumerate(pairs):
                b = wrap(zc + dz) * SIDE + wrap(yc + dy)
                rows = pl.ds(pl.multiple_of(b * feat, feat), feat)
                val = jnp.dot(agbuf[b, rs], w_in_v[rows, :], preferred_element_type=F32)
                if first and i == 0:
                    proj[rs, :] = val
                else:
                    proj[rs, :] += val

        near = ((0, 0), (0, 1), (0, -1), (1, 0), (-1, 0), (1, 1), (1, -1), (-1, 1), (-1, -1))
        away = ((2, 0), (2, 1), (2, 2), (2, 3), (0, 2), (1, 2), (3, 2))

        def scan(u):
            for cb in range(ncb):
                cs = pl.ds(cb * LANE, LANE)
                na = [
                    jnp.broadcast_to(a_ref[l, s : s + 1, cs] * (-LOG2E), (SUB, LANE))
                    for s in range(states)
                ]
                skip = skip_row[:, cb * LANE : (cb + 1) * LANE]

                def scan_step(t, hs):
                    rows = pl.ds(pl.multiple_of(t * SUB, SUB), SUB)
                    st = step[rows, cs]
                    cur = proj[rows, cs]
                    dr = st * cur
                    acc = skip * cur
                    new = []
                    for s in range(states):
                        ls = pl.ds(s * LANE, LANE)
                        hn = jnp.exp2(st * na[s]) * hs[s] + bx[rows, ls] * dr
                        acc = acc + cx[rows, ls] * hn
                        new.append(hn)
                    yv[rows, cs] = acc
                    return tuple(new)

                if u == 0:
                    init = tuple(jnp.zeros((SUB, LANE), F32) for _ in range(states))
                else:
                    init = tuple(hst[s, :, cs] for s in range(states))
                hs = lax.fori_loop(u * steps // 2, (u + 1) * steps // 2, scan_step, init)
                if u == 0:
                    for s in range(states):
                        hst[s, :, cs] = hs[s]
                    continue
                sub = lax.broadcasted_iota(jnp.int32, (SUB, LANE), 0)
                ct = cum[pl.ds((steps - 1) * SUB, SUB), cs]
                for s in range(states):
                    e = hs[s]
                    p = jnp.exp2(ct * na[s])
                    for d in (1, 2, 4):
                        ok = sub >= d
                        e = e + jnp.where(ok, p * pltpu.roll(e, d, 0), 0.0)
                        p = p * jnp.where(ok, pltpu.roll(p, d, 0), 1.0)
                    esend_f[s : s + 1, cs] = e[SUB - 1 : SUB, :]
                    ein[s, :, cs] = jnp.where(sub >= 1, pltpu.roll(e, 1, 0), 0.0)
                    pin[s, :, cs] = jnp.where(sub >= 1, pltpu.roll(p, 1, 0), 1.0)

        ag_wait(1, 16, 17)
        ag_start(1, 18, 19)
        ag_wait(0, 6, 7, 10, 11, 14, 15, 18, 19)
        mm(0, True, near + away)
        proj[:half, :] = proj[:half, :] * fac[:half]
        scan(0)
        mm(1, True, near)
        ag_wait(1, 6, 7, 10, 11, 14, 15, 18, 19)
        mm(1, False, away)
        proj[half:, :] = proj[half:, :] * fac[half:]
        scan(1)

        esend[l] = esend_f[...].astype(BF16)
        for q in range(1, n_seq):
            @pl.when(q > seqi)
            def _():
                e_copy(l, q, True).start()

        for u in range(2):
            for k in range(20):
                for h in range(2):
                    ag_send(u, h, k).wait_send()
        for d in range(1, n_tp):
            ar1(d, True).wait_send()
            ar2(d, True).wait_send()

        rates = a_ref[l] * (-LOG2E)
        for q in range(n_seq - 1):
            @pl.when(q < seqi)
            def _():
                t_copy(l, q, False).wait_recv()
                hdec[q] = jnp.exp2(rates * trecv[l, q, 0:1, :])

        hdev[...] = jnp.zeros_like(hdev)
        for q in range(n_seq - 1):
            @pl.when(q < seqi)
            def _():
                e_copy(l, q, False).wait_recv()
                hdev[...] = hdec[q] * hdev[...] + erecv[l, q].astype(F32)

        def finish(u):
            rs = pl.ds(u * half, half)
            for cb in range(ncb):
                cs = pl.ds(cb * LANE, LANE)
                na = [
                    jnp.broadcast_to(a_ref[l, s : s + 1, cs] * (-LOG2E), (SUB, LANE))
                    for s in range(states)
                ]
                hin = [ein[s, :, cs] + pin[s, :, cs] * hdev[s : s + 1, cs] for s in range(states)]
                th = th_row[:, cb * LANE : (cb + 1) * LANE]

                def fold(t, unused):
                    rows = pl.ds(pl.multiple_of(t * SUB, SUB), SUB)
                    ct = cum[rows, cs]
                    acc = yv[rows, cs]
                    for s in range(states):
                        ls = pl.ds(s * LANE, LANE)
                        acc = acc + cx[rows, ls] * (jnp.exp2(ct * na[s]) * hin[s])
                    yv[rows, cs] = acc
                    return unused

                lax.fori_loop(u * steps // 2, (u + 1) * steps // 2, fold, 0)

                mixed = yv[rs, cs]
                fct = lax.rsqrt(jnp.mean(mixed * mixed, axis=1, keepdims=True) + 1e-05)
                normal = mixed * fct
                shrunk = jnp.maximum(normal - th, 0.0) - jnp.maximum(-normal - th, 0.0)
                gate = proj[rs, pl.ds(chans + cb * LANE, LANE)]
                gated[rs, cs] = (shrunk * (gate / (1.0 + jnp.exp(-gate)))).astype(BF16)

        others = ((0, 0), (0, 1), (0, -1), (1, 0), (-1, 0), (1, 1), (1, -1), (-1, 1), (-1, -1))
        finish(0)
        out_c.wait()
        rs1(l, 0)
        omm(l, 0, others)
        finish(1)
        rs1(l, 1)
        rs2(0)
        omm(l, 1, others)
        rs2(1)
        rs3(0)
        rs4(0)
        rs3(1)
        rs5(0)

        @pl.when(l + 1 < layers)
        def _():
            publish(l + 1, 0)

        rs4(1)
        rs5(1)
        for u in range(2):
            for h in range(2):
                for k in range(8):
                    rs_copy(u, h, k).wait_send()
        for q in range(1, n_seq):
            @pl.when(q > seqi)
            def _():
                t_copy(l, q, True).wait_send()
                e_copy(l, q, True).wait_send()
        return unused

    lax.fori_loop(0, layers, layer, 0)
    out_ref[...] = lax.dot_general(
        perm, hid[...], (((0,), (0,)), ((), ())), preferred_element_type=F32
    ).astype(BF16)


def per_device(n_seq, tokens, norm_gain, w_in, w_low, w_dt, a_rate, dt_bias, skip_gain, threshold, w_out):
    toks, feat = tokens.shape
    layers, model, _, chans = w_in.shape
    states = a_rate.shape[1]
    rank = w_dt.shape[1]
    n_tp = SIDE * SIDE
    half, quart, eighth = toks // 2, toks // 4, toks // 8
    per_d = 2 * chans // LANE
    sel_w = rank + LANE
    dims = (layers, n_seq, toks, feat, chans, states, rank)
    vm = pl.BlockSpec(memory_space=pltpu.VMEM)
    hb = pl.BlockSpec(memory_space=pl.ANY)
    dma = pltpu.SemaphoreType.DMA
    V = pltpu.VMEM
    return pl.pallas_call(
        functools.partial(kernel_body, dims),
        out_shape=jax.ShapeDtypeStruct((toks, feat), BF16),
        in_specs=[vm, vm, hb, hb, hb, vm, vm, vm, vm, hb],
        out_specs=vm,
        scratch_shapes=[
            V((model * per_d, LANE), BF16),
            V((2 * LANE, 2 * LANE), BF16),
            V((model, 2 * chans), BF16),
            V((layers, sel_w, feat), BF16),
            V((layers, rank, chans), BF16),
            V((layers, chans, model), BF16),
            V((toks, feat), BF16),
            V((n_tp, toks, feat), BF16),
            V((toks, LANE), F32),
            V((toks, sel_w), BF16),
            V((n_tp, toks // n_tp, sel_w), BF16),
            V((toks, sel_w), BF16),
            V((LANE, states * LANE), BF16),
            V((LANE, states * LANE), BF16),
            V((toks, states * LANE), F32),
            V((toks, states * LANE), F32),
            V((toks, chans), F32),
            V((toks, chans), F32),
            V((toks, 2 * chans), F32),
            V((toks, chans), F32),
            V((states, SUB, chans), F32),
            V((states, SUB, chans), F32),
            V((states, SUB, chans), F32),
            V((states, chans), F32),
            V((n_seq, states, chans), F32),
            V((states, chans), F32),
            V((layers, states, chans), BF16),
            V((layers, n_seq, states, chans), BF16),
            V((layers, SUB, chans), F32),
            V((layers, n_seq, SUB, chans), F32),
            V((toks, chans), BF16),
            V((2, 2, SIDE, SIDE, quart, feat), BF16),
            V((2, 2, 2, SIDE, eighth, feat), BF16),
            V((2, 2, 2, SIDE, quart, feat), BF16),
            V((2, 2, SIDE, quart, feat), BF16),
            V((2, 2, 2, eighth, feat), BF16),
            V((2, 2, 2, quart, feat), BF16),
            dma((layers, 4)),
            dma((2, 2, 20)),
            dma((2, 2, 20)),
            dma((n_tp,)),
            dma((n_tp,)),
            dma((n_tp,)),
            dma((n_tp,)),
            dma((layers, n_seq)),
            dma((layers, n_seq)),
            dma((layers, n_seq)),
            dma((layers, n_seq)),
            dma((2, 2, 8)),
            dma((2, 2, 8)),
        ],
        compiler_params=pltpu.CompilerParams(
            collective_id=0, has_side_effects=True, vmem_limit_bytes=60 * 1024 * 1024
        ),
    )(
        tokens,
        norm_gain,
        jnp.swapaxes(w_in.reshape(layers, model, 2, chans // LANE, LANE), 2, 3).reshape(
            layers, model * per_d, LANE
        ),
        jnp.swapaxes(w_low, 1, 2),
        w_dt,
        a_rate,
        dt_bias,
        skip_gain,
        threshold,
        w_out,
    )


def solution(mesh):
    in_specs = (
        P("seq", "tp"),
        P(),
        P(None, None, None, "tp"),
        P(None, "tp", None),
        P(None, None, "tp"),
        P(None, None, "tp"),
        P(None, "tp"),
        P(None, "tp"),
        P(None, "tp"),
        P(None, "tp", None),
    )
    return jax.shard_map(
        functools.partial(per_device, mesh.shape["seq"]),
        mesh=mesh,
        in_specs=in_specs,
        out_specs=P("seq", "tp"),
        check_vma=False,
    )
```

```python
import functools
import math

import jax
import jax.numpy as jnp
from jax import lax
from jax.experimental import pallas as pl
from jax.experimental.pallas import tpu as pltpu
from jax.sharding import PartitionSpec as P

MESH = pl.DeviceIdType.MESH
F32 = jnp.float32
BF16 = jnp.bfloat16
SUB = 8
LANE = 128
SIDE = 4
LOG2E = math.log2(math.e)
OFFS = (0, -1, 1, 2)
WIDE = 8
AG_KEYS = (0, 1, 2) + tuple(range(4, 20))


def kernel_body(
    dims,
    tok_ref,
    gain_ref,
    w_in_hbm,
    w_low_hbm,
    w_dt_hbm,
    a_ref,
    bias_ref,
    skip_ref,
    thresh_ref,
    w_out_hbm,
    out_ref,
    raw,
    seld,
    w_in_v,
    w_low_v,
    w_dt_v,
    w_out_v,
    hid,
    agbuf,
    sqv,
    selp,
    arrecv,
    arres,
    expand_b,
    expand_c,
    bx,
    cx,
    step,
    cum,
    proj,
    yv,
    pin,
    ein,
    hst,
    hdev,
    hdec,
    esend_f,
    esend,
    erecv,
    tsend,
    trecv,
    gated,
    pbuf,
    x1,
    x2,
    s2,
    x3,
    wsem,
    ag_s,
    ag_r,
    ar1_s,
    ar1_r,
    ar2_s,
    ar2_r,
    t_s,
    t_r,
    e_s,
    e_r,
    rs_s,
    rs_r,
):
    layers, n_seq, toks, feat, chans, states, rank = dims
    n_tp = SIDE * SIDE
    half = toks // 2
    quart = toks // 4
    eighth = toks // 8
    per_d = 2 * chans // LANE
    steps = toks // SUB
    arow = toks // n_tp
    ncb = chans // LANE
    seqi = lax.axis_index("seq")
    tpi = lax.axis_index("tp")
    zc = tpi // SIDE
    yc = lax.rem(tpi, SIDE)

    def wrap(v):
        return lax.rem(v + 2 * SIDE, SIDE)

    pos = ((yc, zc), (zc, yc))

    def blk(h, c1, c2):
        return c2 * SIDE + c1 if h == 0 else c1 * SIDE + c2

    def nb(h, axis, d):
        p1, p2 = pos[h]
        if axis == 1:
            return {"tp": blk(h, wrap(p1 + d), p2)}
        return {"tp": blk(h, p1, wrap(p2 + d))}

    def rcopy(src, dst, ssem, rsem, dev):
        return pltpu.make_async_remote_copy(
            src_ref=src, dst_ref=dst, send_sem=ssem, recv_sem=rsem,
            device_id=dev, device_id_type=MESH,
        )

    def wcopies(l):
        return (
            pltpu.make_async_copy(w_low_hbm.at[l], w_low_v.at[l, : rank + 2 * states], wsem.at[l, 0]),
            pltpu.make_async_copy(w_dt_hbm.at[l], w_dt_v.at[l], wsem.at[l, 1]),
            pltpu.make_async_copy(w_in_hbm.at[l], raw, wsem.at[l, 2]),
            pltpu.make_async_copy(w_out_hbm.at[l], w_out_v.at[l], wsem.at[l, 3]),
        )

    first_copies = wcopies(0)
    later_copies = wcopies(1)
    for c in (first_copies[0], first_copies[2], first_copies[1], first_copies[3],
              later_copies[0], later_copies[1], later_copies[3]):
        c.start()

    barrier = pltpu.get_barrier_semaphore()
    for d in range(1, n_tp):
        pl.semaphore_signal(barrier, inc=1, device_id={"tp": lax.rem(tpi + d, n_tp)}, device_id_type=MESH)
    for d in range(1, n_seq):
        pl.semaphore_signal(barrier, inc=1, device_id={"seq": lax.rem(seqi + d, n_seq)}, device_id_type=MESH)
    pl.semaphore_wait(barrier, n_tp + n_seq - 2)

    ri = lax.broadcasted_iota(jnp.int32, (toks, toks), 0)
    ci = lax.broadcasted_iota(jnp.int32, (toks, toks), 1)
    perm = jnp.where(ci == lax.rem(ri, SUB) * steps + ri // SUB, 1.0, 0.0).astype(BF16)
    hid[...] = jnp.dot(perm, tok_ref[...], preferred_element_type=F32).astype(BF16)

    def ag_info(u, h, k):
        p1, p2 = pos[h]
        r0 = u * half + h * quart
        full = pl.ds(r0, quart)
        lo = pl.ds(r0, eighth)
        hi = pl.ds(r0 + eighth, eighth)
        if k < 4:
            to = (1, -1, 2)[k]
            src_d, dst_d, rows, ax = 0, -to, full, 1

            def at(d):
                return blk(h, wrap(p1 + d), p2)
        else:
            src_d, dst_d, rows, to = (
                (0, -1, full, 1),
                (0, 1, full, -1),
                (-1, -2, lo, 1),
                (1, 2, hi, -1),
            )[(k - 4) % 4]
            o = OFFS[(k - 4) // 4]
            ax = 2

            def at(d):
                return blk(h, wrap(p1 + o), wrap(p2 + d))

        return at(src_d), at(dst_d), rows, nb(h, ax, to)

    def ag_send(u, h, k):
        src, _, rows, dev = ag_info(u, h, k)
        ref = agbuf.at[src, rows]
        return rcopy(ref, ref, ag_s.at[u, h, k], ag_r.at[u, h, k], dev)

    def ag_start(u, *ks):
        for k in ks:
            for h in range(2):
                ag_send(u, h, k).start()

    def ag_wait(u, *ks):
        for k in ks:
            for h in range(2):
                _, dst, rows, dev = ag_info(u, h, k)
                ref = agbuf.at[dst, rows]
                rcopy(ref, ref, ag_s.at[u, h, k], ag_r.at[u, h, k], dev).wait_recv()

    def publish(l, u):
        rows = pl.ds(u * half, half)
        own = hid[rows, :].astype(F32)
        gain_row = gain_ref[pl.ds(l, 1), pl.ds(pl.multiple_of(tpi * feat, feat), feat)]
        agbuf[tpi, rows] = (own * gain_row).astype(BF16)
        sqv[rows, :] = jnp.broadcast_to(jnp.sum(own * own, axis=1, keepdims=True), (half, LANE))
        ag_start(u, 0, 1, 4, 5, 2)

    publish(0, 0)

    ei = lax.broadcasted_iota(jnp.int32, (LANE, states * LANE), 0)
    ej = lax.broadcasted_iota(jnp.int32, (LANE, states * LANE), 1) // LANE
    expand_b[...] = jnp.where(ei == ej, 1.0, 0.0).astype(BF16)
    expand_c[...] = jnp.where(ei == ej + states, 1.0, 0.0).astype(BF16)
    grp = 2 * LANE // per_d
    gi = lax.broadcasted_iota(jnp.int32, (2 * LANE, 2 * LANE), 0)
    gj = lax.broadcasted_iota(jnp.int32, (2 * LANE, 2 * LANE), 1)
    seld[...] = jnp.where(gj == lax.rem(gi, grp) * per_d + gi // grp, 1.0, 0.0).astype(BF16)
    sel_w = rank + LANE
    pad_from = rank + 2 * states
    for l in range(layers):
        w_low_v[l, pad_from:, :] = jnp.zeros((sel_w - pad_from, feat), BF16)

    def regroup(b0, b1):
        def one(i, unused):
            r = pl.multiple_of(i * WIDE * 2 * LANE, WIDE * 2 * LANE)
            parts = [raw[pl.ds(r + v * 2 * LANE, 2 * LANE), :] for v in range(WIDE)]
            got = jnp.dot(
                seld[...], jnp.concatenate(parts, axis=1), preferred_element_type=F32
            ).astype(BF16)
            d0 = pl.multiple_of(i * WIDE * grp, WIDE * grp)
            for q in range(per_d):
                cols = pl.ds((q % 2) * chans + (q // 2) * LANE, LANE)
                for v in range(WIDE):
                    w_in_v[pl.ds(d0 + v * grp, grp), cols] = got[
                        q * grp : (q + 1) * grp, v * LANE : (v + 1) * LANE
                    ]
            return unused

        lax.fori_loop(b0, b1, one, 0)

    nreg = n_tp * feat // (WIDE * grp)

    def seq_copy(l, src, dst, ss, rs, q, sending):
        slot = seqi if sending else q
        return rcopy(src, dst.at[l, slot], ss.at[l, q], rs.at[l, slot], {"seq": q})

    def t_copy(l, q, sending):
        return seq_copy(l, tsend.at[l], trecv, t_s, t_r, q, sending)

    def e_copy(l, q, sending):
        return seq_copy(l, esend.at[l], erecv, e_s, e_r, q, sending)

    lo = pl.ds(0, eighth)
    hi = pl.ds(eighth, eighth)

    def rpos(h):
        p2, p1 = pos[h]
        return p1, p2

    def rnb(h, axis, d):
        return nb(h, 3 - axis, d)

    def rs_copy(u, h, k):
        p1, p2 = rpos(h)
        src, dst, dev = (
            lambda: (pbuf.at[u, h, wrap(p1 + 2), :, lo], x1.at[u, h, 0], rnb(h, 1, 1)),
            lambda: (pbuf.at[u, h, wrap(p1 + 2), :, hi], x1.at[u, h, 1], rnb(h, 1, -1)),
            lambda: (pbuf.at[u, h, wrap(p1 + 1)], x2.at[u, h, 0], rnb(h, 1, 1)),
            lambda: (pbuf.at[u, h, wrap(p1 - 1)], x2.at[u, h, 1], rnb(h, 1, -1)),
            lambda: (s2.at[u, h, wrap(p2 + 1)], x3.at[u, h, 0], rnb(h, 2, 1)),
            lambda: (s2.at[u, h, wrap(p2 - 1)], x3.at[u, h, 1], rnb(h, 2, -1)),
            lambda: (s2.at[u, h, wrap(p2 + 2)], x3.at[u, h, 2], rnb(h, 2, 2)),
        )[k]()
        return rcopy(src, dst, rs_s.at[u, h, k], rs_r.at[u, h, k], dev)

    def omm(l, u, pairs):
        lhs = gated[u * half : (u + 1) * half, :]
        for dz, dy in pairs:
            z, y = wrap(zc + dz), wrap(yc + dy)
            cols = pl.ds(pl.multiple_of((z * SIDE + y) * feat, feat), feat)
            val = jnp.dot(lhs, w_out_v[l, :, cols], preferred_element_type=F32).astype(BF16)
            pbuf[u, 0, z, y] = val[:quart]
            pbuf[u, 1, y, z] = val[quart:]

    def rs1(l, u):
        omm(l, u, ((2, 0), (2, 1), (2, 2), (2, 3), (0, 2), (1, 2), (3, 2)))
        for h in range(2):
            rs_copy(u, h, 0).start()
            rs_copy(u, h, 1).start()

    def rs2(u):
        for h in range(2):
            p1, _ = rpos(h)
            up = wrap(p1 + 1)
            dn = wrap(p1 - 1)
            rs_copy(u, h, 0).wait_recv()
            pbuf[u, h, up, :, lo] = (
                pbuf[u, h, up, :, lo].astype(F32) + x1[u, h, 0].astype(F32)
            ).astype(BF16)
            rs_copy(u, h, 2).start()
            rs_copy(u, h, 1).wait_recv()
            pbuf[u, h, dn, :, hi] = (
                pbuf[u, h, dn, :, hi].astype(F32) + x1[u, h, 1].astype(F32)
            ).astype(BF16)
            rs_copy(u, h, 3).start()

    def sum3(u, h, p1, c2):
        return (
            pbuf[u, h, p1, c2].astype(F32) + x2[u, h, 0, c2].astype(F32) + x2[u, h, 1, c2].astype(F32)
        )

    def rs3(u):
        for h in range(2):
            p1, p2 = rpos(h)
            rs_copy(u, h, 2).wait_recv()
            rs_copy(u, h, 3).wait_recv()
            for k, d in ((6, 2), (4, 1), (5, -1)):
                c2 = wrap(p2 + d)
                s2[u, h, c2] = sum3(u, h, p1, c2).astype(BF16)
                rs_copy(u, h, k).start()

    def rs4(u):
        for h in range(2):
            p1, p2 = rpos(h)
            total = sum3(u, h, p1, p2)
            for k in range(3):
                rs_copy(u, h, 4 + k).wait_recv()
                total = total + x3[u, h, k].astype(F32)
            rows = pl.ds(u * half + h * quart, quart)
            hid[rows, :] = (hid[rows, :].astype(F32) + total).astype(BF16)

    def layer(l, unused):
        low_c, dt_c, in_c, out_c = wcopies(l)
        publish(l, 1)

        low_c.wait()
        selv = lax.dot_general(
            agbuf[tpi], w_low_v[l], (((1,), (1,)), ((), ())), preferred_element_type=F32
        )
        sq = sqv[:, 0:1]
        sq_hi = sq.astype(BF16).astype(F32)
        lane = lax.broadcasted_iota(jnp.int32, (toks, sel_w), 1)
        selv = jnp.where(lane == pad_from, sq_hi, selv)
        selv = jnp.where(lane == pad_from + 1, sq - sq_hi, selv)
        selp[...] = selv.astype(BF16)
        arrecv[tpi] = selp[pl.ds(pl.multiple_of(tpi * arow, arow), arow), :]

        def ar1(d, sending):
            to = lax.rem(tpi + d, n_tp)
            fr = lax.rem(tpi + n_tp - d, n_tp)
            rows = pl.ds(pl.multiple_of(to * arow, arow), arow)
            dst = arrecv.at[tpi] if sending else arrecv.at[fr]
            return rcopy(selp.at[rows], dst, ar1_s.at[d], ar1_r.at[d], {"tp": to})

        for d in range(1, n_tp):
            ar1(d, True).start()

        @pl.when(l == 0)
        def _():
            in_c.wait()

        ag_wait(0, 0, 1)
        ag_start(0, 8, 9, 12, 13)
        ag_wait(0, 4, 5)
        ag_start(0, 6, 7)
        ag_wait(0, 2)
        ag_start(0, 16, 17)

        @pl.when(l == 0)
        def _():
            regroup(0, nreg // 4)

        ag_wait(1, 0, 1)
        ag_start(1, 8, 9, 12, 13)
        ag_wait(1, 4, 5)
        ag_start(1, 6, 7)
        ag_wait(1, 2)
        ag_start(1, 16, 17)
        ag_wait(0, 8, 9)
        ag_start(0, 10, 11)
        ag_wait(0, 12, 13)
        ag_start(0, 14, 15)
        ag_wait(0, 16, 17)
        ag_start(0, 18, 19)

        for d in range(1, n_tp):
            ar1(d, False).wait_recv()
        tot = jnp.zeros((arow, sel_w), F32)
        for i in range(n_tp):
            tot = tot + arrecv[i].astype(F32)
        lane = lax.broadcasted_iota(jnp.int32, (arow, sel_w), 1)
        is_sq = (lane == pad_from) | (lane == pad_from + 1)
        ssum = jnp.sum(jnp.where(is_sq, tot, 0.0), axis=1, keepdims=True)
        factor = lax.rsqrt(ssum / (n_tp * feat) + 1e-05)
        f_hi = factor.astype(BF16).astype(F32)
        tot = jnp.where(lane == pad_from, f_hi, jnp.where(lane == pad_from + 1, factor - f_hi, tot * factor))
        mine = pl.ds(pl.multiple_of(tpi * arow, arow), arow)
        arres[mine, :] = tot.astype(BF16)

        def ar2(d, sending):
            to = lax.rem(tpi + d, n_tp)
            fr = lax.rem(tpi + n_tp - d, n_tp)
            base = tpi if sending else fr
            rows = pl.ds(pl.multiple_of(base * arow, arow), arow)
            return rcopy(arres.at[rows], arres.at[rows], ar2_s.at[d], ar2_r.at[d], {"tp": to})

        for d in range(1, n_tp):
            ar2(d, True).start()

        @pl.when(l == 0)
        def _():
            regroup(nreg // 4, nreg // 2)

        ag_wait(1, 8, 9)
        ag_start(1, 10, 11)
        ag_wait(1, 12, 13)
        ag_start(1, 14, 15)
        ag_wait(1, 16, 17)
        ag_start(1, 18, 19)

        @pl.when(l == 0)
        def _():
            regroup(nreg // 2, nreg)
            later_copies[2].start()

        for d in range(1, n_tp):
            ar2(d, False).wait_recv()
        tail = arres[:, rank:]
        tl = lax.broadcasted_iota(jnp.int32, (toks, LANE), 1)
        in_f = (tl == 2 * states) | (tl == 2 * states + 1)
        fac = jnp.sum(jnp.where(in_f, tail.astype(F32), 0.0), axis=1, keepdims=True)
        dt_c.wait()
        pre = jnp.dot(arres[:, :rank], w_dt_v[l], preferred_element_type=F32) + bias_ref[pl.ds(l, 1), :]
        step[...] = jnp.maximum(pre, 0.0) + jnp.log1p(jnp.exp(-jnp.abs(pre)))
        bx[...] = jnp.dot(tail, expand_b[...], preferred_element_type=F32)
        cx[...] = jnp.dot(tail, expand_c[...], preferred_element_type=F32)

        def accum(t, run):
            rows = pl.ds(pl.multiple_of(t * SUB, SUB), SUB)
            run = run + step[rows, :]
            cum[rows, :] = run
            return run

        ctot = lax.fori_loop(0, steps, accum, jnp.zeros((SUB, chans), F32))
        tsend[l] = jnp.broadcast_to(jnp.sum(ctot, axis=0, keepdims=True), (SUB, chans))
        for q in range(1, n_seq):
            @pl.when(q > seqi)
            def _():
                t_copy(l, q, True).start()

        skip_row = skip_ref[pl.ds(l, 1), :]
        th_row = thresh_ref[pl.ds(l, 1), :]

        def mm(u, first, pairs):
            rs = pl.ds(u * half, half)
            for i, (dz, dy) in enumerate(pairs):
                b = wrap(zc + dz) * SIDE + wrap(yc + dy)
                rows = pl.ds(pl.multiple_of(b * feat, feat), feat)
                val = jnp.dot(agbuf[b, rs], w_in_v[rows, :], preferred_element_type=F32)
                if first and i == 0:
                    proj[rs, :] = val
                else:
                    proj[rs, :] += val

        near = ((0, 0), (0, 1), (0, -1), (1, 0), (-1, 0), (1, 1), (1, -1), (-1, 1), (-1, -1))
        away = ((2, 0), (2, 1), (2, 2), (2, 3), (0, 2), (1, 2), (3, 2))

        def scan(u):
            for cb in range(ncb):
                cs = pl.ds(cb * LANE, LANE)
                na = [
                    jnp.broadcast_to(a_ref[l, s : s + 1, cs] * (-LOG2E), (SUB, LANE))
                    for s in range(states)
                ]
                skip = skip_row[:, cb * LANE : (cb + 1) * LANE]

                def scan_step(t, hs):
                    rows = pl.ds(pl.multiple_of(t * SUB, SUB), SUB)
                    st = step[rows, cs]
                    cur = proj[rows, cs]
                    dr = st * cur
                    acc = skip * cur
                    new = []
                    for s in range(states):
                        ls = pl.ds(s * LANE, LANE)
                        hn = jnp.exp2(st * na[s]) * hs[s] + bx[rows, ls] * dr
                        acc = acc + cx[rows, ls] * hn
                        new.append(hn)
                    yv[rows, cs] = acc
                    return tuple(new)

                if u == 0:
                    init = tuple(jnp.zeros((SUB, LANE), F32) for _ in range(states))
                else:
                    init = tuple(hst[s, :, cs] for s in range(states))
                hs = lax.fori_loop(u * steps // 2, (u + 1) * steps // 2, scan_step, init, unroll=2)
                if u == 0:
                    for s in range(states):
                        hst[s, :, cs] = hs[s]
                    continue
                sub = lax.broadcasted_iota(jnp.int32, (SUB, LANE), 0)
                ct = cum[pl.ds((steps - 1) * SUB, SUB), cs]
                for s in range(states):
                    e = hs[s]
                    p = jnp.exp2(ct * na[s])
                    for d in (1, 2, 4):
                        ok = sub >= d
                        e = e + jnp.where(ok, p * pltpu.roll(e, d, 0), 0.0)
                        p = p * jnp.where(ok, pltpu.roll(p, d, 0), 1.0)
                    esend_f[s : s + 1, cs] = e[SUB - 1 : SUB, :]
                    ein[s, :, cs] = jnp.where(sub >= 1, pltpu.roll(e, 1, 0), 0.0)
                    pin[s, :, cs] = jnp.where(sub >= 1, pltpu.roll(p, 1, 0), 1.0)

        ag_wait(0, 6, 7, 10, 11, 14, 15, 18, 19)
        mm(0, True, near + away)
        proj[:half, :] = proj[:half, :] * fac[:half]
        scan(0)
        mm(1, True, near)
        ag_wait(1, 6, 7, 10, 11, 14, 15, 18, 19)
        mm(1, False, away)
        proj[half:, :] = proj[half:, :] * fac[half:]
        scan(1)

        esend[l] = esend_f[...].astype(BF16)
        for q in range(1, n_seq):
            @pl.when(q > seqi)
            def _():
                e_copy(l, q, True).start()

        for u in range(2):
            for k in AG_KEYS:
                for h in range(2):
                    ag_send(u, h, k).wait_send()
        for d in range(1, n_tp):
            ar1(d, True).wait_send()
            ar2(d, True).wait_send()

        rates = a_ref[l] * (-LOG2E)
        for q in range(n_seq - 1):
            @pl.when(q < seqi)
            def _():
                t_copy(l, q, False).wait_recv()
                hdec[q] = jnp.exp2(rates * trecv[l, q, 0:1, :])

        hdev[...] = jnp.zeros_like(hdev)
        for q in range(n_seq - 1):
            @pl.when(q < seqi)
            def _():
                e_copy(l, q, False).wait_recv()
                hdev[...] = hdec[q] * hdev[...] + erecv[l, q].astype(F32)

        def finish(u, c0, c1):
            rs = pl.ds(u * half, half)
            for cb in range(c0, c1):
                cs = pl.ds(cb * LANE, LANE)
                na = [
                    jnp.broadcast_to(a_ref[l, s : s + 1, cs] * (-LOG2E), (SUB, LANE))
                    for s in range(states)
                ]
                hin = [ein[s, :, cs] + pin[s, :, cs] * hdev[s : s + 1, cs] for s in range(states)]
                th = th_row[:, cb * LANE : (cb + 1) * LANE]

                def fold(t, unused):
                    rows = pl.ds(pl.multiple_of(t * SUB, SUB), SUB)
                    ct = cum[rows, cs]
                    acc = yv[rows, cs]
                    for s in range(states):
                        ls = pl.ds(s * LANE, LANE)
                        acc = acc + cx[rows, ls] * (jnp.exp2(ct * na[s]) * hin[s])
                    yv[rows, cs] = acc
                    return unused

                lax.fori_loop(u * steps // 2, (u + 1) * steps // 2, fold, 0, unroll=4)

                mixed = yv[rs, cs]
                fct = lax.rsqrt(jnp.mean(mixed * mixed, axis=1, keepdims=True) + 1e-05)
                normal = mixed * fct
                shrunk = jnp.maximum(normal - th, 0.0) - jnp.maximum(-normal - th, 0.0)
                gate = proj[rs, pl.ds(chans + cb * LANE, LANE)]
                gated[rs, cs] = (shrunk * (gate / (1.0 + jnp.exp(-gate)))).astype(BF16)

        others = ((0, 0), (0, 1), (0, -1), (1, 0), (-1, 0), (1, 1), (1, -1), (-1, 1), (-1, -1))
        finish(0, 0, ncb)
        out_c.wait()
        rs1(l, 0)
        omm(l, 0, others)
        finish(1, 0, ncb // 2)
        rs2(0)
        finish(1, ncb // 2, ncb)
        rs1(l, 1)
        omm(l, 1, others)

        @pl.when(l + 1 < layers)
        def _():
            later_copies[2].wait()
            regroup(0, nreg // 4)

        rs2(1)
        rs3(0)

        @pl.when(l + 1 < layers)
        def _():
            regroup(nreg // 4, nreg // 2)

        rs4(0)

        @pl.when(l + 1 < layers)
        def _():
            publish(l + 1, 0)
            regroup(nreg // 2, nreg)

        rs3(1)
        rs4(1)
        for u in range(2):
            for h in range(2):
                for k in range(7):
                    rs_copy(u, h, k).wait_send()
        for q in range(1, n_seq):
            @pl.when(q > seqi)
            def _():
                t_copy(l, q, True).wait_send()
                e_copy(l, q, True).wait_send()
        return unused

    lax.fori_loop(0, layers, layer, 0)
    out_ref[...] = lax.dot_general(
        perm, hid[...], (((0,), (0,)), ((), ())), preferred_element_type=F32
    ).astype(BF16)


def per_device(n_seq, tokens, norm_gain, w_in, w_low, w_dt, a_rate, dt_bias, skip_gain, threshold, w_out):
    toks, feat = tokens.shape
    layers, model, _, chans = w_in.shape
    states = a_rate.shape[1]
    rank = w_dt.shape[1]
    n_tp = SIDE * SIDE
    half, quart, eighth = toks // 2, toks // 4, toks // 8
    per_d = 2 * chans // LANE
    sel_w = rank + LANE
    dims = (layers, n_seq, toks, feat, chans, states, rank)
    vm = pl.BlockSpec(memory_space=pltpu.VMEM)
    hb = pl.BlockSpec(memory_space=pl.ANY)
    dma = pltpu.SemaphoreType.DMA
    V = pltpu.VMEM
    return pl.pallas_call(
        functools.partial(kernel_body, dims),
        out_shape=jax.ShapeDtypeStruct((toks, feat), BF16),
        in_specs=[vm, vm, hb, hb, hb, vm, vm, vm, vm, hb],
        out_specs=vm,
        scratch_shapes=[
            V((model * per_d, LANE), BF16),
            V((2 * LANE, 2 * LANE), BF16),
            V((model, 2 * chans), BF16),
            V((layers, sel_w, feat), BF16),
            V((layers, rank, chans), BF16),
            V((layers, chans, model), BF16),
            V((toks, feat), BF16),
            V((n_tp, toks, feat), BF16),
            V((toks, LANE), F32),
            V((toks, sel_w), BF16),
            V((n_tp, toks // n_tp, sel_w), BF16),
            V((toks, sel_w), BF16),
            V((LANE, states * LANE), BF16),
            V((LANE, states * LANE), BF16),
            V((toks, states * LANE), F32),
            V((toks, states * LANE), F32),
            V((toks, chans), F32),
            V((toks, chans), F32),
            V((toks, 2 * chans), F32),
            V((toks, chans), F32),
            V((states, SUB, chans), F32),
            V((states, SUB, chans), F32),
            V((states, SUB, chans), F32),
            V((states, chans), F32),
            V((n_seq, states, chans), F32),
            V((states, chans), F32),
            V((layers, states, chans), BF16),
            V((layers, n_seq, states, chans), BF16),
            V((layers, SUB, chans), F32),
            V((layers, n_seq, SUB, chans), F32),
            V((toks, chans), BF16),
            V((2, 2, SIDE, SIDE, quart, feat), BF16),
            V((2, 2, 2, SIDE, eighth, feat), BF16),
            V((2, 2, 2, SIDE, quart, feat), BF16),
            V((2, 2, SIDE, quart, feat), BF16),
            V((2, 2, 3, quart, feat), BF16),
            dma((layers, 4)),
            dma((2, 2, 20)),
            dma((2, 2, 20)),
            dma((n_tp,)),
            dma((n_tp,)),
            dma((n_tp,)),
            dma((n_tp,)),
            dma((layers, n_seq)),
            dma((layers, n_seq)),
            dma((layers, n_seq)),
            dma((layers, n_seq)),
            dma((2, 2, 8)),
            dma((2, 2, 8)),
        ],
        compiler_params=pltpu.CompilerParams(
            collective_id=0, has_side_effects=True, vmem_limit_bytes=60 * 1024 * 1024
        ),
    )(
        tokens,
        norm_gain,
        jnp.swapaxes(w_in.reshape(layers, model, 2, chans // LANE, LANE), 2, 3).reshape(
            layers, model * per_d, LANE
        ),
        jnp.swapaxes(w_low, 1, 2),
        w_dt,
        a_rate,
        dt_bias,
        skip_gain,
        threshold,
        w_out,
    )


def solution(mesh):
    in_specs = (
        P("seq", "tp"),
        P(),
        P(None, None, None, "tp"),
        P(None, "tp", None),
        P(None, None, "tp"),
        P(None, None, "tp"),
        P(None, "tp"),
        P(None, "tp"),
        P(None, "tp"),
        P(None, "tp", None),
    )
    return jax.shard_map(
        functools.partial(per_device, mesh.shape["seq"]),
        mesh=mesh,
        in_specs=in_specs,
        out_specs=P("seq", "tp"),
        check_vma=False,
    )
```

```python
import functools
import math

import jax
import jax.numpy as jnp
from jax import lax
from jax.experimental import pallas as pl
from jax.experimental.pallas import tpu as pltpu
from jax.sharding import PartitionSpec as P

MESH = pl.DeviceIdType.MESH
F32 = jnp.float32
BF16 = jnp.bfloat16
SUB = 8
LANE = 128
SIDE = 4
LOG2E = math.log2(math.e)
OFFS = (0, -1, 1, 2)
OUT = (2, 1, -1, 0)
WIDE = 8
AG_KEYS = (0, 1, 2) + tuple(range(4, 20))


def kernel_body(
    dims,
    tok_ref,
    gain_ref,
    w_in_hbm,
    w_low_hbm,
    w_dt_hbm,
    a_ref,
    bias_ref,
    skip_ref,
    thresh_ref,
    w_out_hbm,
    out_ref,
    raw,
    seld,
    w_in_v,
    w_low_v,
    w_dt_v,
    w_out_v,
    hid,
    agbuf,
    sqv,
    selp,
    arrecv,
    arres,
    expand_b,
    expand_c,
    bx,
    cx,
    step,
    cum,
    proj,
    yv,
    pin,
    ein,
    hst,
    hdev,
    hdec,
    esend_f,
    esend,
    erecv,
    tsend,
    trecv,
    gated,
    pbuf,
    x1,
    x2,
    s2,
    x3,
    wsem,
    ag_s,
    ag_r,
    ar1_s,
    ar1_r,
    ar2_s,
    ar2_r,
    t_s,
    t_r,
    e_s,
    e_r,
    rs_s,
    rs_r,
):
    layers, n_seq, toks, feat, chans, states, rank = dims
    n_tp = SIDE * SIDE
    half = toks // 2
    quart = toks // 4
    eighth = toks // 8
    per_d = 2 * chans // LANE
    steps = toks // SUB
    arow = toks // n_tp
    ncb = chans // LANE
    seqi = lax.axis_index("seq")
    tpi = lax.axis_index("tp")
    zc = tpi // SIDE
    yc = lax.rem(tpi, SIDE)

    def wrap(v):
        return lax.rem(v + 2 * SIDE, SIDE)

    pos = ((yc, zc), (zc, yc))

    def blk(h, c1, c2):
        return c2 * SIDE + c1 if h == 0 else c1 * SIDE + c2

    def nb(h, axis, d):
        p1, p2 = pos[h]
        if axis == 1:
            return {"tp": blk(h, wrap(p1 + d), p2)}
        return {"tp": blk(h, p1, wrap(p2 + d))}

    def rcopy(src, dst, ssem, rsem, dev):
        return pltpu.make_async_remote_copy(
            src_ref=src, dst_ref=dst, send_sem=ssem, recv_sem=rsem,
            device_id=dev, device_id_type=MESH,
        )

    def wcopies(l):
        return (
            pltpu.make_async_copy(w_low_hbm.at[l], w_low_v.at[l, : rank + 2 * states], wsem.at[l, 0]),
            pltpu.make_async_copy(w_dt_hbm.at[l], w_dt_v.at[l], wsem.at[l, 1]),
            pltpu.make_async_copy(w_in_hbm.at[l], raw, wsem.at[l, 2]),
            pltpu.make_async_copy(w_out_hbm.at[l], w_out_v.at[l], wsem.at[l, 3]),
        )

    first_copies = wcopies(0)
    later_copies = wcopies(1)
    for c in (first_copies[0], first_copies[2]):
        c.start()

    barrier = pltpu.get_barrier_semaphore()
    for d in range(1, n_tp):
        pl.semaphore_signal(barrier, inc=1, device_id={"tp": lax.rem(tpi + d, n_tp)}, device_id_type=MESH)
    for d in range(1, n_seq):
        pl.semaphore_signal(barrier, inc=1, device_id={"seq": lax.rem(seqi + d, n_seq)}, device_id_type=MESH)
    pl.semaphore_wait(barrier, n_tp + n_seq - 2)

    ri = lax.broadcasted_iota(jnp.int32, (toks, toks), 0)
    ci = lax.broadcasted_iota(jnp.int32, (toks, toks), 1)
    perm = jnp.where(ci == lax.rem(ri, SUB) * steps + ri // SUB, 1.0, 0.0).astype(BF16)
    hid[...] = jnp.dot(perm, tok_ref[...], preferred_element_type=F32).astype(BF16)

    def ag_info(u, h, k):
        p1, p2 = pos[h]
        r0 = u * half + h * quart
        full = pl.ds(r0, quart)
        lo = pl.ds(r0, eighth)
        hi = pl.ds(r0 + eighth, eighth)
        if k < 4:
            to = (1, -1, 2)[k]
            src_d, dst_d, rows, ax = 0, -to, full, 1

            def at(d):
                return blk(h, wrap(p1 + d), p2)
        else:
            src_d, dst_d, rows, to = (
                (0, -1, full, 1),
                (0, 1, full, -1),
                (-1, -2, lo, 1),
                (1, 2, hi, -1),
            )[(k - 4) % 4]
            o = OFFS[(k - 4) // 4]
            ax = 2

            def at(d):
                return blk(h, wrap(p1 + o), wrap(p2 + d))

        return at(src_d), at(dst_d), rows, nb(h, ax, to)

    def ag_send(u, h, k):
        src, _, rows, dev = ag_info(u, h, k)
        ref = agbuf.at[src, rows]
        return rcopy(ref, ref, ag_s.at[u, h, k], ag_r.at[u, h, k], dev)

    def ag_start(u, *ks):
        for k in ks:
            for h in range(2):
                ag_send(u, h, k).start()

    def ag_wait(u, *ks):
        for k in ks:
            for h in range(2):
                _, dst, rows, dev = ag_info(u, h, k)
                ref = agbuf.at[dst, rows]
                rcopy(ref, ref, ag_s.at[u, h, k], ag_r.at[u, h, k], dev).wait_recv()

    def publish(l, u):
        rows = pl.ds(u * half, half)
        own = hid[rows, :].astype(F32)
        gain_row = gain_ref[pl.ds(l, 1), pl.ds(pl.multiple_of(tpi * feat, feat), feat)]
        agbuf[tpi, rows] = (own * gain_row).astype(BF16)
        sqv[rows, :] = jnp.broadcast_to(jnp.sum(own * own, axis=1, keepdims=True), (half, LANE))
        ag_start(u, 0, 1, 4, 5, 2)

    publish(0, 0)

    ei = lax.broadcasted_iota(jnp.int32, (LANE, states * LANE), 0)
    ej = lax.broadcasted_iota(jnp.int32, (LANE, states * LANE), 1) // LANE
    expand_b[...] = jnp.where(ei == ej, 1.0, 0.0).astype(BF16)
    expand_c[...] = jnp.where(ei == ej + states, 1.0, 0.0).astype(BF16)
    grp = 2 * LANE // per_d
    gi = lax.broadcasted_iota(jnp.int32, (2 * LANE, 2 * LANE), 0)
    gj = lax.broadcasted_iota(jnp.int32, (2 * LANE, 2 * LANE), 1)
    seld[...] = jnp.where(gj == lax.rem(gi, grp) * per_d + gi // grp, 1.0, 0.0).astype(BF16)
    sel_w = rank + LANE
    pad_from = rank + 2 * states
    for l in range(layers):
        w_low_v[l, pad_from:, :] = jnp.zeros((sel_w - pad_from, feat), BF16)

    def regroup(b0, b1):
        def one(i, unused):
            r = pl.multiple_of(i * WIDE * 2 * LANE, WIDE * 2 * LANE)
            parts = [raw[pl.ds(r + v * 2 * LANE, 2 * LANE), :] for v in range(WIDE)]
            got = jnp.dot(
                seld[...], jnp.concatenate(parts, axis=1), preferred_element_type=F32
            ).astype(BF16)
            d0 = pl.multiple_of(i * WIDE * grp, WIDE * grp)
            for q in range(per_d):
                cols = pl.ds((q % 2) * chans + (q // 2) * LANE, LANE)
                for v in range(WIDE):
                    w_in_v[pl.ds(d0 + v * grp, grp), cols] = got[
                        q * grp : (q + 1) * grp, v * LANE : (v + 1) * LANE
                    ]
            return unused

        lax.fori_loop(b0, b1, one, 0)

    nreg = n_tp * feat // (WIDE * grp)

    def seq_copy(l, src, dst, ss, rs, q, sending):
        slot = seqi if sending else q
        return rcopy(src, dst.at[l, slot], ss.at[l, q], rs.at[l, slot], {"seq": q})

    def t_copy(l, q, sending):
        return seq_copy(l, tsend.at[l], trecv, t_s, t_r, q, sending)

    def e_copy(l, q, sending):
        return seq_copy(l, esend.at[l], erecv, e_s, e_r, q, sending)

    lo = pl.ds(0, eighth)
    hi = pl.ds(eighth, eighth)

    def rpos(h):
        p2, p1 = pos[h]
        return p1, p2

    def rnb(h, axis, d):
        return nb(h, 3 - axis, d)

    ahead, up, down, here = range(SIDE)
    parts = (pl.ds(0, 2), pl.ds(2, 2))

    def rs_copy(u, h, k):
        if k < 8:
            piece = parts[(k // 2) % 2]
            way = k % 2
            if k < 4:
                src = pbuf.at[u, h, ahead, piece, (lo, hi)[way]]
                dst = x1.at[u, h, way, piece]
            else:
                src = pbuf.at[u, h, (up, down)[way], piece]
                dst = x2.at[u, h, way, piece]
            dev = rnb(h, 1, (1, -1)[way])
        else:
            src = s2.at[u, h, (ahead, up, down)[k - 8]]
            dst = x3.at[u, h, k - 8]
            dev = rnb(h, 2, OUT[k - 8])
        return rcopy(src, dst, rs_s.at[u, h, k], rs_r.at[u, h, k], dev)

    def omm(l, u, pairs):
        lhs = gated[u * half : (u + 1) * half, :]
        for dz, dy in pairs:
            z, y = wrap(zc + dz), wrap(yc + dy)
            cols = pl.ds(pl.multiple_of((z * SIDE + y) * feat, feat), feat)
            val = jnp.dot(lhs, w_out_v[l, :, cols], preferred_element_type=F32).astype(BF16)
            iz, iy = OUT.index(dz), OUT.index(dy)
            pbuf[u, 0, iz, iy] = val[:quart]
            pbuf[u, 1, iy, iz] = val[quart:]

    def rs1(l, u):
        omm(l, u, ((2, 2), (2, 1), (1, 2)))
        for h in range(2):
            rs_copy(u, h, 0).start()
            rs_copy(u, h, 1).start()
        omm(l, u, ((2, -1), (2, 0), (-1, 2), (0, 2)))
        for h in range(2):
            rs_copy(u, h, 2).start()
            rs_copy(u, h, 3).start()
        omm(l, u, ((1, 1), (1, -1), (1, 0), (-1, 1), (-1, -1), (-1, 0), (0, 1), (0, -1)))
        omm(l, u, ((0, 0),))

    def rs2(u):
        for p in range(2):
            piece = parts[p]
            for h in range(2):
                for way in range(2):
                    rows = (lo, hi)[way]
                    side = (up, down)[way]
                    rs_copy(u, h, 2 * p + way).wait_recv()
                    pbuf[u, h, side, piece, rows] = (
                        pbuf[u, h, side, piece, rows].astype(F32) + x1[u, h, way, piece].astype(F32)
                    ).astype(BF16)
                    rs_copy(u, h, 4 + 2 * p + way).start()

    def sum3(u, h, c2):
        return (
            pbuf[u, h, here, c2].astype(F32) + x2[u, h, 0, c2].astype(F32) + x2[u, h, 1, c2].astype(F32)
        )

    def rs3(u):
        for p in range(2):
            for h in range(2):
                rs_copy(u, h, 4 + 2 * p).wait_recv()
                rs_copy(u, h, 5 + 2 * p).wait_recv()
                for c2 in (ahead, up) if p == 0 else (down,):
                    s2[u, h, c2] = sum3(u, h, c2).astype(BF16)
                    rs_copy(u, h, 8 + c2).start()

    def rs4(u):
        for h in range(2):
            total = sum3(u, h, here)
            for k in range(3):
                rs_copy(u, h, 8 + k).wait_recv()
                total = total + x3[u, h, k].astype(F32)
            rows = pl.ds(u * half + h * quart, quart)
            hid[rows, :] = (hid[rows, :].astype(F32) + total).astype(BF16)

    def layer(l, unused):
        low_c, dt_c, in_c, out_c = wcopies(l)
        publish(l, 1)

        low_c.wait()
        selv = lax.dot_general(
            agbuf[tpi], w_low_v[l], (((1,), (1,)), ((), ())), preferred_element_type=F32
        )
        sq = sqv[:, 0:1]
        sq_hi = sq.astype(BF16).astype(F32)
        lane = lax.broadcasted_iota(jnp.int32, (toks, sel_w), 1)
        selv = jnp.where(lane == pad_from, sq_hi, selv)
        selv = jnp.where(lane == pad_from + 1, sq - sq_hi, selv)
        selp[...] = selv.astype(BF16)
        arrecv[tpi] = selp[pl.ds(pl.multiple_of(tpi * arow, arow), arow), :]

        def ar1(d, sending):
            to = lax.rem(tpi + d, n_tp)
            fr = lax.rem(tpi + n_tp - d, n_tp)
            rows = pl.ds(pl.multiple_of(to * arow, arow), arow)
            dst = arrecv.at[tpi] if sending else arrecv.at[fr]
            return rcopy(selp.at[rows], dst, ar1_s.at[d], ar1_r.at[d], {"tp": to})

        for d in range(1, n_tp):
            ar1(d, True).start()

        ag_wait(0, 0, 1)
        ag_start(0, 8, 9, 12, 13)
        ag_wait(0, 4, 5)
        ag_start(0, 6, 7)
        ag_wait(0, 2)
        ag_start(0, 16, 17)

        @pl.when(l == 0)
        def _():
            in_c.wait()
            for c in (first_copies[1], first_copies[3], later_copies[0], later_copies[1], later_copies[3]):
                c.start()
            regroup(0, nreg // 4)

        ag_wait(1, 0, 1)
        ag_start(1, 8, 9, 12, 13)
        ag_wait(1, 4, 5)
        ag_start(1, 6, 7)
        ag_wait(1, 2)
        ag_start(1, 16, 17)
        ag_wait(0, 8, 9)
        ag_start(0, 10, 11)
        ag_wait(0, 12, 13)
        ag_start(0, 14, 15)
        ag_wait(0, 16, 17)
        ag_start(0, 18, 19)

        for d in range(1, n_tp):
            ar1(d, False).wait_recv()
        tot = jnp.zeros((arow, sel_w), F32)
        for i in range(n_tp):
            tot = tot + arrecv[i].astype(F32)
        lane = lax.broadcasted_iota(jnp.int32, (arow, sel_w), 1)
        is_sq = (lane == pad_from) | (lane == pad_from + 1)
        ssum = jnp.sum(jnp.where(is_sq, tot, 0.0), axis=1, keepdims=True)
        factor = lax.rsqrt(ssum / (n_tp * feat) + 1e-05)
        f_hi = factor.astype(BF16).astype(F32)
        tot = jnp.where(lane == pad_from, f_hi, jnp.where(lane == pad_from + 1, factor - f_hi, tot * factor))
        mine = pl.ds(pl.multiple_of(tpi * arow, arow), arow)
        arres[mine, :] = tot.astype(BF16)

        def ar2(d, sending):
            to = lax.rem(tpi + d, n_tp)
            fr = lax.rem(tpi + n_tp - d, n_tp)
            base = tpi if sending else fr
            rows = pl.ds(pl.multiple_of(base * arow, arow), arow)
            return rcopy(arres.at[rows], arres.at[rows], ar2_s.at[d], ar2_r.at[d], {"tp": to})

        for d in range(1, n_tp):
            ar2(d, True).start()

        @pl.when(l == 0)
        def _():
            regroup(nreg // 4, nreg // 2)

        ag_wait(1, 8, 9)
        ag_start(1, 10, 11)
        ag_wait(1, 12, 13)
        ag_start(1, 14, 15)
        ag_wait(1, 16, 17)
        ag_start(1, 18, 19)

        @pl.when(l == 0)
        def _():
            regroup(nreg // 2, nreg)
            later_copies[2].start()

        for d in range(1, n_tp):
            ar2(d, False).wait_recv()
        tail = arres[:, rank:]
        tl = lax.broadcasted_iota(jnp.int32, (toks, LANE), 1)
        in_f = (tl == 2 * states) | (tl == 2 * states + 1)
        fac = jnp.sum(jnp.where(in_f, tail.astype(F32), 0.0), axis=1, keepdims=True)
        dt_c.wait()
        pre = jnp.dot(arres[:, :rank], w_dt_v[l], preferred_element_type=F32) + bias_ref[pl.ds(l, 1), :]
        step[...] = jnp.maximum(pre, 0.0) + jnp.log1p(jnp.exp(-jnp.abs(pre)))
        bx[...] = jnp.dot(tail, expand_b[...], preferred_element_type=F32)
        cx[...] = jnp.dot(tail, expand_c[...], preferred_element_type=F32)

        def accum(t, run):
            rows = pl.ds(pl.multiple_of(t * SUB, SUB), SUB)
            run = run + step[rows, :]
            cum[rows, :] = run
            return run

        ctot = lax.fori_loop(0, steps, accum, jnp.zeros((SUB, chans), F32))
        tsend[l] = jnp.broadcast_to(jnp.sum(ctot, axis=0, keepdims=True), (SUB, chans))
        for q in range(1, n_seq):
            @pl.when(q > seqi)
            def _():
                t_copy(l, q, True).start()

        skip_row = skip_ref[pl.ds(l, 1), :]
        th_row = thresh_ref[pl.ds(l, 1), :]

        def mm(u, first, pairs):
            rs = pl.ds(u * half, half)
            for i, (dz, dy) in enumerate(pairs):
                b = wrap(zc + dz) * SIDE + wrap(yc + dy)
                rows = pl.ds(pl.multiple_of(b * feat, feat), feat)
                val = jnp.dot(agbuf[b, rs], w_in_v[rows, :], preferred_element_type=F32)
                if first and i == 0:
                    proj[rs, :] = val
                else:
                    proj[rs, :] += val

        near = ((0, 0), (0, 1), (0, -1), (1, 0), (-1, 0), (1, 1), (1, -1), (-1, 1), (-1, -1))
        away = ((2, 0), (2, 1), (2, 2), (2, 3), (0, 2), (1, 2), (3, 2))

        def scan(u):
            for cb in range(ncb):
                cs = pl.ds(cb * LANE, LANE)
                na = [
                    jnp.broadcast_to(a_ref[l, s : s + 1, cs] * (-LOG2E), (SUB, LANE))
                    for s in range(states)
                ]
                skip = skip_row[:, cb * LANE : (cb + 1) * LANE]

                def scan_step(t, hs):
                    rows = pl.ds(pl.multiple_of(t * SUB, SUB), SUB)
                    st = step[rows, cs]
                    cur = proj[rows, cs]
                    dr = st * cur
                    acc = skip * cur
                    new = []
                    for s in range(states):
                        ls = pl.ds(s * LANE, LANE)
                        hn = jnp.exp2(st * na[s]) * hs[s] + bx[rows, ls] * dr
                        acc = acc + cx[rows, ls] * hn
                        new.append(hn)
                    yv[rows, cs] = acc
                    return tuple(new)

                if u == 0:
                    init = tuple(jnp.zeros((SUB, LANE), F32) for _ in range(states))
                else:
                    init = tuple(hst[s, :, cs] for s in range(states))
                hs = lax.fori_loop(u * steps // 2, (u + 1) * steps // 2, scan_step, init, unroll=2)
                if u == 0:
                    for s in range(states):
                        hst[s, :, cs] = hs[s]
                    continue
                sub = lax.broadcasted_iota(jnp.int32, (SUB, LANE), 0)
                ct = cum[pl.ds((steps - 1) * SUB, SUB), cs]
                for s in range(states):
                    e = hs[s]
                    p = jnp.exp2(ct * na[s])
                    for d in (1, 2, 4):
                        ok = sub >= d
                        e = e + jnp.where(ok, p * pltpu.roll(e, d, 0), 0.0)
                        p = p * jnp.where(ok, pltpu.roll(p, d, 0), 1.0)
                    esend_f[s : s + 1, cs] = e[SUB - 1 : SUB, :]
                    ein[s, :, cs] = jnp.where(sub >= 1, pltpu.roll(e, 1, 0), 0.0)
                    pin[s, :, cs] = jnp.where(sub >= 1, pltpu.roll(p, 1, 0), 1.0)

        ag_wait(0, 6, 7, 10, 11, 14, 15, 18, 19)
        mm(0, True, near + away)
        proj[:half, :] = proj[:half, :] * fac[:half]
        scan(0)
        mm(1, True, near)
        ag_wait(1, 6, 7, 10, 11, 14, 15, 18, 19)
        mm(1, False, away)
        proj[half:, :] = proj[half:, :] * fac[half:]
        scan(1)

        esend[l] = esend_f[...].astype(BF16)
        for q in range(1, n_seq):
            @pl.when(q > seqi)
            def _():
                e_copy(l, q, True).start()

        for u in range(2):
            for k in AG_KEYS:
                for h in range(2):
                    ag_send(u, h, k).wait_send()
        for d in range(1, n_tp):
            ar1(d, True).wait_send()
            ar2(d, True).wait_send()

        rates = a_ref[l] * (-LOG2E)
        for q in range(n_seq - 1):
            @pl.when(q < seqi)
            def _():
                t_copy(l, q, False).wait_recv()
                hdec[q] = jnp.exp2(rates * trecv[l, q, 0:1, :])

        hdev[...] = jnp.zeros_like(hdev)
        for q in range(n_seq - 1):
            @pl.when(q < seqi)
            def _():
                e_copy(l, q, False).wait_recv()
                hdev[...] = hdec[q] * hdev[...] + erecv[l, q].astype(F32)

        def finish(u, c0, c1):
            rs = pl.ds(u * half, half)
            for cb in range(c0, c1):
                cs = pl.ds(cb * LANE, LANE)
                na = [
                    jnp.broadcast_to(a_ref[l, s : s + 1, cs] * (-LOG2E), (SUB, LANE))
                    for s in range(states)
                ]
                hin = [ein[s, :, cs] + pin[s, :, cs] * hdev[s : s + 1, cs] for s in range(states)]
                th = th_row[:, cb * LANE : (cb + 1) * LANE]

                def fold(t, unused):
                    rows = pl.ds(pl.multiple_of(t * SUB, SUB), SUB)
                    ct = cum[rows, cs]
                    acc = yv[rows, cs]
                    for s in range(states):
                        ls = pl.ds(s * LANE, LANE)
                        acc = acc + cx[rows, ls] * (jnp.exp2(ct * na[s]) * hin[s])
                    yv[rows, cs] = acc
                    return unused

                lax.fori_loop(u * steps // 2, (u + 1) * steps // 2, fold, 0, unroll=4)

                mixed = yv[rs, cs]
                fct = lax.rsqrt(jnp.mean(mixed * mixed, axis=1, keepdims=True) + 1e-05)
                normal = mixed * fct
                shrunk = jnp.maximum(normal - th, 0.0) - jnp.maximum(-normal - th, 0.0)
                gate = proj[rs, pl.ds(chans + cb * LANE, LANE)]
                gated[rs, cs] = (shrunk * (gate / (1.0 + jnp.exp(-gate)))).astype(BF16)

        finish(0, 0, ncb)
        out_c.wait()
        rs1(l, 0)
        finish(1, 0, ncb // 2)
        rs2(0)
        finish(1, ncb // 2, ncb)
        rs1(l, 1)

        @pl.when(l + 1 < layers)
        def _():
            later_copies[2].wait()
            regroup(0, nreg // 4)

        rs2(1)
        rs3(0)

        @pl.when(l + 1 < layers)
        def _():
            regroup(nreg // 4, nreg // 2)

        rs4(0)

        @pl.when(l + 1 < layers)
        def _():
            publish(l + 1, 0)
            regroup(nreg // 2, nreg)

        rs3(1)
        rs4(1)
        for u in range(2):
            for h in range(2):
                for k in range(11):
                    rs_copy(u, h, k).wait_send()
        for q in range(1, n_seq):
            @pl.when(q > seqi)
            def _():
                t_copy(l, q, True).wait_send()
                e_copy(l, q, True).wait_send()
        return unused

    lax.fori_loop(0, layers, layer, 0)
    out_ref[...] = lax.dot_general(
        perm, hid[...], (((0,), (0,)), ((), ())), preferred_element_type=F32
    ).astype(BF16)


def per_device(n_seq, tokens, norm_gain, w_in, w_low, w_dt, a_rate, dt_bias, skip_gain, threshold, w_out):
    toks, feat = tokens.shape
    layers, model, _, chans = w_in.shape
    states = a_rate.shape[1]
    rank = w_dt.shape[1]
    n_tp = SIDE * SIDE
    half, quart, eighth = toks // 2, toks // 4, toks // 8
    per_d = 2 * chans // LANE
    sel_w = rank + LANE
    dims = (layers, n_seq, toks, feat, chans, states, rank)
    vm = pl.BlockSpec(memory_space=pltpu.VMEM)
    hb = pl.BlockSpec(memory_space=pl.ANY)
    dma = pltpu.SemaphoreType.DMA
    V = pltpu.VMEM
    return pl.pallas_call(
        functools.partial(kernel_body, dims),
        out_shape=jax.ShapeDtypeStruct((toks, feat), BF16),
        in_specs=[vm, vm, hb, hb, hb, vm, vm, vm, vm, hb],
        out_specs=vm,
        scratch_shapes=[
            V((model * per_d, LANE), BF16),
            V((2 * LANE, 2 * LANE), BF16),
            V((model, 2 * chans), BF16),
            V((layers, sel_w, feat), BF16),
            V((layers, rank, chans), BF16),
            V((layers, chans, model), BF16),
            V((toks, feat), BF16),
            V((n_tp, toks, feat), BF16),
            V((toks, LANE), F32),
            V((toks, sel_w), BF16),
            V((n_tp, toks // n_tp, sel_w), BF16),
            V((toks, sel_w), BF16),
            V((LANE, states * LANE), BF16),
            V((LANE, states * LANE), BF16),
            V((toks, states * LANE), F32),
            V((toks, states * LANE), F32),
            V((toks, chans), F32),
            V((toks, chans), F32),
            V((toks, 2 * chans), F32),
            V((toks, chans), F32),
            V((states, SUB, chans), F32),
            V((states, SUB, chans), F32),
            V((states, SUB, chans), F32),
            V((states, chans), F32),
            V((n_seq, states, chans), F32),
            V((states, chans), F32),
            V((layers, states, chans), BF16),
            V((layers, n_seq, states, chans), BF16),
            V((layers, SUB, chans), F32),
            V((layers, n_seq, SUB, chans), F32),
            V((toks, chans), BF16),
            V((2, 2, SIDE, SIDE, quart, feat), BF16),
            V((2, 2, 2, SIDE, eighth, feat), BF16),
            V((2, 2, 2, SIDE, quart, feat), BF16),
            V((2, 2, SIDE, quart, feat), BF16),
            V((2, 2, 3, quart, feat), BF16),
            dma((layers, 4)),
            dma((2, 2, 20)),
            dma((2, 2, 20)),
            dma((n_tp,)),
            dma((n_tp,)),
            dma((n_tp,)),
            dma((n_tp,)),
            dma((layers, n_seq)),
            dma((layers, n_seq)),
            dma((layers, n_seq)),
            dma((layers, n_seq)),
            dma((2, 2, 11)),
            dma((2, 2, 11)),
        ],
        compiler_params=pltpu.CompilerParams(
            collective_id=0, has_side_effects=True, vmem_limit_bytes=60 * 1024 * 1024
        ),
    )(
        tokens,
        norm_gain,
        jnp.swapaxes(w_in.reshape(layers, model, 2, chans // LANE, LANE), 2, 3).reshape(
            layers, model * per_d, LANE
        ),
        jnp.swapaxes(w_low, 1, 2),
        w_dt,
        a_rate,
        dt_bias,
        skip_gain,
        threshold,
        w_out,
    )


def solution(mesh):
    in_specs = (
        P("seq", "tp"),
        P(),
        P(None, None, None, "tp"),
        P(None, "tp", None),
        P(None, None, "tp"),
        P(None, None, "tp"),
        P(None, "tp"),
        P(None, "tp"),
        P(None, "tp"),
        P(None, "tp", None),
    )
    return jax.shard_map(
        functools.partial(per_device, mesh.shape["seq"]),
        mesh=mesh,
        in_specs=in_specs,
        out_specs=P("seq", "tp"),
        check_vma=False,
    )
```

```python
import functools
import math

import jax
import jax.numpy as jnp
from jax import lax
from jax.experimental import pallas as pl
from jax.experimental.pallas import tpu as pltpu
from jax.sharding import PartitionSpec as P

MESH = pl.DeviceIdType.MESH
F32 = jnp.float32
BF16 = jnp.bfloat16
SUB = 8
LANE = 128
SIDE = 4
LOG2E = math.log2(math.e)
OFFS = (0, -1, 1, 2)
OUT = (2, 1, -1, 0)
WIDE = 8
AG_KEYS = (0, 1, 2) + tuple(range(4, 20))


def kernel_body(
    dims,
    tok_ref,
    gain_ref,
    w_in_hbm,
    w_low_hbm,
    w_dt_hbm,
    a_ref,
    bias_ref,
    skip_ref,
    thresh_ref,
    w_out_hbm,
    out_ref,
    raw,
    seld,
    w_in_v,
    w_low_v,
    w_dt_v,
    w_out_v,
    hid,
    agbuf,
    sqv,
    facv,
    selp,
    arrecv,
    arres,
    expand_b,
    expand_c,
    bx,
    cx,
    step,
    cum,
    proj,
    yv,
    pin,
    ein,
    hdev,
    hrun,
    esend_f,
    esend,
    erecv,
    tsend,
    trecv,
    spread,
    obuf,
    orecv,
    gated,
    pbuf,
    x1,
    x2,
    s2,
    x3,
    wsem,
    ag_s,
    ag_r,
    ar1_s,
    ar1_r,
    ar2_s,
    ar2_r,
    t_s,
    t_r,
    e_s,
    e_r,
    d_s,
    d_r,
    o_s,
    o_r,
    rs_s,
    rs_r,
):
    layers, n_seq, toks, feat, chans, states, rank = dims
    n_tp = SIDE * SIDE
    half = toks // 2
    quart = toks // 4
    eighth = toks // 8
    per_d = 2 * chans // LANE
    steps = toks // SUB
    arow = toks // n_tp
    ncb = chans // LANE
    seqi = lax.axis_index("seq")
    tpi = lax.axis_index("tp")
    zc = tpi // SIDE
    yc = lax.rem(tpi, SIDE)

    def wrap(v):
        return lax.rem(v + 2 * SIDE, SIDE)

    pos = ((yc, zc), (zc, yc))

    def blk(h, c1, c2):
        return c2 * SIDE + c1 if h == 0 else c1 * SIDE + c2

    def nb(h, axis, d):
        p1, p2 = pos[h]
        if axis == 1:
            return {"tp": blk(h, wrap(p1 + d), p2)}
        return {"tp": blk(h, p1, wrap(p2 + d))}

    def rcopy(src, dst, ssem, rsem, dev):
        return pltpu.make_async_remote_copy(
            src_ref=src, dst_ref=dst, send_sem=ssem, recv_sem=rsem,
            device_id=dev, device_id_type=MESH,
        )

    def wcopies(l):
        return (
            pltpu.make_async_copy(w_low_hbm.at[l], w_low_v.at[l, : rank + 2 * states], wsem.at[l, 0]),
            pltpu.make_async_copy(w_dt_hbm.at[l], w_dt_v.at[l], wsem.at[l, 1]),
            pltpu.make_async_copy(w_in_hbm.at[l], raw, wsem.at[l, 2]),
            pltpu.make_async_copy(w_out_hbm.at[l], w_out_v.at[l], wsem.at[l, 3]),
        )

    first_copies = wcopies(0)
    later_copies = wcopies(1)
    for c in (first_copies[0], first_copies[2]):
        c.start()

    barrier = pltpu.get_barrier_semaphore()
    for d in range(1, n_tp):
        pl.semaphore_signal(barrier, inc=1, device_id={"tp": lax.rem(tpi + d, n_tp)}, device_id_type=MESH)
    for d in range(1, n_seq):
        pl.semaphore_signal(barrier, inc=1, device_id={"seq": lax.rem(seqi + d, n_seq)}, device_id_type=MESH)
    pl.semaphore_wait(barrier, n_tp + n_seq - 2)

    hn = n_seq // 2
    seq_half, seq_rest = seqi // hn, lax.rem(seqi, hn)

    def spread_copy(b, q):
        return rcopy(
            tok_ref.at[pl.ds(b * half, half)], spread.at[seq_half], d_s.at[b], d_r.at[seq_half], {"seq": q}
        )

    def spread_wait(u):
        src = u * hn + seqi // 2

        @pl.when(src != seqi)
        def _():
            rcopy(
                tok_ref.at[pl.ds(0, half)], spread.at[u], d_s.at[0], d_r.at[u], {"seq": src}
            ).wait_recv()

    for b in range(2):
        q = 2 * seq_rest + b

        @pl.when(q != seqi)
        def _():
            spread_copy(b, q).start()

        @pl.when(q == seqi)
        def _():
            spread[seq_half] = tok_ref[b * half : (b + 1) * half, :]

    hsteps = steps // 2
    ri = lax.broadcasted_iota(jnp.int32, (half, half), 0)
    ci = lax.broadcasted_iota(jnp.int32, (half, half), 1)
    perm = jnp.where(ci == lax.rem(ri, SUB) * hsteps + ri // SUB, 1.0, 0.0).astype(BF16)

    def ag_info(u, h, k):
        p1, p2 = pos[h]
        r0 = u * half + h * quart
        full = pl.ds(r0, quart)
        lo = pl.ds(r0, eighth)
        hi = pl.ds(r0 + eighth, eighth)
        if k < 4:
            to = (1, -1, 2)[k]
            src_d, dst_d, rows, ax = 0, -to, full, 1

            def at(d):
                return blk(h, wrap(p1 + d), p2)
        else:
            src_d, dst_d, rows, to = (
                (0, -1, full, 1),
                (0, 1, full, -1),
                (-1, -2, lo, 1),
                (1, 2, hi, -1),
            )[(k - 4) % 4]
            o = OFFS[(k - 4) // 4]
            ax = 2

            def at(d):
                return blk(h, wrap(p1 + o), wrap(p2 + d))

        return at(src_d), at(dst_d), rows, nb(h, ax, to)

    def ag_send(u, h, k):
        src, _, rows, dev = ag_info(u, h, k)
        ref = agbuf.at[src, rows]
        return rcopy(ref, ref, ag_s.at[u, h, k], ag_r.at[u, h, k], dev)

    def ag_start(u, *ks):
        for k in ks:
            for h in range(2):
                ag_send(u, h, k).start()

    def ag_wait(u, *ks):
        for k in ks:
            for h in range(2):
                _, dst, rows, dev = ag_info(u, h, k)
                ref = agbuf.at[dst, rows]
                rcopy(ref, ref, ag_s.at[u, h, k], ag_r.at[u, h, k], dev).wait_recv()

    def publish(l, u):
        rows = pl.ds(u * half, half)
        own = hid[rows, :].astype(F32)
        gain_row = gain_ref[pl.ds(l, 1), pl.ds(pl.multiple_of(tpi * feat, feat), feat)]
        agbuf[tpi, rows] = (own * gain_row).astype(BF16)
        sqv[rows, :] = jnp.broadcast_to(jnp.sum(own * own, axis=1, keepdims=True), (half, LANE))
        ag_start(u, 0, 1, 4, 5, 2)


    ei = lax.broadcasted_iota(jnp.int32, (LANE, states * LANE), 0)
    ej = lax.broadcasted_iota(jnp.int32, (LANE, states * LANE), 1) // LANE
    expand_b[...] = jnp.where(ei == ej, 1.0, 0.0).astype(BF16)
    expand_c[...] = jnp.where(ei == ej + states, 1.0, 0.0).astype(BF16)
    grp = 2 * LANE // per_d
    gi = lax.broadcasted_iota(jnp.int32, (2 * LANE, 2 * LANE), 0)
    gj = lax.broadcasted_iota(jnp.int32, (2 * LANE, 2 * LANE), 1)
    seld[...] = jnp.where(gj == lax.rem(gi, grp) * per_d + gi // grp, 1.0, 0.0).astype(BF16)
    sel_w = rank + LANE
    pad_from = rank + 2 * states
    for l in range(layers):
        w_low_v[l, pad_from:, :] = jnp.zeros((sel_w - pad_from, feat), BF16)

    def regroup(b0, b1):
        def one(i, unused):
            r = pl.multiple_of(i * WIDE * 2 * LANE, WIDE * 2 * LANE)
            parts = [raw[pl.ds(r + v * 2 * LANE, 2 * LANE), :] for v in range(WIDE)]
            got = jnp.dot(
                seld[...], jnp.concatenate(parts, axis=1), preferred_element_type=F32
            ).astype(BF16)
            d0 = pl.multiple_of(i * WIDE * grp, WIDE * grp)
            for q in range(per_d):
                cols = pl.ds((q % 2) * chans + (q // 2) * LANE, LANE)
                for v in range(WIDE):
                    w_in_v[pl.ds(d0 + v * grp, grp), cols] = got[
                        q * grp : (q + 1) * grp, v * LANE : (v + 1) * LANE
                    ]
            return unused

        lax.fori_loop(b0, b1, one, 0)

    nreg = n_tp * feat // (WIDE * grp)

    def seq_copy(l, u, src, dst, ss, rs, q, sending):
        slot = seqi if sending else q
        return rcopy(
            src.at[l, u], dst.at[l, u, slot], ss.at[l, u, q], rs.at[l, u, slot], {"seq": q}
        )

    def t_copy(l, u, q, sending):
        return seq_copy(l, u, tsend, trecv, t_s, t_r, q, sending)

    def e_copy(l, u, q, sending):
        return seq_copy(l, u, esend, erecv, e_s, e_r, q, sending)

    def to_peers(u, act):
        for q in range(n_seq):
            @pl.when((q != seqi) if u == 0 else (q > seqi))
            def _():
                act(q)

    lo = pl.ds(0, eighth)
    hi = pl.ds(eighth, eighth)

    def rpos(h):
        p2, p1 = pos[h]
        return p1, p2

    def rnb(h, axis, d):
        return nb(h, 3 - axis, d)

    ahead, up, down, here = range(SIDE)
    parts = (pl.ds(0, 2), pl.ds(2, 2))

    def rs_copy(u, h, k):
        if k < 8:
            piece = parts[(k // 2) % 2]
            way = k % 2
            if k < 4:
                src = pbuf.at[u, h, ahead, piece, (lo, hi)[way]]
                dst = x1.at[u, h, way, piece]
            else:
                src = pbuf.at[u, h, (up, down)[way], piece]
                dst = x2.at[u, h, way, piece]
            dev = rnb(h, 1, (1, -1)[way])
        else:
            src = s2.at[u, h, (ahead, up, down)[k - 8]]
            dst = x3.at[u, h, k - 8]
            dev = rnb(h, 2, OUT[k - 8])
        return rcopy(src, dst, rs_s.at[u, h, k], rs_r.at[u, h, k], dev)

    def omm(l, u, pairs):
        lhs = gated[u * half : (u + 1) * half, :]
        for dz, dy in pairs:
            z, y = wrap(zc + dz), wrap(yc + dy)
            cols = pl.ds(pl.multiple_of((z * SIDE + y) * feat, feat), feat)
            val = jnp.dot(lhs, w_out_v[l, :, cols], preferred_element_type=F32).astype(BF16)
            iz, iy = OUT.index(dz), OUT.index(dy)
            pbuf[u, 0, iz, iy] = val[:quart]
            pbuf[u, 1, iy, iz] = val[quart:]

    def rs1(l, u):
        omm(l, u, ((2, 2), (2, 1), (1, 2)))
        for h in range(2):
            rs_copy(u, h, 0).start()
            rs_copy(u, h, 1).start()
        omm(l, u, ((2, -1), (2, 0), (-1, 2), (0, 2)))
        for h in range(2):
            rs_copy(u, h, 2).start()
            rs_copy(u, h, 3).start()
        omm(l, u, ((1, 1), (1, -1), (1, 0), (-1, 1), (-1, -1), (-1, 0), (0, 1), (0, -1)))
        omm(l, u, ((0, 0),))

    def rs2(u):
        for p in range(2):
            piece = parts[p]
            for h in range(2):
                for way in range(2):
                    rows = (lo, hi)[way]
                    side = (up, down)[way]
                    rs_copy(u, h, 2 * p + way).wait_recv()
                    pbuf[u, h, side, piece, rows] = (
                        pbuf[u, h, side, piece, rows].astype(F32) + x1[u, h, way, piece].astype(F32)
                    ).astype(BF16)
                    rs_copy(u, h, 4 + 2 * p + way).start()

    def sum3(u, h, c2):
        return (
            pbuf[u, h, here, c2].astype(F32) + x2[u, h, 0, c2].astype(F32) + x2[u, h, 1, c2].astype(F32)
        )

    def rs3(u):
        for p in range(2):
            for h in range(2):
                rs_copy(u, h, 4 + 2 * p).wait_recv()
                rs_copy(u, h, 5 + 2 * p).wait_recv()
                for c2 in (ahead, up) if p == 0 else (down,):
                    s2[u, h, c2] = sum3(u, h, c2).astype(BF16)
                    rs_copy(u, h, 8 + c2).start()

    def rs4(u):
        for h in range(2):
            total = sum3(u, h, here)
            for k in range(3):
                rs_copy(u, h, 8 + k).wait_recv()
                total = total + x3[u, h, k].astype(F32)
            rows = pl.ds(u * half + h * quart, quart)
            hid[rows, :] = (hid[rows, :].astype(F32) + total).astype(BF16)

    hred = n_tp // 2

    def sel_copy(u, d, sending):
        to = u * hred + lax.rem(tpi + d, hred)
        rows = pl.ds(pl.multiple_of(u * half + lax.rem(tpi + d, hred) * arow, arow), arow)
        return rcopy(selp.at[rows], arrecv.at[tpi], ar1_s.at[u, d], ar1_r.at[tpi], {"tp": to})

    def each_reducer(u, act):
        for d in range(hred):
            if d == 0:
                @pl.when(tpi // hred != u)
                def _():
                    act(0)
            else:
                act(d)

    def sel(l, u):
        rs = pl.ds(u * half, half)
        selv = lax.dot_general(
            agbuf[tpi, rs], w_low_v[l], (((1,), (1,)), ((), ())), preferred_element_type=F32
        )
        sq = sqv[rs, 0:1]
        sq_hi = sq.astype(BF16).astype(F32)
        lane = lax.broadcasted_iota(jnp.int32, (half, sel_w), 1)
        selv = jnp.where(lane == pad_from, sq_hi, selv)
        selv = jnp.where(lane == pad_from + 1, sq - sq_hi, selv)
        selp[rs, :] = selv.astype(BF16)
        each_reducer(u, lambda d: sel_copy(u, d, True).start())

        @pl.when(tpi // hred == u)
        def _():
            own = pl.ds(pl.multiple_of(u * half + lax.rem(tpi, hred) * arow, arow), arow)
            arrecv[tpi] = selp[own, :]

    def res_copy(u, d):
        rows = pl.ds(pl.multiple_of(u * half + lax.rem(tpi, hred) * arow, arow), arow)
        return rcopy(
            arres.at[rows], arres.at[rows], ar2_s.at[d], ar2_r.at[u, lax.rem(tpi, hred)],
            {"tp": lax.rem(tpi + d, n_tp)},
        )

    def res_wait(u, d):
        i = lax.rem(tpi + d, hred)
        rows = pl.ds(pl.multiple_of(u * half + i * arow, arow), arow)
        rcopy(
            arres.at[rows], arres.at[rows], ar2_s.at[0], ar2_r.at[u, i], {"tp": u * hred + i}
        ).wait_recv()

    def red(u):
        @pl.when(tpi // hred == u)
        def _():
            for d in range(1, n_tp):
                fr = lax.rem(tpi + n_tp - d, n_tp)
                rcopy(
                    selp.at[pl.ds(0, arow)], arrecv.at[fr], ar1_s.at[u, 0], ar1_r.at[fr], {"tp": fr}
                ).wait_recv()
            tot = jnp.zeros((arow, sel_w), F32)
            for i in range(n_tp):
                tot = tot + arrecv[i].astype(F32)
            lane = lax.broadcasted_iota(jnp.int32, (arow, sel_w), 1)
            is_sq = (lane == pad_from) | (lane == pad_from + 1)
            ssum = jnp.sum(jnp.where(is_sq, tot, 0.0), axis=1, keepdims=True)
            factor = lax.rsqrt(ssum / (n_tp * feat) + 1e-05)
            f_hi = factor.astype(BF16).astype(F32)
            tot = jnp.where(
                lane == pad_from, f_hi, jnp.where(lane == pad_from + 1, factor - f_hi, tot * factor)
            )
            mine = pl.ds(pl.multiple_of(u * half + lax.rem(tpi, hred) * arow, arow), arow)
            arres[mine, :] = tot.astype(BF16)
            for d in range(1, n_tp):
                res_copy(u, d).start()

    def dt(l, u):
        rs = pl.ds(u * half, half)
        each_reducer(u, lambda d: res_wait(u, d))
        tail = arres[rs, rank:]
        tl = lax.broadcasted_iota(jnp.int32, (half, LANE), 1)
        in_f = (tl == 2 * states) | (tl == 2 * states + 1)
        fac = jnp.sum(jnp.where(in_f, tail.astype(F32), 0.0), axis=1, keepdims=True)
        facv[rs, :] = jnp.broadcast_to(fac, (half, LANE))
        pre = jnp.dot(arres[rs, :rank], w_dt_v[l], preferred_element_type=F32) + bias_ref[pl.ds(l, 1), :]
        step[rs, :] = jnp.maximum(pre, 0.0) + jnp.log1p(jnp.exp(-jnp.abs(pre)))
        bx[rs, :] = jnp.dot(tail, expand_b[...], preferred_element_type=F32)
        cx[rs, :] = jnp.dot(tail, expand_c[...], preferred_element_type=F32)

        def accum(t, run):
            rows = pl.ds(pl.multiple_of(t * SUB, SUB), SUB)
            run = run + step[rows, :]
            cum[rows, :] = run
            return run

        ctot = lax.fori_loop(u * hsteps, (u + 1) * hsteps, accum, jnp.zeros((SUB, chans), F32))
        both = jnp.broadcast_to(jnp.sum(ctot, axis=0, keepdims=True), (SUB, chans))
        tsend[l, u] = both
        trecv[l, u, seqi] = both
        to_peers(u, lambda q: t_copy(l, u, q, True).start())

    def ag_g2(u):
        ag_wait(u, 0, 1)
        ag_start(u, 8, 9, 12, 13)
        ag_wait(u, 4, 5)
        ag_start(u, 6, 7)
        ag_wait(u, 2)
        ag_start(u, 16, 17)

    def ag_g3(u):
        ag_wait(u, 8, 9)
        ag_start(u, 10, 11)
        ag_wait(u, 12, 13)
        ag_start(u, 14, 15)
        ag_wait(u, 16, 17)
        ag_start(u, 18, 19)

    near = ((0, 0), (0, 1), (0, -1), (1, 0), (-1, 0), (1, 1), (1, -1), (-1, 1), (-1, -1))
    away = ((2, 0), (2, 1), (2, 2), (2, 3), (0, 2), (1, 2), (3, 2))

    def mm(u, first, pairs):
        rs = pl.ds(u * half, half)
        for i, (dz, dy) in enumerate(pairs):
            b = wrap(zc + dz) * SIDE + wrap(yc + dy)
            rows = pl.ds(pl.multiple_of(b * feat, feat), feat)
            val = jnp.dot(agbuf[b, rs], w_in_v[rows, :], preferred_element_type=F32)
            if first and i == 0:
                proj[rs, :] = val
            else:
                proj[rs, :] += val

    def project(u):
        mm(u, True, near)
        ag_wait(u, 6, 7, 10, 11, 14, 15, 18, 19)
        mm(u, False, away)
        rs = pl.ds(u * half, half)
        proj[rs, :] = proj[rs, :] * facv[rs, 0:1]

    def decay_rows(l, cs):
        return [
            jnp.broadcast_to(a_ref[l, s : s + 1, cs] * (-LOG2E), (SUB, LANE)) for s in range(states)
        ]

    def scan(l, u):
        skip_row = skip_ref[pl.ds(l, 1), :]
        for cb in range(ncb):
            cs = pl.ds(cb * LANE, LANE)
            na = decay_rows(l, cs)
            skip = skip_row[:, cb * LANE : (cb + 1) * LANE]

            def scan_step(t, hs):
                rows = pl.ds(pl.multiple_of(t * SUB, SUB), SUB)
                st = step[rows, cs]
                cur = proj[rows, cs]
                dr = st * cur
                acc = skip * cur
                new = []
                for s in range(states):
                    ls = pl.ds(s * LANE, LANE)
                    hn = jnp.exp2(st * na[s]) * hs[s] + bx[rows, ls] * dr
                    acc = acc + cx[rows, ls] * hn
                    new.append(hn)
                yv[rows, cs] = acc
                return tuple(new)

            init = tuple(jnp.zeros((SUB, LANE), F32) for _ in range(states))
            hs = lax.fori_loop(u * hsteps, (u + 1) * hsteps, scan_step, init, unroll=2)
            sub = lax.broadcasted_iota(jnp.int32, (SUB, LANE), 0)
            ct = cum[pl.ds(((u + 1) * hsteps - 1) * SUB, SUB), cs]
            for s in range(states):
                e = hs[s]
                p = jnp.exp2(ct * na[s])
                for d in (1, 2, 4):
                    ok = sub >= d
                    e = e + jnp.where(ok, p * pltpu.roll(e, d, 0), 0.0)
                    p = p * jnp.where(ok, pltpu.roll(p, d, 0), 1.0)
                esend_f[s : s + 1, cs] = e[SUB - 1 : SUB, :]
                ein[s, :, cs] = jnp.where(sub >= 1, pltpu.roll(e, 1, 0), 0.0)
                pin[s, :, cs] = jnp.where(sub >= 1, pltpu.roll(p, 1, 0), 1.0)
        ends = esend_f[...].astype(BF16)
        esend[l, u] = ends
        erecv[l, u, seqi] = ends
        to_peers(u, lambda q: e_copy(l, u, q, True).start())

    def absorb(l, u, q):
        dec = jnp.exp2(a_ref[l] * (-LOG2E) * trecv[l, u, q, 0:1, :])
        hrun[...] = dec * hrun[...] + erecv[l, u, q].astype(F32)

    def arrive(l, u, q):
        t_copy(l, u, q, False).wait_recv()
        e_copy(l, u, q, False).wait_recv()

    def carry(l, u):
        if u == 0:
            hrun[...] = jnp.zeros_like(hrun)
        else:
            for q in range(n_seq):
                @pl.when(q > seqi)
                def _():
                    arrive(l, 0, q)

                @pl.when(q >= seqi)
                def _():
                    absorb(l, 0, q)
        for q in range(n_seq - 1):
            @pl.when(q < seqi)
            def _():
                arrive(l, u, q)
                absorb(l, u, q)
        hdev[...] = hrun[...]

    def finish(l, u, c0, c1):
        rs = pl.ds(u * half, half)
        th_row = thresh_ref[pl.ds(l, 1), :]
        for cb in range(c0, c1):
            cs = pl.ds(cb * LANE, LANE)
            na = decay_rows(l, cs)
            hin = [ein[s, :, cs] + pin[s, :, cs] * hdev[s : s + 1, cs] for s in range(states)]
            th = th_row[:, cb * LANE : (cb + 1) * LANE]

            def fold(t, unused):
                rows = pl.ds(pl.multiple_of(t * SUB, SUB), SUB)
                ct = cum[rows, cs]
                acc = yv[rows, cs]
                for s in range(states):
                    ls = pl.ds(s * LANE, LANE)
                    acc = acc + cx[rows, ls] * (jnp.exp2(ct * na[s]) * hin[s])
                yv[rows, cs] = acc
                return unused

            lax.fori_loop(u * hsteps, (u + 1) * hsteps, fold, 0, unroll=4)

            mixed = yv[rs, cs]
            fct = lax.rsqrt(jnp.mean(mixed * mixed, axis=1, keepdims=True) + 1e-05)
            normal = mixed * fct
            shrunk = jnp.maximum(normal - th, 0.0) - jnp.maximum(-normal - th, 0.0)
            gate = proj[rs, pl.ds(chans + cb * LANE, LANE)]
            gated[rs, cs] = (shrunk * (gate / (1.0 + jnp.exp(-gate)))).astype(BF16)

    def gather_sent(u):
        for h in range(2):
            for k in AG_KEYS:
                ag_send(u, h, k).wait_send()

    def sent(u):
        for h in range(2):
            for k in range(11):
                rs_copy(u, h, k).wait_send()
        each_reducer(u, lambda d: sel_copy(u, d, True).wait_send())

        @pl.when(tpi // hred == u)
        def _():
            for d in range(1, n_tp):
                res_copy(u, d).wait_send()

    low_c, in_c, dt_c, out_c = first_copies[0], first_copies[2], first_copies[1], first_copies[3]
    for u in range(2):
        spread_wait(u)
        rs = pl.ds(u * half, half)
        hid[rs, :] = jnp.dot(perm, spread[u], preferred_element_type=F32).astype(BF16)
        publish(0, u)
        if u == 0:
            low_c.wait()
        sel(0, u)
    ag_g2(0)
    in_c.wait()
    for c in (dt_c, out_c, later_copies[0], later_copies[1], later_copies[3]):
        c.start()
    regroup(0, nreg // 2)
    ag_g3(0)
    red(0)
    regroup(nreg // 2, nreg)
    later_copies[2].start()
    dt_c.wait()
    dt(0, 0)

    def layer(l, unused):
        more = l + 1 < layers
        project(0)
        ag_g2(1)
        scan(l, 0)
        red(1)
        carry(l, 0)
        ag_g3(1)
        finish(l, 0, 0, ncb)

        @pl.when(l == 0)
        def _():
            out_c.wait()

        gather_sent(0)
        rs1(l, 0)
        dt(l, 1)
        rs2(0)
        project(1)
        scan(l, 1)
        rs3(0)
        carry(l, 1)
        finish(l, 1, 0, ncb // 2)
        rs4(0)
        sent(0)

        @pl.when(more)
        def _():
            for i in (0, 1, 3):
                later_copies[i].wait()
            publish(l + 1, 0)
            sel(l + 1, 0)

        finish(l, 1, ncb // 2, ncb)
        gather_sent(1)
        rs1(l, 1)

        @pl.when(more)
        def _():
            later_copies[2].wait()
            regroup(0, nreg // 2)
            ag_g2(0)

        rs2(1)

        @pl.when(more)
        def _():
            regroup(nreg // 2, nreg)
            red(0)
            ag_g3(0)

        rs3(1)

        @pl.when(more)
        def _():
            dt(l + 1, 0)

        rs4(1)
        sent(1)

        @pl.when(more)
        def _():
            publish(l + 1, 1)
            sel(l + 1, 1)

        for u in range(2):
            to_peers(u, lambda q: t_copy(l, u, q, True).wait_send())
            to_peers(u, lambda q: e_copy(l, u, q, True).wait_send())
        return unused

    lax.fori_loop(0, layers, layer, 0)

    for b in range(2):
        q = 2 * seq_rest + b

        @pl.when(q != seqi)
        def _():
            spread_copy(b, q).wait_send()

    odd = lax.rem(seqi, 2)
    for u in range(2):
        obuf[u] = lax.dot_general(
            perm, hid[u * half : (u + 1) * half, :], (((0,), (0,)), ((), ())), preferred_element_type=F32
        ).astype(BF16)
        dst = u * hn + seqi // 2

        @pl.when(dst != seqi)
        def _():
            rcopy(obuf.at[u], orecv.at[odd], o_s.at[u], o_r.at[odd], {"seq": dst}).start()

        @pl.when(dst == seqi)
        def _():
            orecv[odd] = obuf[u]

    for b in range(2):
        src = 2 * seq_rest + b

        @pl.when(src != seqi)
        def _():
            rcopy(obuf.at[0], orecv.at[b], o_s.at[0], o_r.at[b], {"seq": src}).wait_recv()

        out_ref[b * half : (b + 1) * half, :] = orecv[b]
    for u in range(2):
        dst = u * hn + seqi // 2

        @pl.when(dst != seqi)
        def _():
            rcopy(obuf.at[u], orecv.at[odd], o_s.at[u], o_r.at[odd], {"seq": dst}).wait_send()


def per_device(n_seq, tokens, norm_gain, w_in, w_low, w_dt, a_rate, dt_bias, skip_gain, threshold, w_out):
    toks, feat = tokens.shape
    layers, model, _, chans = w_in.shape
    states = a_rate.shape[1]
    rank = w_dt.shape[1]
    n_tp = SIDE * SIDE
    half, quart, eighth = toks // 2, toks // 4, toks // 8
    per_d = 2 * chans // LANE
    sel_w = rank + LANE
    dims = (layers, n_seq, toks, feat, chans, states, rank)
    vm = pl.BlockSpec(memory_space=pltpu.VMEM)
    hb = pl.BlockSpec(memory_space=pl.ANY)
    dma = pltpu.SemaphoreType.DMA
    V = pltpu.VMEM
    return pl.pallas_call(
        functools.partial(kernel_body, dims),
        out_shape=jax.ShapeDtypeStruct((toks, feat), BF16),
        in_specs=[vm, vm, hb, hb, hb, vm, vm, vm, vm, hb],
        out_specs=vm,
        scratch_shapes=[
            V((model * per_d, LANE), BF16),
            V((2 * LANE, 2 * LANE), BF16),
            V((model, 2 * chans), BF16),
            V((layers, sel_w, feat), BF16),
            V((layers, rank, chans), BF16),
            V((layers, chans, model), BF16),
            V((toks, feat), BF16),
            V((n_tp, toks, feat), BF16),
            V((toks, LANE), F32),
            V((toks, LANE), F32),
            V((toks, sel_w), BF16),
            V((n_tp, toks // n_tp, sel_w), BF16),
            V((toks, sel_w), BF16),
            V((LANE, states * LANE), BF16),
            V((LANE, states * LANE), BF16),
            V((toks, states * LANE), F32),
            V((toks, states * LANE), F32),
            V((toks, chans), F32),
            V((toks, chans), F32),
            V((toks, 2 * chans), F32),
            V((toks, chans), F32),
            V((states, SUB, chans), F32),
            V((states, SUB, chans), F32),
            V((states, chans), F32),
            V((states, chans), F32),
            V((states, chans), F32),
            V((layers, 2, states, chans), BF16),
            V((layers, 2, n_seq, states, chans), BF16),
            V((layers, 2, SUB, chans), F32),
            V((layers, 2, n_seq, SUB, chans), F32),
            V((2, half, feat), BF16),
            V((2, half, feat), BF16),
            V((2, half, feat), BF16),
            V((toks, chans), BF16),
            V((2, 2, SIDE, SIDE, quart, feat), BF16),
            V((2, 2, 2, SIDE, eighth, feat), BF16),
            V((2, 2, 2, SIDE, quart, feat), BF16),
            V((2, 2, SIDE, quart, feat), BF16),
            V((2, 2, 3, quart, feat), BF16),
            dma((layers, 4)),
            dma((2, 2, 20)),
            dma((2, 2, 20)),
            dma((2, n_tp // 2)),
            dma((n_tp,)),
            dma((n_tp,)),
            dma((2, n_tp // 2)),
            dma((layers, 2, n_seq)),
            dma((layers, 2, n_seq)),
            dma((layers, 2, n_seq)),
            dma((layers, 2, n_seq)),
            dma((2,)),
            dma((2,)),
            dma((2,)),
            dma((2,)),
            dma((2, 2, 11)),
            dma((2, 2, 11)),
        ],
        compiler_params=pltpu.CompilerParams(
            collective_id=0, has_side_effects=True, vmem_limit_bytes=60 * 1024 * 1024
        ),
    )(
        tokens,
        norm_gain,
        jnp.swapaxes(w_in.reshape(layers, model, 2, chans // LANE, LANE), 2, 3).reshape(
            layers, model * per_d, LANE
        ),
        jnp.swapaxes(w_low, 1, 2),
        w_dt,
        a_rate,
        dt_bias,
        skip_gain,
        threshold,
        w_out,
    )


def solution(mesh):
    in_specs = (
        P("seq", "tp"),
        P(),
        P(None, None, None, "tp"),
        P(None, "tp", None),
        P(None, None, "tp"),
        P(None, None, "tp"),
        P(None, "tp"),
        P(None, "tp"),
        P(None, "tp"),
        P(None, "tp", None),
    )
    return jax.shard_map(
        functools.partial(per_device, mesh.shape["seq"]),
        mesh=mesh,
        in_specs=in_specs,
        out_specs=P("seq", "tp"),
        check_vma=False,
    )
```

```python
import functools
import math

import jax
import jax.numpy as jnp
from jax import lax
from jax.experimental import pallas as pl
from jax.experimental.pallas import tpu as pltpu
from jax.sharding import PartitionSpec as P

MESH = pl.DeviceIdType.MESH
F32 = jnp.float32
BF16 = jnp.bfloat16
SUB = 8
LANE = 128
SIDE = 4
LOG2E = math.log2(math.e)
OFFS = (0, -1, 1, 2)
OUT = (2, 1, -1, 0)
WIDE = 8
AG_KEYS = (0, 1, 2) + tuple(range(4, 20))


def kernel_body(
    dims,
    tok_ref,
    gain_ref,
    w_in_hbm,
    w_low_hbm,
    w_dt_hbm,
    a_ref,
    bias_ref,
    skip_ref,
    thresh_ref,
    w_out_hbm,
    out_ref,
    raw,
    seld,
    w_in_v,
    w_low_v,
    w_dt_v,
    w_out_v,
    hid,
    agbuf,
    sqv,
    selp,
    arrecv,
    arres,
    expand_b,
    expand_c,
    bx,
    cx,
    step,
    cum,
    proj,
    yv,
    pin,
    ein,
    hst,
    hdev,
    hdec,
    esend_f,
    esend,
    erecv,
    tsend,
    trecv,
    gated,
    pbuf,
    x1,
    x2,
    s2,
    x3,
    wsem,
    ag_s,
    ag_r,
    ar1_s,
    ar1_r,
    ar2_s,
    ar2_r,
    t_s,
    t_r,
    e_s,
    e_r,
    rs_s,
    rs_r,
):
    layers, n_seq, toks, feat, chans, states, rank = dims
    n_tp = SIDE * SIDE
    half = toks // 2
    quart = toks // 4
    eighth = toks // 8
    per_d = 2 * chans // LANE
    steps = toks // SUB
    arow = toks // n_tp
    ncb = chans // LANE
    seqi = lax.axis_index("seq")
    tpi = lax.axis_index("tp")
    zc = tpi // SIDE
    yc = lax.rem(tpi, SIDE)

    def wrap(v):
        return lax.rem(v + 2 * SIDE, SIDE)

    pos = ((yc, zc), (zc, yc))

    def blk(h, c1, c2):
        return c2 * SIDE + c1 if h == 0 else c1 * SIDE + c2

    def nb(h, axis, d):
        p1, p2 = pos[h]
        if axis == 1:
            return {"tp": blk(h, wrap(p1 + d), p2)}
        return {"tp": blk(h, p1, wrap(p2 + d))}

    def rcopy(src, dst, ssem, rsem, dev):
        return pltpu.make_async_remote_copy(
            src_ref=src, dst_ref=dst, send_sem=ssem, recv_sem=rsem,
            device_id=dev, device_id_type=MESH,
        )

    def wcopies(l):
        return (
            pltpu.make_async_copy(w_low_hbm.at[l], w_low_v.at[l, : rank + 2 * states], wsem.at[l, 0]),
            pltpu.make_async_copy(w_dt_hbm.at[l], w_dt_v.at[l], wsem.at[l, 1]),
            pltpu.make_async_copy(w_in_hbm.at[l], raw, wsem.at[l, 2]),
            pltpu.make_async_copy(w_out_hbm.at[l], w_out_v.at[l], wsem.at[l, 3]),
        )

    first_copies = wcopies(0)
    later_copies = wcopies(1)
    for c in (first_copies[0], first_copies[2]):
        c.start()

    barrier = pltpu.get_barrier_semaphore()
    for d in range(1, n_tp):
        pl.semaphore_signal(barrier, inc=1, device_id={"tp": lax.rem(tpi + d, n_tp)}, device_id_type=MESH)
    for d in range(1, n_seq):
        pl.semaphore_signal(barrier, inc=1, device_id={"seq": lax.rem(seqi + d, n_seq)}, device_id_type=MESH)
    pl.semaphore_wait(barrier, n_tp + n_seq - 2)

    ri = lax.broadcasted_iota(jnp.int32, (toks, toks), 0)
    ci = lax.broadcasted_iota(jnp.int32, (toks, toks), 1)
    perm = jnp.where(ci == lax.rem(ri, SUB) * steps + ri // SUB, 1.0, 0.0).astype(BF16)
    hid[...] = jnp.dot(perm, tok_ref[...], preferred_element_type=F32).astype(BF16)

    def ag_info(u, h, k):
        p1, p2 = pos[h]
        r0 = u * half + h * quart
        full = pl.ds(r0, quart)
        lo = pl.ds(r0, eighth)
        hi = pl.ds(r0 + eighth, eighth)
        if k < 4:
            to = (1, -1, 2)[k]
            src_d, dst_d, rows, ax = 0, -to, full, 1

            def at(d):
                return blk(h, wrap(p1 + d), p2)
        else:
            src_d, dst_d, rows, to = (
                (0, -1, full, 1),
                (0, 1, full, -1),
                (-1, -2, lo, 1),
                (1, 2, hi, -1),
            )[(k - 4) % 4]
            o = OFFS[(k - 4) // 4]
            ax = 2

            def at(d):
                return blk(h, wrap(p1 + o), wrap(p2 + d))

        return at(src_d), at(dst_d), rows, nb(h, ax, to)

    def ag_send(u, h, k):
        src, _, rows, dev = ag_info(u, h, k)
        ref = agbuf.at[src, rows]
        return rcopy(ref, ref, ag_s.at[u, h, k], ag_r.at[u, h, k], dev)

    def ag_start(u, *ks):
        for k in ks:
            for h in range(2):
                ag_send(u, h, k).start()

    def ag_wait(u, *ks):
        for k in ks:
            for h in range(2):
                _, dst, rows, dev = ag_info(u, h, k)
                ref = agbuf.at[dst, rows]
                rcopy(ref, ref, ag_s.at[u, h, k], ag_r.at[u, h, k], dev).wait_recv()

    def publish(l, u):
        rows = pl.ds(u * half, half)
        own = hid[rows, :].astype(F32)
        gain_row = gain_ref[pl.ds(l, 1), pl.ds(pl.multiple_of(tpi * feat, feat), feat)]
        agbuf[tpi, rows] = (own * gain_row).astype(BF16)
        sqv[rows, :] = jnp.broadcast_to(jnp.sum(own * own, axis=1, keepdims=True), (half, LANE))
        ag_start(u, 0, 1, 4, 5, 2)

    publish(0, 0)

    ei = lax.broadcasted_iota(jnp.int32, (LANE, states * LANE), 0)
    ej = lax.broadcasted_iota(jnp.int32, (LANE, states * LANE), 1) // LANE
    expand_b[...] = jnp.where(ei == ej, 1.0, 0.0).astype(BF16)
    expand_c[...] = jnp.where(ei == ej + states, 1.0, 0.0).astype(BF16)
    grp = 2 * LANE // per_d
    gi = lax.broadcasted_iota(jnp.int32, (2 * LANE, 2 * LANE), 0)
    gj = lax.broadcasted_iota(jnp.int32, (2 * LANE, 2 * LANE), 1)
    seld[...] = jnp.where(gj == lax.rem(gi, grp) * per_d + gi // grp, 1.0, 0.0).astype(BF16)
    sel_w = rank + LANE
    pad_from = rank + 2 * states
    for l in range(layers):
        w_low_v[l, pad_from:, :] = jnp.zeros((sel_w - pad_from, feat), BF16)

    def regroup(l, b0, b1):
        def one(i, unused):
            r = pl.multiple_of(i * WIDE * 2 * LANE, WIDE * 2 * LANE)
            parts = [raw[pl.ds(r + v * 2 * LANE, 2 * LANE), :] for v in range(WIDE)]
            got = jnp.dot(
                seld[...], jnp.concatenate(parts, axis=1), preferred_element_type=F32
            ).astype(BF16)
            d0 = pl.multiple_of(i * WIDE * grp, WIDE * grp)
            for q in range(per_d):
                cols = pl.ds((q % 2) * chans + (q // 2) * LANE, LANE)
                for v in range(WIDE):
                    w_in_v[l, pl.ds(d0 + v * grp, grp), cols] = got[
                        q * grp : (q + 1) * grp, v * LANE : (v + 1) * LANE
                    ]
            return unused

        lax.fori_loop(b0, b1, one, 0)

    nreg = n_tp * feat // (WIDE * grp)

    def seq_copy(l, src, dst, ss, rs, q, sending):
        slot = seqi if sending else q
        return rcopy(src, dst.at[l, slot], ss.at[l, q], rs.at[l, slot], {"seq": q})

    def t_copy(l, q, sending):
        return seq_copy(l, tsend.at[l], trecv, t_s, t_r, q, sending)

    def e_copy(l, q, sending):
        return seq_copy(l, esend.at[l], erecv, e_s, e_r, q, sending)

    lo = pl.ds(0, eighth)
    hi = pl.ds(eighth, eighth)

    def rpos(h):
        p2, p1 = pos[h]
        return p1, p2

    def rnb(h, axis, d):
        return nb(h, 3 - axis, d)

    ahead, up, down, here = range(SIDE)
    parts = (pl.ds(0, 2), pl.ds(2, 2))

    def rs_copy(u, h, k):
        if k < 8:
            piece = parts[(k // 2) % 2]
            way = k % 2
            if k < 4:
                src = pbuf.at[u, h, ahead, piece, (lo, hi)[way]]
                dst = x1.at[u, h, way, piece]
            else:
                src = pbuf.at[u, h, (up, down)[way], piece]
                dst = x2.at[u, h, way, piece]
            dev = rnb(h, 1, (1, -1)[way])
        else:
            src = s2.at[u, h, (ahead, up, down)[k - 8]]
            dst = x3.at[u, h, k - 8]
            dev = rnb(h, 2, OUT[k - 8])
        return rcopy(src, dst, rs_s.at[u, h, k], rs_r.at[u, h, k], dev)

    def omm(l, u, pairs):
        lhs = gated[u * half : (u + 1) * half, :]
        for dz, dy in pairs:
            z, y = wrap(zc + dz), wrap(yc + dy)
            cols = pl.ds(pl.multiple_of((z * SIDE + y) * feat, feat), feat)
            val = jnp.dot(lhs, w_out_v[l, :, cols], preferred_element_type=F32).astype(BF16)
            iz, iy = OUT.index(dz), OUT.index(dy)
            pbuf[u, 0, iz, iy] = val[:quart]
            pbuf[u, 1, iy, iz] = val[quart:]

    def rs1(l, u):
        omm(l, u, ((2, 2), (2, 1), (1, 2)))
        for h in range(2):
            rs_copy(u, h, 0).start()
            rs_copy(u, h, 1).start()
        omm(l, u, ((2, -1), (2, 0), (-1, 2), (0, 2)))
        for h in range(2):
            rs_copy(u, h, 2).start()
            rs_copy(u, h, 3).start()
        omm(l, u, ((1, 1), (1, -1), (1, 0), (-1, 1), (-1, -1), (-1, 0), (0, 1), (0, -1)))
        omm(l, u, ((0, 0),))

    def rs2(u):
        for p in range(2):
            piece = parts[p]
            for h in range(2):
                for way in range(2):
                    rows = (lo, hi)[way]
                    side = (up, down)[way]
                    rs_copy(u, h, 2 * p + way).wait_recv()
                    pbuf[u, h, side, piece, rows] = (
                        pbuf[u, h, side, piece, rows].astype(F32) + x1[u, h, way, piece].astype(F32)
                    ).astype(BF16)
                    rs_copy(u, h, 4 + 2 * p + way).start()

    def sum3(u, h, c2):
        return (
            pbuf[u, h, here, c2].astype(F32) + x2[u, h, 0, c2].astype(F32) + x2[u, h, 1, c2].astype(F32)
        )

    def rs3(u):
        for p in range(2):
            for h in range(2):
                rs_copy(u, h, 4 + 2 * p).wait_recv()
                rs_copy(u, h, 5 + 2 * p).wait_recv()
                for c2 in (ahead, up) if p == 0 else (down,):
                    s2[u, h, c2] = sum3(u, h, c2).astype(BF16)
                    rs_copy(u, h, 8 + c2).start()

    def rs4(u):
        for h in range(2):
            total = sum3(u, h, here)
            for k in range(3):
                rs_copy(u, h, 8 + k).wait_recv()
                total = total + x3[u, h, k].astype(F32)
            rows = pl.ds(u * half + h * quart, quart)
            hid[rows, :] = (hid[rows, :].astype(F32) + total).astype(BF16)

    def layer(l, unused):
        low_c, dt_c, in_c, out_c = wcopies(l)
        publish(l, 1)

        low_c.wait()
        selv = lax.dot_general(
            agbuf[tpi], w_low_v[l], (((1,), (1,)), ((), ())), preferred_element_type=F32
        )
        sq = sqv[:, 0:1]
        sq_hi = sq.astype(BF16).astype(F32)
        lane = lax.broadcasted_iota(jnp.int32, (toks, sel_w), 1)
        selv = jnp.where(lane == pad_from, sq_hi, selv)
        selv = jnp.where(lane == pad_from + 1, sq - sq_hi, selv)
        selp[...] = selv.astype(BF16)
        arrecv[tpi] = selp[pl.ds(pl.multiple_of(tpi * arow, arow), arow), :]

        def ar1(d, sending):
            to = lax.rem(tpi + d, n_tp)
            fr = lax.rem(tpi + n_tp - d, n_tp)
            rows = pl.ds(pl.multiple_of(to * arow, arow), arow)
            dst = arrecv.at[tpi] if sending else arrecv.at[fr]
            return rcopy(selp.at[rows], dst, ar1_s.at[d], ar1_r.at[d], {"tp": to})

        for d in range(1, n_tp):
            ar1(d, True).start()

        ag_wait(0, 0, 1)
        ag_start(0, 8, 9, 12, 13)
        ag_wait(0, 4, 5)
        ag_start(0, 6, 7)
        ag_wait(0, 2)
        ag_start(0, 16, 17)

        @pl.when(l == 0)
        def _():
            in_c.wait()
            for c in (first_copies[1], first_copies[3], later_copies[0], later_copies[1], later_copies[3]):
                c.start()
            regroup(0, 0, nreg // 4)

        ag_wait(1, 0, 1)
        ag_start(1, 8, 9, 12, 13)
        ag_wait(1, 4, 5)
        ag_start(1, 6, 7)
        ag_wait(1, 2)
        ag_start(1, 16, 17)
        ag_wait(0, 8, 9)
        ag_start(0, 10, 11)
        ag_wait(0, 12, 13)
        ag_start(0, 14, 15)
        ag_wait(0, 16, 17)
        ag_start(0, 18, 19)

        for d in range(1, n_tp):
            ar1(d, False).wait_recv()
        tot = jnp.zeros((arow, sel_w), F32)
        for i in range(n_tp):
            tot = tot + arrecv[i].astype(F32)
        lane = lax.broadcasted_iota(jnp.int32, (arow, sel_w), 1)
        is_sq = (lane == pad_from) | (lane == pad_from + 1)
        ssum = jnp.sum(jnp.where(is_sq, tot, 0.0), axis=1, keepdims=True)
        factor = lax.rsqrt(ssum / (n_tp * feat) + 1e-05)
        f_hi = factor.astype(BF16).astype(F32)
        tot = jnp.where(lane == pad_from, f_hi, jnp.where(lane == pad_from + 1, factor - f_hi, tot * factor))
        mine = pl.ds(pl.multiple_of(tpi * arow, arow), arow)
        arres[mine, :] = tot.astype(BF16)

        def ar2(d, sending):
            to = lax.rem(tpi + d, n_tp)
            fr = lax.rem(tpi + n_tp - d, n_tp)
            base = tpi if sending else fr
            rows = pl.ds(pl.multiple_of(base * arow, arow), arow)
            return rcopy(arres.at[rows], arres.at[rows], ar2_s.at[d], ar2_r.at[d], {"tp": to})

        for d in range(1, n_tp):
            ar2(d, True).start()

        @pl.when(l == 0)
        def _():
            regroup(0, nreg // 4, nreg // 2)

        ag_wait(1, 8, 9)
        ag_start(1, 10, 11)
        ag_wait(1, 12, 13)
        ag_start(1, 14, 15)
        ag_wait(1, 16, 17)
        ag_start(1, 18, 19)

        @pl.when(l == 0)
        def _():
            regroup(0, nreg // 2, nreg)
            later_copies[2].start()

        for d in range(1, n_tp):
            ar2(d, False).wait_recv()
        tail = arres[:, rank:]
        tl = lax.broadcasted_iota(jnp.int32, (toks, LANE), 1)
        in_f = (tl == 2 * states) | (tl == 2 * states + 1)
        fac = jnp.sum(jnp.where(in_f, tail.astype(F32), 0.0), axis=1, keepdims=True)
        dt_c.wait()
        pre = jnp.dot(arres[:, :rank], w_dt_v[l], preferred_element_type=F32) + bias_ref[pl.ds(l, 1), :]
        step[...] = jnp.maximum(pre, 0.0) + jnp.log1p(jnp.exp(-jnp.abs(pre)))
        bx[...] = jnp.dot(tail, expand_b[...], preferred_element_type=F32)
        cx[...] = jnp.dot(tail, expand_c[...], preferred_element_type=F32)

        def accum(t, run):
            rows = pl.ds(pl.multiple_of(t * SUB, SUB), SUB)
            run = run + step[rows, :]
            cum[rows, :] = run
            return run

        ctot = lax.fori_loop(0, steps, accum, jnp.zeros((SUB, chans), F32))
        tsend[l] = jnp.broadcast_to(jnp.sum(ctot, axis=0, keepdims=True), (SUB, chans))
        for q in range(1, n_seq):
            @pl.when(q > seqi)
            def _():
                t_copy(l, q, True).start()

        skip_row = skip_ref[pl.ds(l, 1), :]
        th_row = thresh_ref[pl.ds(l, 1), :]

        def mm(u, first, pairs):
            rs = pl.ds(u * half, half)
            for i, (dz, dy) in enumerate(pairs):
                b = wrap(zc + dz) * SIDE + wrap(yc + dy)
                rows = pl.ds(pl.multiple_of(b * feat, feat), feat)
                val = jnp.dot(agbuf[b, rs], w_in_v[l, rows, :], preferred_element_type=F32)
                if first and i == 0:
                    proj[rs, :] = val
                else:
                    proj[rs, :] += val

        near = ((0, 0), (0, 1), (0, -1), (1, 0), (-1, 0), (1, 1), (1, -1), (-1, 1), (-1, -1))
        away = ((2, 0), (2, 1), (2, 2), (2, 3), (0, 2), (1, 2), (3, 2))

        def scan(u):
            for cb in range(ncb):
                cs = pl.ds(cb * LANE, LANE)
                na = [
                    jnp.broadcast_to(a_ref[l, s : s + 1, cs] * (-LOG2E), (SUB, LANE))
                    for s in range(states)
                ]
                skip = skip_row[:, cb * LANE : (cb + 1) * LANE]

                def scan_step(t, hs):
                    rows = pl.ds(pl.multiple_of(t * SUB, SUB), SUB)
                    st = step[rows, cs]
                    cur = proj[rows, cs]
                    dr = st * cur
                    acc = skip * cur
                    new = []
                    for s in range(states):
                        ls = pl.ds(s * LANE, LANE)
                        hn = jnp.exp2(st * na[s]) * hs[s] + bx[rows, ls] * dr
                        acc = acc + cx[rows, ls] * hn
                        new.append(hn)
                    yv[rows, cs] = acc
                    return tuple(new)

                if u == 0:
                    init = tuple(jnp.zeros((SUB, LANE), F32) for _ in range(states))
                else:
                    init = tuple(hst[s, :, cs] for s in range(states))
                hs = lax.fori_loop(u * steps // 2, (u + 1) * steps // 2, scan_step, init, unroll=4)
                if u == 0:
                    for s in range(states):
                        hst[s, :, cs] = hs[s]
                    continue
                sub = lax.broadcasted_iota(jnp.int32, (SUB, LANE), 0)
                ct = cum[pl.ds((steps - 1) * SUB, SUB), cs]
                for s in range(states):
                    e = hs[s]
                    p = jnp.exp2(ct * na[s])
                    for d in (1, 2, 4):
                        ok = sub >= d
                        e = e + jnp.where(ok, p * pltpu.roll(e, d, 0), 0.0)
                        p = p * jnp.where(ok, pltpu.roll(p, d, 0), 1.0)
                    esend_f[s : s + 1, cs] = e[SUB - 1 : SUB, :]
                    ein[s, :, cs] = jnp.where(sub >= 1, pltpu.roll(e, 1, 0), 0.0)
                    pin[s, :, cs] = jnp.where(sub >= 1, pltpu.roll(p, 1, 0), 1.0)

        @pl.when(l == 0)
        def _():
            later_copies[2].wait()
            regroup(1, 0, nreg)

        ag_wait(0, 6, 7, 10, 11, 14, 15, 18, 19)
        mm(0, True, near + away)
        proj[:half, :] = proj[:half, :] * fac[:half]
        scan(0)
        mm(1, True, near)
        ag_wait(1, 6, 7, 10, 11, 14, 15, 18, 19)
        mm(1, False, away)
        proj[half:, :] = proj[half:, :] * fac[half:]
        scan(1)

        esend[l] = esend_f[...].astype(BF16)
        for q in range(1, n_seq):
            @pl.when(q > seqi)
            def _():
                e_copy(l, q, True).start()

        for u in range(2):
            for k in AG_KEYS:
                for h in range(2):
                    ag_send(u, h, k).wait_send()
        for d in range(1, n_tp):
            ar1(d, True).wait_send()
            ar2(d, True).wait_send()

        rates = a_ref[l] * (-LOG2E)
        for q in range(n_seq - 1):
            @pl.when(q < seqi)
            def _():
                t_copy(l, q, False).wait_recv()
                hdec[q] = jnp.exp2(rates * trecv[l, q, 0:1, :])

        hdev[...] = jnp.zeros_like(hdev)
        for q in range(n_seq - 1):
            @pl.when(q < seqi)
            def _():
                e_copy(l, q, False).wait_recv()
                hdev[...] = hdec[q] * hdev[...] + erecv[l, q].astype(F32)

        def finish(u, c0, c1):
            rs = pl.ds(u * half, half)
            for cb in range(c0, c1):
                cs = pl.ds(cb * LANE, LANE)
                na = [
                    jnp.broadcast_to(a_ref[l, s : s + 1, cs] * (-LOG2E), (SUB, LANE))
                    for s in range(states)
                ]
                hin = [ein[s, :, cs] + pin[s, :, cs] * hdev[s : s + 1, cs] for s in range(states)]
                th = th_row[:, cb * LANE : (cb + 1) * LANE]

                def fold(t, unused):
                    rows = pl.ds(pl.multiple_of(t * SUB, SUB), SUB)
                    ct = cum[rows, cs]
                    acc = yv[rows, cs]
                    for s in range(states):
                        ls = pl.ds(s * LANE, LANE)
                        acc = acc + cx[rows, ls] * (jnp.exp2(ct * na[s]) * hin[s])
                    yv[rows, cs] = acc
                    return unused

                lax.fori_loop(u * steps // 2, (u + 1) * steps // 2, fold, 0, unroll=4)

                mixed = yv[rs, cs]
                fct = lax.rsqrt(jnp.mean(mixed * mixed, axis=1, keepdims=True) + 1e-05)
                normal = mixed * fct
                shrunk = jnp.maximum(normal - th, 0.0) - jnp.maximum(-normal - th, 0.0)
                gate = proj[rs, pl.ds(chans + cb * LANE, LANE)]
                gated[rs, cs] = (shrunk * (gate / (1.0 + jnp.exp(-gate)))).astype(BF16)

        finish(0, 0, ncb)
        out_c.wait()
        rs1(l, 0)
        finish(1, 0, ncb // 2)
        rs2(0)
        finish(1, ncb // 2, ncb)
        rs1(l, 1)

        rs2(1)
        rs3(0)

        rs4(0)

        @pl.when(l + 1 < layers)
        def _():
            publish(l + 1, 0)

        rs3(1)
        rs4(1)
        for u in range(2):
            for h in range(2):
                for k in range(11):
                    rs_copy(u, h, k).wait_send()
        for q in range(1, n_seq):
            @pl.when(q > seqi)
            def _():
                t_copy(l, q, True).wait_send()
                e_copy(l, q, True).wait_send()
        return unused

    lax.fori_loop(0, layers, layer, 0)
    out_ref[...] = lax.dot_general(
        perm, hid[...], (((0,), (0,)), ((), ())), preferred_element_type=F32
    ).astype(BF16)


def per_device(n_seq, tokens, norm_gain, w_in, w_low, w_dt, a_rate, dt_bias, skip_gain, threshold, w_out):
    toks, feat = tokens.shape
    layers, model, _, chans = w_in.shape
    states = a_rate.shape[1]
    rank = w_dt.shape[1]
    n_tp = SIDE * SIDE
    half, quart, eighth = toks // 2, toks // 4, toks // 8
    per_d = 2 * chans // LANE
    sel_w = rank + LANE
    dims = (layers, n_seq, toks, feat, chans, states, rank)
    vm = pl.BlockSpec(memory_space=pltpu.VMEM)
    hb = pl.BlockSpec(memory_space=pl.ANY)
    dma = pltpu.SemaphoreType.DMA
    V = pltpu.VMEM
    return pl.pallas_call(
        functools.partial(kernel_body, dims),
        out_shape=jax.ShapeDtypeStruct((toks, feat), BF16),
        in_specs=[vm, vm, hb, hb, hb, vm, vm, vm, vm, hb],
        out_specs=vm,
        scratch_shapes=[
            V((model * per_d, LANE), BF16),
            V((2 * LANE, 2 * LANE), BF16),
            V((layers, model, 2 * chans), BF16),
            V((layers, sel_w, feat), BF16),
            V((layers, rank, chans), BF16),
            V((layers, chans, model), BF16),
            V((toks, feat), BF16),
            V((n_tp, toks, feat), BF16),
            V((toks, LANE), F32),
            V((toks, sel_w), BF16),
            V((n_tp, toks // n_tp, sel_w), BF16),
            V((toks, sel_w), BF16),
            V((LANE, states * LANE), BF16),
            V((LANE, states * LANE), BF16),
            V((toks, states * LANE), F32),
            V((toks, states * LANE), F32),
            V((toks, chans), F32),
            V((toks, chans), F32),
            V((toks, 2 * chans), F32),
            V((toks, chans), F32),
            V((states, SUB, chans), F32),
            V((states, SUB, chans), F32),
            V((states, SUB, chans), F32),
            V((states, chans), F32),
            V((n_seq, states, chans), F32),
            V((states, chans), F32),
            V((layers, states, chans), BF16),
            V((layers, n_seq, states, chans), BF16),
            V((layers, SUB, chans), F32),
            V((layers, n_seq, SUB, chans), F32),
            V((toks, chans), BF16),
            V((2, 2, SIDE, SIDE, quart, feat), BF16),
            V((2, 2, 2, SIDE, eighth, feat), BF16),
            V((2, 2, 2, SIDE, quart, feat), BF16),
            V((2, 2, SIDE, quart, feat), BF16),
            V((2, 2, 3, quart, feat), BF16),
            dma((layers, 4)),
            dma((2, 2, 20)),
            dma((2, 2, 20)),
            dma((n_tp,)),
            dma((n_tp,)),
            dma((n_tp,)),
            dma((n_tp,)),
            dma((layers, n_seq)),
            dma((layers, n_seq)),
            dma((layers, n_seq)),
            dma((layers, n_seq)),
            dma((2, 2, 11)),
            dma((2, 2, 11)),
        ],
        compiler_params=pltpu.CompilerParams(
            collective_id=0, has_side_effects=True, vmem_limit_bytes=60 * 1024 * 1024
        ),
    )(
        tokens,
        norm_gain,
        jnp.swapaxes(w_in.reshape(layers, model, 2, chans // LANE, LANE), 2, 3).reshape(
            layers, model * per_d, LANE
        ),
        jnp.swapaxes(w_low, 1, 2),
        w_dt,
        a_rate,
        dt_bias,
        skip_gain,
        threshold,
        w_out,
    )


def solution(mesh):
    in_specs = (
        P("seq", "tp"),
        P(),
        P(None, None, None, "tp"),
        P(None, "tp", None),
        P(None, None, "tp"),
        P(None, None, "tp"),
        P(None, "tp"),
        P(None, "tp"),
        P(None, "tp"),
        P(None, "tp", None),
    )
    return jax.shard_map(
        functools.partial(per_device, mesh.shape["seq"]),
        mesh=mesh,
        in_specs=in_specs,
        out_specs=P("seq", "tp"),
        check_vma=False,
    )
```

```python
import functools
import math

import jax
import jax.numpy as jnp
from jax import lax
from jax.experimental import pallas as pl
from jax.experimental.pallas import tpu as pltpu
from jax.sharding import PartitionSpec as P

MESH = pl.DeviceIdType.MESH
F32 = jnp.float32
BF16 = jnp.bfloat16
SUB = 8
LANE = 128
SIDE = 4
LOG2E = math.log2(math.e)
OFFS = (0, -1, 1, 2)
OUT = (2, 1, -1, 0)
WIDE = 8
AG_KEYS = (0, 1, 2) + tuple(range(4, 20))


def kernel_body(
    dims,
    tok_ref,
    gain_ref,
    w_in_hbm,
    w_low_hbm,
    w_dt_hbm,
    a_ref,
    bias_ref,
    skip_ref,
    thresh_ref,
    w_out_hbm,
    out_ref,
    raw,
    seld,
    w_in_v,
    w_low_v,
    w_dt_v,
    w_out_v,
    hid,
    agbuf,
    sqv,
    selp,
    arrecv,
    arres,
    expand_b,
    expand_c,
    bx,
    cx,
    step,
    cum,
    proj,
    yv,
    pin,
    ein,
    hst,
    hdev,
    hdec,
    esend_f,
    esend,
    erecv,
    tsend,
    trecv,
    gated,
    pbuf,
    x1,
    x2,
    s2,
    x3,
    wsem,
    ag_s,
    ag_r,
    ar1_s,
    ar1_r,
    ar2_s,
    ar2_r,
    t_s,
    t_r,
    e_s,
    e_r,
    rs_s,
    rs_r,
):
    layers, n_seq, toks, feat, chans, states, rank = dims
    n_tp = SIDE * SIDE
    half = toks // 2
    quart = toks // 4
    eighth = toks // 8
    per_d = 2 * chans // LANE
    steps = toks // SUB
    arow = toks // n_tp
    ncb = chans // LANE
    seqi = lax.axis_index("seq")
    tpi = lax.axis_index("tp")
    zc = tpi // SIDE
    yc = lax.rem(tpi, SIDE)

    def wrap(v):
        return lax.rem(v + 2 * SIDE, SIDE)

    pos = ((yc, zc), (zc, yc))

    def blk(h, c1, c2):
        return c2 * SIDE + c1 if h == 0 else c1 * SIDE + c2

    def nb(h, axis, d):
        p1, p2 = pos[h]
        if axis == 1:
            return {"tp": blk(h, wrap(p1 + d), p2)}
        return {"tp": blk(h, p1, wrap(p2 + d))}

    def rcopy(src, dst, ssem, rsem, dev):
        return pltpu.make_async_remote_copy(
            src_ref=src, dst_ref=dst, send_sem=ssem, recv_sem=rsem,
            device_id=dev, device_id_type=MESH,
        )

    def wcopies(l):
        return (
            pltpu.make_async_copy(w_low_hbm.at[l], w_low_v.at[l, : rank + 2 * states], wsem.at[l, 0]),
            pltpu.make_async_copy(w_dt_hbm.at[l], w_dt_v.at[l], wsem.at[l, 1]),
            pltpu.make_async_copy(w_in_hbm.at[l], raw, wsem.at[l, 2]),
            pltpu.make_async_copy(w_out_hbm.at[l], w_out_v.at[l], wsem.at[l, 3]),
        )

    first_copies = wcopies(0)
    later_copies = wcopies(1)
    for c in (first_copies[0], first_copies[2]):
        c.start()

    barrier = pltpu.get_barrier_semaphore()
    for d in range(1, n_tp):
        pl.semaphore_signal(barrier, inc=1, device_id={"tp": lax.rem(tpi + d, n_tp)}, device_id_type=MESH)
    for d in range(1, n_seq):
        pl.semaphore_signal(barrier, inc=1, device_id={"seq": lax.rem(seqi + d, n_seq)}, device_id_type=MESH)
    pl.semaphore_wait(barrier, n_tp + n_seq - 2)

    ri = lax.broadcasted_iota(jnp.int32, (toks, toks), 0)
    ci = lax.broadcasted_iota(jnp.int32, (toks, toks), 1)
    perm = jnp.where(ci == lax.rem(ri, SUB) * steps + ri // SUB, 1.0, 0.0).astype(BF16)
    hid[...] = jnp.dot(perm, tok_ref[...], preferred_element_type=F32).astype(BF16)

    def ag_info(u, h, k):
        p1, p2 = pos[h]
        r0 = u * half + h * quart
        full = pl.ds(r0, quart)
        lo = pl.ds(r0, eighth)
        hi = pl.ds(r0 + eighth, eighth)
        if k < 4:
            to = (1, -1, 2)[k]
            src_d, dst_d, rows, ax = 0, -to, full, 1

            def at(d):
                return blk(h, wrap(p1 + d), p2)
        else:
            src_d, dst_d, rows, to = (
                (0, -1, full, 1),
                (0, 1, full, -1),
                (-1, -2, lo, 1),
                (1, 2, hi, -1),
            )[(k - 4) % 4]
            o = OFFS[(k - 4) // 4]
            ax = 2

            def at(d):
                return blk(h, wrap(p1 + o), wrap(p2 + d))

        return at(src_d), at(dst_d), rows, nb(h, ax, to)

    def ag_send(u, h, k):
        src, _, rows, dev = ag_info(u, h, k)
        ref = agbuf.at[src, rows]
        return rcopy(ref, ref, ag_s.at[u, h, k], ag_r.at[u, h, k], dev)

    def ag_start(u, *ks):
        for k in ks:
            for h in range(2):
                ag_send(u, h, k).start()

    def ag_wait(u, *ks):
        for k in ks:
            for h in range(2):
                _, dst, rows, dev = ag_info(u, h, k)
                ref = agbuf.at[dst, rows]
                rcopy(ref, ref, ag_s.at[u, h, k], ag_r.at[u, h, k], dev).wait_recv()

    def publish(l, u):
        rows = pl.ds(u * half, half)
        own = hid[rows, :].astype(F32)
        gain_row = gain_ref[pl.ds(l, 1), pl.ds(pl.multiple_of(tpi * feat, feat), feat)]
        agbuf[tpi, rows] = (own * gain_row).astype(BF16)
        sqv[rows, :] = jnp.broadcast_to(jnp.sum(own * own, axis=1, keepdims=True), (half, LANE))
        ag_start(u, 0, 1, 4, 5, 2)

    publish(0, 0)

    ei = lax.broadcasted_iota(jnp.int32, (LANE, states * LANE), 0)
    ej = lax.broadcasted_iota(jnp.int32, (LANE, states * LANE), 1) // LANE
    expand_b[...] = jnp.where(ei == ej, 1.0, 0.0).astype(BF16)
    expand_c[...] = jnp.where(ei == ej + states, 1.0, 0.0).astype(BF16)
    grp = 2 * LANE // per_d
    gi = lax.broadcasted_iota(jnp.int32, (2 * LANE, 2 * LANE), 0)
    gj = lax.broadcasted_iota(jnp.int32, (2 * LANE, 2 * LANE), 1)
    seld[...] = jnp.where(gj == lax.rem(gi, grp) * per_d + gi // grp, 1.0, 0.0).astype(BF16)
    sel_w = rank + LANE
    pad_from = rank + 2 * states
    for l in range(layers):
        w_low_v[l, pad_from:, :] = jnp.zeros((sel_w - pad_from, feat), BF16)

    def regroup(b0, b1):
        def one(i, unused):
            r = pl.multiple_of(i * WIDE * 2 * LANE, WIDE * 2 * LANE)
            parts = [raw[pl.ds(r + v * 2 * LANE, 2 * LANE), :] for v in range(WIDE)]
            got = jnp.dot(
                seld[...], jnp.concatenate(parts, axis=1), preferred_element_type=F32
            ).astype(BF16)
            d0 = pl.multiple_of(i * WIDE * grp, WIDE * grp)
            for q in range(per_d):
                cols = pl.ds((q % 2) * chans + (q // 2) * LANE, LANE)
                for v in range(WIDE):
                    w_in_v[pl.ds(d0 + v * grp, grp), cols] = got[
                        q * grp : (q + 1) * grp, v * LANE : (v + 1) * LANE
                    ]
            return unused

        lax.fori_loop(b0, b1, one, 0)

    nreg = n_tp * feat // (WIDE * grp)

    def seq_copy(l, src, dst, ss, rs, q, sending):
        slot = seqi if sending else q
        return rcopy(src, dst.at[l, slot], ss.at[l, q], rs.at[l, slot], {"seq": q})

    def t_copy(l, q, sending):
        return seq_copy(l, tsend.at[l], trecv, t_s, t_r, q, sending)

    def e_copy(l, q, sending):
        return seq_copy(l, esend.at[l], erecv, e_s, e_r, q, sending)

    lo = pl.ds(0, eighth)
    hi = pl.ds(eighth, eighth)

    def rpos(h):
        p2, p1 = pos[h]
        return p1, p2

    def rnb(h, axis, d):
        return nb(h, 3 - axis, d)

    ahead, up, down, here = range(SIDE)
    parts = (pl.ds(0, 2), pl.ds(2, 2))

    def rs_copy(u, h, k):
        if k < 8:
            piece = parts[(k // 2) % 2]
            way = k % 2
            if k < 4:
                src = pbuf.at[u, h, ahead, piece, (lo, hi)[way]]
                dst = x1.at[u, h, way, piece]
            else:
                src = pbuf.at[u, h, (up, down)[way], piece]
                dst = x2.at[u, h, way, piece]
            dev = rnb(h, 1, (1, -1)[way])
        else:
            src = s2.at[u, h, (ahead, up, down)[k - 8]]
            dst = x3.at[u, h, k - 8]
            dev = rnb(h, 2, OUT[k - 8])
        return rcopy(src, dst, rs_s.at[u, h, k], rs_r.at[u, h, k], dev)

    def omm(l, u, pairs):
        lhs = gated[u * half : (u + 1) * half, :]
        for dz, dy in pairs:
            z, y = wrap(zc + dz), wrap(yc + dy)
            cols = pl.ds(pl.multiple_of((z * SIDE + y) * feat, feat), feat)
            val = jnp.dot(lhs, w_out_v[l, :, cols], preferred_element_type=F32).astype(BF16)
            iz, iy = OUT.index(dz), OUT.index(dy)
            pbuf[u, 0, iz, iy] = val[:quart]
            pbuf[u, 1, iy, iz] = val[quart:]

    def rs1(l, u):
        omm(l, u, ((2, 2), (2, 1), (1, 2)))
        for h in range(2):
            rs_copy(u, h, 0).start()
            rs_copy(u, h, 1).start()
        omm(l, u, ((2, -1), (2, 0), (-1, 2), (0, 2)))
        for h in range(2):
            rs_copy(u, h, 2).start()
            rs_copy(u, h, 3).start()
        omm(l, u, ((1, 1), (1, -1), (1, 0), (-1, 1), (-1, -1), (-1, 0), (0, 1), (0, -1)))
        omm(l, u, ((0, 0),))

    def rs2(u):
        for p in range(2):
            piece = parts[p]
            for h in range(2):
                for way in range(2):
                    rows = (lo, hi)[way]
                    side = (up, down)[way]
                    rs_copy(u, h, 2 * p + way).wait_recv()
                    pbuf[u, h, side, piece, rows] = (
                        pbuf[u, h, side, piece, rows].astype(F32) + x1[u, h, way, piece].astype(F32)
                    ).astype(BF16)
                    rs_copy(u, h, 4 + 2 * p + way).start()

    def sum3(u, h, c2):
        return (
            pbuf[u, h, here, c2].astype(F32) + x2[u, h, 0, c2].astype(F32) + x2[u, h, 1, c2].astype(F32)
        )

    def rs3(u):
        for p in range(2):
            for h in range(2):
                rs_copy(u, h, 4 + 2 * p).wait_recv()
                rs_copy(u, h, 5 + 2 * p).wait_recv()
                for c2 in (ahead, up) if p == 0 else (down,):
                    s2[u, h, c2] = sum3(u, h, c2).astype(BF16)
                    rs_copy(u, h, 8 + c2).start()

    def rs4(u):
        for h in range(2):
            total = sum3(u, h, here)
            for k in range(3):
                rs_copy(u, h, 8 + k).wait_recv()
                total = total + x3[u, h, k].astype(F32)
            rows = pl.ds(u * half + h * quart, quart)
            hid[rows, :] = (hid[rows, :].astype(F32) + total).astype(BF16)

    def layer(l, unused):
        low_c, dt_c, in_c, out_c = wcopies(l)
        publish(l, 1)

        low_c.wait()
        selv = lax.dot_general(
            agbuf[tpi], w_low_v[l], (((1,), (1,)), ((), ())), preferred_element_type=F32
        )
        sq = sqv[:, 0:1]
        sq_hi = sq.astype(BF16).astype(F32)
        lane = lax.broadcasted_iota(jnp.int32, (toks, sel_w), 1)
        selv = jnp.where(lane == pad_from, sq_hi, selv)
        selv = jnp.where(lane == pad_from + 1, sq - sq_hi, selv)
        selp[...] = selv.astype(BF16)
        arrecv[tpi] = selp[pl.ds(pl.multiple_of(tpi * arow, arow), arow), :]

        def ar1(d, sending):
            to = lax.rem(tpi + d, n_tp)
            fr = lax.rem(tpi + n_tp - d, n_tp)
            rows = pl.ds(pl.multiple_of(to * arow, arow), arow)
            dst = arrecv.at[tpi] if sending else arrecv.at[fr]
            return rcopy(selp.at[rows], dst, ar1_s.at[d], ar1_r.at[d], {"tp": to})

        for d in range(1, n_tp):
            ar1(d, True).start()

        ag_wait(0, 0, 1)
        ag_start(0, 8, 9, 12, 13)
        ag_wait(0, 4, 5)
        ag_start(0, 6, 7)
        ag_wait(0, 2)
        ag_start(0, 16, 17)

        @pl.when(l == 0)
        def _():
            in_c.wait()
            for c in (first_copies[1], first_copies[3], later_copies[0], later_copies[1], later_copies[3]):
                c.start()
            regroup(0, nreg // 4)

        ag_wait(1, 0, 1)
        ag_start(1, 8, 9, 12, 13)
        ag_wait(1, 4, 5)
        ag_start(1, 6, 7)
        ag_wait(1, 2)
        ag_start(1, 16, 17)
        ag_wait(0, 8, 9)
        ag_start(0, 10, 11)
        ag_wait(0, 12, 13)
        ag_start(0, 14, 15)
        ag_wait(0, 16, 17)
        ag_start(0, 18, 19)

        for d in range(1, n_tp):
            ar1(d, False).wait_recv()
        tot = jnp.zeros((arow, sel_w), F32)
        for i in range(n_tp):
            tot = tot + arrecv[i].astype(F32)
        lane = lax.broadcasted_iota(jnp.int32, (arow, sel_w), 1)
        is_sq = (lane == pad_from) | (lane == pad_from + 1)
        ssum = jnp.sum(jnp.where(is_sq, tot, 0.0), axis=1, keepdims=True)
        factor = lax.rsqrt(ssum / (n_tp * feat) + 1e-05)
        f_hi = factor.astype(BF16).astype(F32)
        tot = jnp.where(lane == pad_from, f_hi, jnp.where(lane == pad_from + 1, factor - f_hi, tot * factor))
        mine = pl.ds(pl.multiple_of(tpi * arow, arow), arow)
        arres[mine, :] = tot.astype(BF16)

        def ar2(d, sending):
            to = lax.rem(tpi + d, n_tp)
            fr = lax.rem(tpi + n_tp - d, n_tp)
            base = tpi if sending else fr
            rows = pl.ds(pl.multiple_of(base * arow, arow), arow)
            return rcopy(arres.at[rows], arres.at[rows], ar2_s.at[d], ar2_r.at[d], {"tp": to})

        for d in range(1, n_tp):
            ar2(d, True).start()

        @pl.when(l == 0)
        def _():
            regroup(nreg // 4, nreg // 2)

        ag_wait(1, 8, 9)
        ag_start(1, 10, 11)
        ag_wait(1, 12, 13)
        ag_start(1, 14, 15)
        ag_wait(1, 16, 17)
        ag_start(1, 18, 19)

        @pl.when(l == 0)
        def _():
            regroup(nreg // 2, nreg)
            later_copies[2].start()

        def mm(u, first, pairs):
            rs = pl.ds(u * half, half)
            for i, (dz, dy) in enumerate(pairs):
                b = wrap(zc + dz) * SIDE + wrap(yc + dy)
                rows = pl.ds(pl.multiple_of(b * feat, feat), feat)
                val = jnp.dot(agbuf[b, rs], w_in_v[rows, :], preferred_element_type=F32)
                if first and i == 0:
                    proj[rs, :] = val
                else:
                    proj[rs, :] += val

        near = ((0, 0), (0, 1), (0, -1), (1, 0), (-1, 0), (1, 1), (1, -1), (-1, 1), (-1, -1))
        away = ((2, 0), (2, 1), (2, 2), (2, 3), (0, 2), (1, 2), (3, 2))

        mm(0, True, near)
        ag_wait(0, 6, 7, 10, 11, 14, 15, 18, 19)
        mm(0, False, away)
        mm(1, True, near)
        for d in range(1, n_tp):
            ar2(d, False).wait_recv()
        tail = arres[:, rank:]
        tl = lax.broadcasted_iota(jnp.int32, (toks, LANE), 1)
        in_f = (tl == 2 * states) | (tl == 2 * states + 1)
        fac = jnp.sum(jnp.where(in_f, tail.astype(F32), 0.0), axis=1, keepdims=True)
        dt_c.wait()
        pre = jnp.dot(arres[:, :rank], w_dt_v[l], preferred_element_type=F32) + bias_ref[pl.ds(l, 1), :]
        step[...] = jnp.maximum(pre, 0.0) + jnp.log1p(jnp.exp(-jnp.abs(pre)))
        bx[...] = jnp.dot(tail, expand_b[...], preferred_element_type=F32)
        cx[...] = jnp.dot(tail, expand_c[...], preferred_element_type=F32)

        def accum(t, run):
            rows = pl.ds(pl.multiple_of(t * SUB, SUB), SUB)
            run = run + step[rows, :]
            cum[rows, :] = run
            return run

        ctot = lax.fori_loop(0, steps, accum, jnp.zeros((SUB, chans), F32))
        tsend[l] = jnp.broadcast_to(jnp.sum(ctot, axis=0, keepdims=True), (SUB, chans))
        for q in range(1, n_seq):
            @pl.when(q > seqi)
            def _():
                t_copy(l, q, True).start()

        skip_row = skip_ref[pl.ds(l, 1), :]
        th_row = thresh_ref[pl.ds(l, 1), :]

        def scan(u):
            for cb in range(ncb):
                cs = pl.ds(cb * LANE, LANE)
                na = [
                    jnp.broadcast_to(a_ref[l, s : s + 1, cs] * (-LOG2E), (SUB, LANE))
                    for s in range(states)
                ]
                skip = skip_row[:, cb * LANE : (cb + 1) * LANE]

                def scan_step(t, hs):
                    rows = pl.ds(pl.multiple_of(t * SUB, SUB), SUB)
                    st = step[rows, cs]
                    cur = proj[rows, cs]
                    dr = st * cur
                    acc = skip * cur
                    new = []
                    for s in range(states):
                        ls = pl.ds(s * LANE, LANE)
                        hn = jnp.exp2(st * na[s]) * hs[s] + bx[rows, ls] * dr
                        acc = acc + cx[rows, ls] * hn
                        new.append(hn)
                    yv[rows, cs] = acc
                    return tuple(new)

                if u == 0:
                    init = tuple(jnp.zeros((SUB, LANE), F32) for _ in range(states))
                else:
                    init = tuple(hst[s, :, cs] for s in range(states))
                hs = lax.fori_loop(u * steps // 2, (u + 1) * steps // 2, scan_step, init, unroll=2)
                if u == 0:
                    for s in range(states):
                        hst[s, :, cs] = hs[s]
                    continue
                sub = lax.broadcasted_iota(jnp.int32, (SUB, LANE), 0)
                ct = cum[pl.ds((steps - 1) * SUB, SUB), cs]
                for s in range(states):
                    e = hs[s]
                    p = jnp.exp2(ct * na[s])
                    for d in (1, 2, 4):
                        ok = sub >= d
                        e = e + jnp.where(ok, p * pltpu.roll(e, d, 0), 0.0)
                        p = p * jnp.where(ok, pltpu.roll(p, d, 0), 1.0)
                    esend_f[s : s + 1, cs] = e[SUB - 1 : SUB, :]
                    ein[s, :, cs] = jnp.where(sub >= 1, pltpu.roll(e, 1, 0), 0.0)
                    pin[s, :, cs] = jnp.where(sub >= 1, pltpu.roll(p, 1, 0), 1.0)

        proj[:half, :] = proj[:half, :] * fac[:half]
        scan(0)
        ag_wait(1, 6, 7, 10, 11, 14, 15, 18, 19)
        mm(1, False, away)
        proj[half:, :] = proj[half:, :] * fac[half:]
        scan(1)

        esend[l] = esend_f[...].astype(BF16)
        for q in range(1, n_seq):
            @pl.when(q > seqi)
            def _():
                e_copy(l, q, True).start()

        for u in range(2):
            for k in AG_KEYS:
                for h in range(2):
                    ag_send(u, h, k).wait_send()
        for d in range(1, n_tp):
            ar1(d, True).wait_send()
            ar2(d, True).wait_send()

        rates = a_ref[l] * (-LOG2E)
        for q in range(n_seq - 1):
            @pl.when(q < seqi)
            def _():
                t_copy(l, q, False).wait_recv()
                hdec[q] = jnp.exp2(rates * trecv[l, q, 0:1, :])

        hdev[...] = jnp.zeros_like(hdev)
        for q in range(n_seq - 1):
            @pl.when(q < seqi)
            def _():
                e_copy(l, q, False).wait_recv()
                hdev[...] = hdec[q] * hdev[...] + erecv[l, q].astype(F32)

        def finish(u, c0, c1):
            rs = pl.ds(u * half, half)
            for cb in range(c0, c1):
                cs = pl.ds(cb * LANE, LANE)
                na = [
                    jnp.broadcast_to(a_ref[l, s : s + 1, cs] * (-LOG2E), (SUB, LANE))
                    for s in range(states)
                ]
                hin = [ein[s, :, cs] + pin[s, :, cs] * hdev[s : s + 1, cs] for s in range(states)]
                th = th_row[:, cb * LANE : (cb + 1) * LANE]

                def fold(t, unused):
                    rows = pl.ds(pl.multiple_of(t * SUB, SUB), SUB)
                    ct = cum[rows, cs]
                    acc = yv[rows, cs]
                    for s in range(states):
                        ls = pl.ds(s * LANE, LANE)
                        acc = acc + cx[rows, ls] * (jnp.exp2(ct * na[s]) * hin[s])
                    yv[rows, cs] = acc
                    return unused

                lax.fori_loop(u * steps // 2, (u + 1) * steps // 2, fold, 0, unroll=4)

                mixed = yv[rs, cs]
                fct = lax.rsqrt(jnp.mean(mixed * mixed, axis=1, keepdims=True) + 1e-05)
                normal = mixed * fct
                shrunk = jnp.maximum(normal - th, 0.0) - jnp.maximum(-normal - th, 0.0)
                gate = proj[rs, pl.ds(chans + cb * LANE, LANE)]
                gated[rs, cs] = (shrunk * (gate / (1.0 + jnp.exp(-gate)))).astype(BF16)

        finish(0, 0, ncb)
        out_c.wait()
        rs1(l, 0)
        finish(1, 0, ncb // 2)
        rs2(0)
        finish(1, ncb // 2, ncb)
        rs1(l, 1)

        @pl.when(l + 1 < layers)
        def _():
            later_copies[2].wait()
            regroup(0, nreg // 8)

        rs2(1)
        rs3(0)

        @pl.when(l + 1 < layers)
        def _():
            regroup(nreg // 8, nreg // 2)

        rs4(0)

        @pl.when(l + 1 < layers)
        def _():
            publish(l + 1, 0)

        rs3(1)

        @pl.when(l + 1 < layers)
        def _():
            regroup(nreg // 2, nreg)

        rs4(1)
        for u in range(2):
            for h in range(2):
                for k in range(11):
                    rs_copy(u, h, k).wait_send()
        for q in range(1, n_seq):
            @pl.when(q > seqi)
            def _():
                t_copy(l, q, True).wait_send()
                e_copy(l, q, True).wait_send()
        return unused

    lax.fori_loop(0, layers, layer, 0)
    out_ref[...] = lax.dot_general(
        perm, hid[...], (((0,), (0,)), ((), ())), preferred_element_type=F32
    ).astype(BF16)


def per_device(n_seq, tokens, norm_gain, w_in, w_low, w_dt, a_rate, dt_bias, skip_gain, threshold, w_out):
    toks, feat = tokens.shape
    layers, model, _, chans = w_in.shape
    states = a_rate.shape[1]
    rank = w_dt.shape[1]
    n_tp = SIDE * SIDE
    half, quart, eighth = toks // 2, toks // 4, toks // 8
    per_d = 2 * chans // LANE
    sel_w = rank + LANE
    dims = (layers, n_seq, toks, feat, chans, states, rank)
    vm = pl.BlockSpec(memory_space=pltpu.VMEM)
    hb = pl.BlockSpec(memory_space=pl.ANY)
    dma = pltpu.SemaphoreType.DMA
    V = pltpu.VMEM
    return pl.pallas_call(
        functools.partial(kernel_body, dims),
        out_shape=jax.ShapeDtypeStruct((toks, feat), BF16),
        in_specs=[vm, vm, hb, hb, hb, vm, vm, vm, vm, hb],
        out_specs=vm,
        scratch_shapes=[
            V((model * per_d, LANE), BF16),
            V((2 * LANE, 2 * LANE), BF16),
            V((model, 2 * chans), BF16),
            V((layers, sel_w, feat), BF16),
            V((layers, rank, chans), BF16),
            V((layers, chans, model), BF16),
            V((toks, feat), BF16),
            V((n_tp, toks, feat), BF16),
            V((toks, LANE), F32),
            V((toks, sel_w), BF16),
            V((n_tp, toks // n_tp, sel_w), BF16),
            V((toks, sel_w), BF16),
            V((LANE, states * LANE), BF16),
            V((LANE, states * LANE), BF16),
            V((toks, states * LANE), F32),
            V((toks, states * LANE), F32),
            V((toks, chans), F32),
            V((toks, chans), F32),
            V((toks, 2 * chans), F32),
            V((toks, chans), F32),
            V((states, SUB, chans), F32),
            V((states, SUB, chans), F32),
            V((states, SUB, chans), F32),
            V((states, chans), F32),
            V((n_seq, states, chans), F32),
            V((states, chans), F32),
            V((layers, states, chans), BF16),
            V((layers, n_seq, states, chans), BF16),
            V((layers, SUB, chans), F32),
            V((layers, n_seq, SUB, chans), F32),
            V((toks, chans), BF16),
            V((2, 2, SIDE, SIDE, quart, feat), BF16),
            V((2, 2, 2, SIDE, eighth, feat), BF16),
            V((2, 2, 2, SIDE, quart, feat), BF16),
            V((2, 2, SIDE, quart, feat), BF16),
            V((2, 2, 3, quart, feat), BF16),
            dma((layers, 4)),
            dma((2, 2, 20)),
            dma((2, 2, 20)),
            dma((n_tp,)),
            dma((n_tp,)),
            dma((n_tp,)),
            dma((n_tp,)),
            dma((layers, n_seq)),
            dma((layers, n_seq)),
            dma((layers, n_seq)),
            dma((layers, n_seq)),
            dma((2, 2, 11)),
            dma((2, 2, 11)),
        ],
        compiler_params=pltpu.CompilerParams(
            collective_id=0, has_side_effects=True, vmem_limit_bytes=60 * 1024 * 1024
        ),
    )(
        tokens,
        norm_gain,
        jnp.swapaxes(w_in.reshape(layers, model, 2, chans // LANE, LANE), 2, 3).reshape(
            layers, model * per_d, LANE
        ),
        jnp.swapaxes(w_low, 1, 2),
        w_dt,
        a_rate,
        dt_bias,
        skip_gain,
        threshold,
        w_out,
    )


def solution(mesh):
    in_specs = (
        P("seq", "tp"),
        P(),
        P(None, None, None, "tp"),
        P(None, "tp", None),
        P(None, None, "tp"),
        P(None, None, "tp"),
        P(None, "tp"),
        P(None, "tp"),
        P(None, "tp"),
        P(None, "tp", None),
    )
    return jax.shard_map(
        functools.partial(per_device, mesh.shape["seq"]),
        mesh=mesh,
        in_specs=in_specs,
        out_specs=P("seq", "tp"),
        check_vma=False,
    )
```

```python
import functools
import math

import jax
import jax.numpy as jnp
from jax import lax
from jax.experimental import pallas as pl
from jax.experimental.pallas import tpu as pltpu
from jax.sharding import PartitionSpec as P

MESH = pl.DeviceIdType.MESH
F32 = jnp.float32
BF16 = jnp.bfloat16
SUB = 8
LANE = 128
SIDE = 4
LOG2E = math.log2(math.e)
OFFS = (0, -1, 1, 2)
OUT = (2, 1, -1, 0)
WIDE = 8
AG_KEYS = (0, 1, 2) + tuple(range(4, 20))


def kernel_body(
    dims,
    tok_ref,
    gain_ref,
    w_in_hbm,
    w_low_hbm,
    w_dt_hbm,
    a_ref,
    bias_ref,
    skip_ref,
    thresh_ref,
    w_out_hbm,
    out_ref,
    raw,
    seld,
    w_in_v,
    w_low_v,
    w_dt_v,
    w_out_v,
    hid,
    agbuf,
    sqv,
    selp,
    arrecv,
    arres,
    expand_b,
    expand_c,
    bx,
    cx,
    step,
    cum,
    proj,
    yv,
    pin,
    ein,
    hst,
    hdev,
    hdec,
    esend_f,
    esend,
    erecv,
    tsend,
    trecv,
    gated,
    pbuf,
    x1,
    x2,
    s2,
    x3,
    wsem,
    ag_s,
    ag_r,
    ar1_s,
    ar1_r,
    ar2_s,
    ar2_r,
    t_s,
    t_r,
    e_s,
    e_r,
    rs_s,
    rs_r,
):
    layers, n_seq, toks, feat, chans, states, rank = dims
    n_tp = SIDE * SIDE
    half = toks // 2
    quart = toks // 4
    eighth = toks // 8
    per_d = 2 * chans // LANE
    steps = toks // SUB
    arow = toks // n_tp
    ncb = chans // LANE
    seqi = lax.axis_index("seq")
    tpi = lax.axis_index("tp")
    zc = tpi // SIDE
    yc = lax.rem(tpi, SIDE)

    def wrap(v):
        return lax.rem(v + 2 * SIDE, SIDE)

    pos = ((yc, zc), (zc, yc))

    def blk(h, c1, c2):
        return c2 * SIDE + c1 if h == 0 else c1 * SIDE + c2

    def nb(h, axis, d):
        p1, p2 = pos[h]
        if axis == 1:
            return {"tp": blk(h, wrap(p1 + d), p2)}
        return {"tp": blk(h, p1, wrap(p2 + d))}

    def rcopy(src, dst, ssem, rsem, dev):
        return pltpu.make_async_remote_copy(
            src_ref=src, dst_ref=dst, send_sem=ssem, recv_sem=rsem,
            device_id=dev, device_id_type=MESH,
        )

    def wcopies(l):
        return (
            pltpu.make_async_copy(w_low_hbm.at[l], w_low_v.at[l, : rank + 2 * states], wsem.at[l, 0]),
            pltpu.make_async_copy(w_dt_hbm.at[l], w_dt_v.at[l], wsem.at[l, 1]),
            pltpu.make_async_copy(w_in_hbm.at[l], raw, wsem.at[l, 2]),
            pltpu.make_async_copy(w_out_hbm.at[l], w_out_v.at[l], wsem.at[l, 3]),
        )

    first_copies = wcopies(0)
    later_copies = wcopies(1)
    for c in (first_copies[0], first_copies[2]):
        c.start()

    barrier = pltpu.get_barrier_semaphore()
    for d in range(1, n_tp):
        pl.semaphore_signal(barrier, inc=1, device_id={"tp": lax.rem(tpi + d, n_tp)}, device_id_type=MESH)
    for d in range(1, n_seq):
        pl.semaphore_signal(barrier, inc=1, device_id={"seq": lax.rem(seqi + d, n_seq)}, device_id_type=MESH)
    pl.semaphore_wait(barrier, n_tp + n_seq - 2)

    ri = lax.broadcasted_iota(jnp.int32, (toks, toks), 0)
    ci = lax.broadcasted_iota(jnp.int32, (toks, toks), 1)
    perm = jnp.where(ci == lax.rem(ri, SUB) * steps + ri // SUB, 1.0, 0.0).astype(BF16)
    hid[...] = jnp.dot(perm, tok_ref[...], preferred_element_type=F32).astype(BF16)

    def ag_info(u, h, k):
        p1, p2 = pos[h]
        r0 = u * half + h * quart
        full = pl.ds(r0, quart)
        lo = pl.ds(r0, eighth)
        hi = pl.ds(r0 + eighth, eighth)
        if k < 4:
            to = (1, -1, 2)[k]
            src_d, dst_d, rows, ax = 0, -to, full, 1

            def at(d):
                return blk(h, wrap(p1 + d), p2)
        else:
            src_d, dst_d, rows, to = (
                (0, -1, full, 1),
                (0, 1, full, -1),
                (-1, -2, lo, 1),
                (1, 2, hi, -1),
            )[(k - 4) % 4]
            o = OFFS[(k - 4) // 4]
            ax = 2

            def at(d):
                return blk(h, wrap(p1 + o), wrap(p2 + d))

        return at(src_d), at(dst_d), rows, nb(h, ax, to)

    def ag_send(u, h, k):
        src, _, rows, dev = ag_info(u, h, k)
        ref = agbuf.at[src, rows]
        return rcopy(ref, ref, ag_s.at[u, h, k], ag_r.at[u, h, k], dev)

    def ag_start(u, *ks):
        for k in ks:
            for h in range(2):
                ag_send(u, h, k).start()

    def ag_wait(u, *ks):
        for k in ks:
            for h in range(2):
                _, dst, rows, dev = ag_info(u, h, k)
                ref = agbuf.at[dst, rows]
                rcopy(ref, ref, ag_s.at[u, h, k], ag_r.at[u, h, k], dev).wait_recv()

    def publish(l, u):
        rows = pl.ds(u * half, half)
        own = hid[rows, :].astype(F32)
        gain_row = gain_ref[pl.ds(l, 1), pl.ds(pl.multiple_of(tpi * feat, feat), feat)]
        agbuf[tpi, rows] = (own * gain_row).astype(BF16)
        sqv[rows, :] = jnp.broadcast_to(jnp.sum(own * own, axis=1, keepdims=True), (half, LANE))

    publish(0, 0)
    ag_start(0, 0, 1, 4, 5, 2)

    ei = lax.broadcasted_iota(jnp.int32, (LANE, states * LANE), 0)
    ej = lax.broadcasted_iota(jnp.int32, (LANE, states * LANE), 1) // LANE
    expand_b[...] = jnp.where(ei == ej, 1.0, 0.0).astype(BF16)
    expand_c[...] = jnp.where(ei == ej + states, 1.0, 0.0).astype(BF16)
    grp = 2 * LANE // per_d
    gi = lax.broadcasted_iota(jnp.int32, (2 * LANE, 2 * LANE), 0)
    gj = lax.broadcasted_iota(jnp.int32, (2 * LANE, 2 * LANE), 1)
    seld[...] = jnp.where(gj == lax.rem(gi, grp) * per_d + gi // grp, 1.0, 0.0).astype(BF16)
    sel_w = rank + LANE
    pad_from = rank + 2 * states
    for l in range(layers):
        w_low_v[l, pad_from:, :] = jnp.zeros((sel_w - pad_from, feat), BF16)

    def regroup(b0, b1):
        def one(i, unused):
            r = pl.multiple_of(i * WIDE * 2 * LANE, WIDE * 2 * LANE)
            parts = [raw[pl.ds(r + v * 2 * LANE, 2 * LANE), :] for v in range(WIDE)]
            got = jnp.dot(
                seld[...], jnp.concatenate(parts, axis=1), preferred_element_type=F32
            ).astype(BF16)
            d0 = pl.multiple_of(i * WIDE * grp, WIDE * grp)
            for q in range(per_d):
                cols = pl.ds((q % 2) * chans + (q // 2) * LANE, LANE)
                for v in range(WIDE):
                    w_in_v[pl.ds(d0 + v * grp, grp), cols] = got[
                        q * grp : (q + 1) * grp, v * LANE : (v + 1) * LANE
                    ]
            return unused

        lax.fori_loop(b0, b1, one, 0)

    nreg = n_tp * feat // (WIDE * grp)

    def seq_copy(l, src, dst, ss, rs, q, sending):
        slot = seqi if sending else q
        return rcopy(src, dst.at[l, slot], ss.at[l, q], rs.at[l, slot], {"seq": q})

    def t_copy(l, q, sending):
        return seq_copy(l, tsend.at[l], trecv, t_s, t_r, q, sending)

    def e_copy(l, q, sending):
        return seq_copy(l, esend.at[l], erecv, e_s, e_r, q, sending)

    lo = pl.ds(0, eighth)
    hi = pl.ds(eighth, eighth)

    def rpos(h):
        p2, p1 = pos[h]
        return p1, p2

    def rnb(h, axis, d):
        return nb(h, 3 - axis, d)

    ahead, up, down, here = range(SIDE)
    parts = (pl.ds(0, 2), pl.ds(2, 2))

    def rs_copy(u, h, k):
        if k < 8:
            piece = parts[(k // 2) % 2]
            way = k % 2
            if k < 4:
                src = pbuf.at[u, h, ahead, piece, (lo, hi)[way]]
                dst = x1.at[u, h, way, piece]
            else:
                src = pbuf.at[u, h, (up, down)[way], piece]
                dst = x2.at[u, h, way, piece]
            dev = rnb(h, 1, (1, -1)[way])
        else:
            src = s2.at[u, h, (ahead, up, down)[k - 8]]
            dst = x3.at[u, h, k - 8]
            dev = rnb(h, 2, OUT[k - 8])
        return rcopy(src, dst, rs_s.at[u, h, k], rs_r.at[u, h, k], dev)

    def omm(l, u, pairs):
        lhs = gated[u * half : (u + 1) * half, :]
        for dz, dy in pairs:
            z, y = wrap(zc + dz), wrap(yc + dy)
            cols = pl.ds(pl.multiple_of((z * SIDE + y) * feat, feat), feat)
            val = jnp.dot(lhs, w_out_v[l, :, cols], preferred_element_type=F32).astype(BF16)
            iz, iy = OUT.index(dz), OUT.index(dy)
            pbuf[u, 0, iz, iy] = val[:quart]
            pbuf[u, 1, iy, iz] = val[quart:]

    def rs1(l, u):
        omm(l, u, ((2, 2), (2, 1), (1, 2)))
        for h in range(2):
            rs_copy(u, h, 0).start()
            rs_copy(u, h, 1).start()
        omm(l, u, ((2, -1), (2, 0), (-1, 2), (0, 2)))
        for h in range(2):
            rs_copy(u, h, 2).start()
            rs_copy(u, h, 3).start()
        omm(l, u, ((1, 1), (1, -1), (1, 0), (-1, 1), (-1, -1), (-1, 0), (0, 1), (0, -1)))
        omm(l, u, ((0, 0),))

    def rs2(u):
        for p in range(2):
            piece = parts[p]
            for h in range(2):
                for way in range(2):
                    rows = (lo, hi)[way]
                    side = (up, down)[way]
                    rs_copy(u, h, 2 * p + way).wait_recv()
                    pbuf[u, h, side, piece, rows] = (
                        pbuf[u, h, side, piece, rows].astype(F32) + x1[u, h, way, piece].astype(F32)
                    ).astype(BF16)
                    rs_copy(u, h, 4 + 2 * p + way).start()

    def sum3(u, h, c2):
        return (
            pbuf[u, h, here, c2].astype(F32) + x2[u, h, 0, c2].astype(F32) + x2[u, h, 1, c2].astype(F32)
        )

    def rs3(u):
        for p in range(2):
            for h in range(2):
                rs_copy(u, h, 4 + 2 * p).wait_recv()
                rs_copy(u, h, 5 + 2 * p).wait_recv()
                for c2 in (ahead, up) if p == 0 else (down,):
                    s2[u, h, c2] = sum3(u, h, c2).astype(BF16)
                    rs_copy(u, h, 8 + c2).start()

    def rs4(u):
        for h in range(2):
            total = sum3(u, h, here)
            for k in range(3):
                rs_copy(u, h, 8 + k).wait_recv()
                total = total + x3[u, h, k].astype(F32)
            rows = pl.ds(u * half + h * quart, quart)
            hid[rows, :] = (hid[rows, :].astype(F32) + total).astype(BF16)

    def layer(l, unused):
        low_c, dt_c, in_c, out_c = wcopies(l)
        publish(l, 1)

        low_c.wait()
        selv = lax.dot_general(
            agbuf[tpi], w_low_v[l], (((1,), (1,)), ((), ())), preferred_element_type=F32
        )
        sq = sqv[:, 0:1]
        sq_hi = sq.astype(BF16).astype(F32)
        lane = lax.broadcasted_iota(jnp.int32, (toks, sel_w), 1)
        selv = jnp.where(lane == pad_from, sq_hi, selv)
        selv = jnp.where(lane == pad_from + 1, sq - sq_hi, selv)
        selp[...] = selv.astype(BF16)
        arrecv[tpi] = selp[pl.ds(pl.multiple_of(tpi * arow, arow), arow), :]

        def ar1(d, sending):
            to = lax.rem(tpi + d, n_tp)
            fr = lax.rem(tpi + n_tp - d, n_tp)
            rows = pl.ds(pl.multiple_of(to * arow, arow), arow)
            dst = arrecv.at[tpi] if sending else arrecv.at[fr]
            return rcopy(selp.at[rows], dst, ar1_s.at[d], ar1_r.at[d], {"tp": to})

        for d in range(1, n_tp):
            ar1(d, True).start()
        ag_start(1, 0, 1, 4, 5, 2)

        ag_wait(0, 0, 1)
        ag_start(0, 8, 9, 12, 13)
        ag_wait(0, 4, 5)
        ag_start(0, 6, 7)
        ag_wait(0, 2)
        ag_start(0, 16, 17)

        @pl.when(l == 0)
        def _():
            in_c.wait()
            for c in (first_copies[1], first_copies[3], later_copies[0], later_copies[1], later_copies[3]):
                c.start()
            regroup(0, nreg // 4)

        for d in range(1, n_tp):
            ar1(d, False).wait_recv()
        tot = jnp.zeros((arow, sel_w), F32)
        for i in range(n_tp):
            tot = tot + arrecv[i].astype(F32)
        lane = lax.broadcasted_iota(jnp.int32, (arow, sel_w), 1)
        is_sq = (lane == pad_from) | (lane == pad_from + 1)
        ssum = jnp.sum(jnp.where(is_sq, tot, 0.0), axis=1, keepdims=True)
        factor = lax.rsqrt(ssum / (n_tp * feat) + 1e-05)
        f_hi = factor.astype(BF16).astype(F32)
        tot = jnp.where(lane == pad_from, f_hi, jnp.where(lane == pad_from + 1, factor - f_hi, tot * factor))
        mine = pl.ds(pl.multiple_of(tpi * arow, arow), arow)
        arres[mine, :] = tot.astype(BF16)

        def ar2(d, sending):
            to = lax.rem(tpi + d, n_tp)
            fr = lax.rem(tpi + n_tp - d, n_tp)
            base = tpi if sending else fr
            rows = pl.ds(pl.multiple_of(base * arow, arow), arow)
            return rcopy(arres.at[rows], arres.at[rows], ar2_s.at[d], ar2_r.at[d], {"tp": to})

        for d in range(1, n_tp):
            ar2(d, True).start()

        ag_wait(0, 8, 9)
        ag_start(0, 10, 11)
        ag_wait(0, 12, 13)
        ag_start(0, 14, 15)
        ag_wait(0, 16, 17)
        ag_start(0, 18, 19)
        ag_wait(1, 0, 1)
        ag_start(1, 8, 9, 12, 13)
        ag_wait(1, 4, 5)
        ag_start(1, 6, 7)
        ag_wait(1, 2)
        ag_start(1, 16, 17)

        @pl.when(l == 0)
        def _():
            regroup(nreg // 4, nreg // 2)

        ag_wait(1, 8, 9)
        ag_start(1, 10, 11)
        ag_wait(1, 12, 13)
        ag_start(1, 14, 15)
        ag_wait(1, 16, 17)
        ag_start(1, 18, 19)

        @pl.when(l == 0)
        def _():
            regroup(nreg // 2, nreg)
            later_copies[2].start()

        def mm(u, first, pairs):
            rs = pl.ds(u * half, half)
            for i, (dz, dy) in enumerate(pairs):
                b = wrap(zc + dz) * SIDE + wrap(yc + dy)
                rows = pl.ds(pl.multiple_of(b * feat, feat), feat)
                val = jnp.dot(agbuf[b, rs], w_in_v[rows, :], preferred_element_type=F32)
                if first and i == 0:
                    proj[rs, :] = val
                else:
                    proj[rs, :] += val

        near = ((0, 0), (0, 1), (0, -1), (1, 0), (-1, 0), (1, 1), (1, -1), (-1, 1), (-1, -1))
        away = ((2, 0), (2, 1), (2, 2), (2, 3), (0, 2), (1, 2), (3, 2))

        mm(0, True, near)
        ag_wait(0, 6, 7, 10, 11, 14, 15, 18, 19)
        mm(0, False, away)
        mm(1, True, near)
        for d in range(1, n_tp):
            ar2(d, False).wait_recv()
        tail = arres[:, rank:]
        tl = lax.broadcasted_iota(jnp.int32, (toks, LANE), 1)
        in_f = (tl == 2 * states) | (tl == 2 * states + 1)
        fac = jnp.sum(jnp.where(in_f, tail.astype(F32), 0.0), axis=1, keepdims=True)
        dt_c.wait()
        pre = jnp.dot(arres[:, :rank], w_dt_v[l], preferred_element_type=F32) + bias_ref[pl.ds(l, 1), :]
        step[...] = jnp.maximum(pre, 0.0) + jnp.log1p(jnp.exp(-jnp.abs(pre)))
        bx[...] = jnp.dot(tail, expand_b[...], preferred_element_type=F32)
        cx[...] = jnp.dot(tail, expand_c[...], preferred_element_type=F32)

        def accum(t, run):
            rows = pl.ds(pl.multiple_of(t * SUB, SUB), SUB)
            run = run + step[rows, :]
            cum[rows, :] = run
            return run

        ctot = lax.fori_loop(0, steps, accum, jnp.zeros((SUB, chans), F32))
        tsend[l] = jnp.broadcast_to(jnp.sum(ctot, axis=0, keepdims=True), (SUB, chans))
        for q in range(1, n_seq):
            @pl.when(q > seqi)
            def _():
                t_copy(l, q, True).start()

        skip_row = skip_ref[pl.ds(l, 1), :]
        th_row = thresh_ref[pl.ds(l, 1), :]

        def scan(u):
            for cb in range(ncb):
                cs = pl.ds(cb * LANE, LANE)
                na = [
                    jnp.broadcast_to(a_ref[l, s : s + 1, cs] * (-LOG2E), (SUB, LANE))
                    for s in range(states)
                ]
                skip = skip_row[:, cb * LANE : (cb + 1) * LANE]

                def scan_step(t, hs):
                    rows = pl.ds(pl.multiple_of(t * SUB, SUB), SUB)
                    st = step[rows, cs]
                    cur = proj[rows, cs]
                    dr = st * cur
                    acc = skip * cur
                    new = []
                    for s in range(states):
                        ls = pl.ds(s * LANE, LANE)
                        hn = jnp.exp2(st * na[s]) * hs[s] + bx[rows, ls] * dr
                        acc = acc + cx[rows, ls] * hn
                        new.append(hn)
                    yv[rows, cs] = acc
                    return tuple(new)

                if u == 0:
                    init = tuple(jnp.zeros((SUB, LANE), F32) for _ in range(states))
                else:
                    init = tuple(hst[s, :, cs] for s in range(states))
                hs = lax.fori_loop(u * steps // 2, (u + 1) * steps // 2, scan_step, init, unroll=2)
                if u == 0:
                    for s in range(states):
                        hst[s, :, cs] = hs[s]
                    continue
                sub = lax.broadcasted_iota(jnp.int32, (SUB, LANE), 0)
                ct = cum[pl.ds((steps - 1) * SUB, SUB), cs]
                for s in range(states):
                    e = hs[s]
                    p = jnp.exp2(ct * na[s])
                    for d in (1, 2, 4):
                        ok = sub >= d
                        e = e + jnp.where(ok, p * pltpu.roll(e, d, 0), 0.0)
                        p = p * jnp.where(ok, pltpu.roll(p, d, 0), 1.0)
                    esend_f[s : s + 1, cs] = e[SUB - 1 : SUB, :]
                    ein[s, :, cs] = jnp.where(sub >= 1, pltpu.roll(e, 1, 0), 0.0)
                    pin[s, :, cs] = jnp.where(sub >= 1, pltpu.roll(p, 1, 0), 1.0)

        proj[:half, :] = proj[:half, :] * fac[:half]
        scan(0)
        ag_wait(1, 6, 7, 10, 11, 14, 15, 18, 19)
        mm(1, False, away)
        proj[half:, :] = proj[half:, :] * fac[half:]
        scan(1)

        esend[l] = esend_f[...].astype(BF16)
        for q in range(1, n_seq):
            @pl.when(q > seqi)
            def _():
                e_copy(l, q, True).start()

        for u in range(2):
            for k in AG_KEYS:
                for h in range(2):
                    ag_send(u, h, k).wait_send()
        for d in range(1, n_tp):
            ar1(d, True).wait_send()
            ar2(d, True).wait_send()

        rates = a_ref[l] * (-LOG2E)
        for q in range(n_seq - 1):
            @pl.when(q < seqi)
            def _():
                t_copy(l, q, False).wait_recv()
                hdec[q] = jnp.exp2(rates * trecv[l, q, 0:1, :])

        hdev[...] = jnp.zeros_like(hdev)
        for q in range(n_seq - 1):
            @pl.when(q < seqi)
            def _():
                e_copy(l, q, False).wait_recv()
                hdev[...] = hdec[q] * hdev[...] + erecv[l, q].astype(F32)

        def finish(u, c0, c1):
            rs = pl.ds(u * half, half)
            for cb in range(c0, c1):
                cs = pl.ds(cb * LANE, LANE)
                na = [
                    jnp.broadcast_to(a_ref[l, s : s + 1, cs] * (-LOG2E), (SUB, LANE))
                    for s in range(states)
                ]
                hin = [ein[s, :, cs] + pin[s, :, cs] * hdev[s : s + 1, cs] for s in range(states)]
                th = th_row[:, cb * LANE : (cb + 1) * LANE]

                def fold(t, unused):
                    rows = pl.ds(pl.multiple_of(t * SUB, SUB), SUB)
                    ct = cum[rows, cs]
                    acc = yv[rows, cs]
                    for s in range(states):
                        ls = pl.ds(s * LANE, LANE)
                        acc = acc + cx[rows, ls] * (jnp.exp2(ct * na[s]) * hin[s])
                    yv[rows, cs] = acc
                    return unused

                lax.fori_loop(u * steps // 2, (u + 1) * steps // 2, fold, 0, unroll=4)

                mixed = yv[rs, cs]
                fct = lax.rsqrt(jnp.mean(mixed * mixed, axis=1, keepdims=True) + 1e-05)
                normal = mixed * fct
                shrunk = jnp.maximum(normal - th, 0.0) - jnp.maximum(-normal - th, 0.0)
                gate = proj[rs, pl.ds(chans + cb * LANE, LANE)]
                gated[rs, cs] = (shrunk * (gate / (1.0 + jnp.exp(-gate)))).astype(BF16)

        finish(0, 0, ncb)
        out_c.wait()
        rs1(l, 0)
        finish(1, 0, ncb // 2)
        rs2(0)
        finish(1, ncb // 2, ncb)
        rs1(l, 1)

        @pl.when(l + 1 < layers)
        def _():
            later_copies[2].wait()
            regroup(0, nreg // 8)

        rs2(1)
        rs3(0)

        @pl.when(l + 1 < layers)
        def _():
            regroup(nreg // 8, nreg // 2)

        rs4(0)

        @pl.when(l + 1 < layers)
        def _():
            publish(l + 1, 0)
            ag_start(0, 0, 1, 4, 5, 2)

        rs3(1)

        @pl.when(l + 1 < layers)
        def _():
            regroup(nreg // 2, nreg)

        rs4(1)
        for u in range(2):
            for h in range(2):
                for k in range(11):
                    rs_copy(u, h, k).wait_send()
        for q in range(1, n_seq):
            @pl.when(q > seqi)
            def _():
                t_copy(l, q, True).wait_send()
                e_copy(l, q, True).wait_send()
        return unused

    lax.fori_loop(0, layers, layer, 0)
    out_ref[...] = lax.dot_general(
        perm, hid[...], (((0,), (0,)), ((), ())), preferred_element_type=F32
    ).astype(BF16)


def per_device(n_seq, tokens, norm_gain, w_in, w_low, w_dt, a_rate, dt_bias, skip_gain, threshold, w_out):
    toks, feat = tokens.shape
    layers, model, _, chans = w_in.shape
    states = a_rate.shape[1]
    rank = w_dt.shape[1]
    n_tp = SIDE * SIDE
    half, quart, eighth = toks // 2, toks // 4, toks // 8
    per_d = 2 * chans // LANE
    sel_w = rank + LANE
    dims = (layers, n_seq, toks, feat, chans, states, rank)
    vm = pl.BlockSpec(memory_space=pltpu.VMEM)
    hb = pl.BlockSpec(memory_space=pl.ANY)
    dma = pltpu.SemaphoreType.DMA
    V = pltpu.VMEM
    return pl.pallas_call(
        functools.partial(kernel_body, dims),
        out_shape=jax.ShapeDtypeStruct((toks, feat), BF16),
        in_specs=[vm, vm, hb, hb, hb, vm, vm, vm, vm, hb],
        out_specs=vm,
        scratch_shapes=[
            V((model * per_d, LANE), BF16),
            V((2 * LANE, 2 * LANE), BF16),
            V((model, 2 * chans), BF16),
            V((layers, sel_w, feat), BF16),
            V((layers, rank, chans), BF16),
            V((layers, chans, model), BF16),
            V((toks, feat), BF16),
            V((n_tp, toks, feat), BF16),
            V((toks, LANE), F32),
            V((toks, sel_w), BF16),
            V((n_tp, toks // n_tp, sel_w), BF16),
            V((toks, sel_w), BF16),
            V((LANE, states * LANE), BF16),
            V((LANE, states * LANE), BF16),
            V((toks, states * LANE), F32),
            V((toks, states * LANE), F32),
            V((toks, chans), F32),
            V((toks, chans), F32),
            V((toks, 2 * chans), F32),
            V((toks, chans), F32),
            V((states, SUB, chans), F32),
            V((states, SUB, chans), F32),
            V((states, SUB, chans), F32),
            V((states, chans), F32),
            V((n_seq, states, chans), F32),
            V((states, chans), F32),
            V((layers, states, chans), BF16),
            V((layers, n_seq, states, chans), BF16),
            V((layers, SUB, chans), F32),
            V((layers, n_seq, SUB, chans), F32),
            V((toks, chans), BF16),
            V((2, 2, SIDE, SIDE, quart, feat), BF16),
            V((2, 2, 2, SIDE, eighth, feat), BF16),
            V((2, 2, 2, SIDE, quart, feat), BF16),
            V((2, 2, SIDE, quart, feat), BF16),
            V((2, 2, 3, quart, feat), BF16),
            dma((layers, 4)),
            dma((2, 2, 20)),
            dma((2, 2, 20)),
            dma((n_tp,)),
            dma((n_tp,)),
            dma((n_tp,)),
            dma((n_tp,)),
            dma((layers, n_seq)),
            dma((layers, n_seq)),
            dma((layers, n_seq)),
            dma((layers, n_seq)),
            dma((2, 2, 11)),
            dma((2, 2, 11)),
        ],
        compiler_params=pltpu.CompilerParams(
            collective_id=0, has_side_effects=True, vmem_limit_bytes=60 * 1024 * 1024
        ),
    )(
        tokens,
        norm_gain,
        jnp.swapaxes(w_in.reshape(layers, model, 2, chans // LANE, LANE), 2, 3).reshape(
            layers, model * per_d, LANE
        ),
        jnp.swapaxes(w_low, 1, 2),
        w_dt,
        a_rate,
        dt_bias,
        skip_gain,
        threshold,
        w_out,
    )


def solution(mesh):
    in_specs = (
        P("seq", "tp"),
        P(),
        P(None, None, None, "tp"),
        P(None, "tp", None),
        P(None, None, "tp"),
        P(None, None, "tp"),
        P(None, "tp"),
        P(None, "tp"),
        P(None, "tp"),
        P(None, "tp", None),
    )
    return jax.shard_map(
        functools.partial(per_device, mesh.shape["seq"]),
        mesh=mesh,
        in_specs=in_specs,
        out_specs=P("seq", "tp"),
        check_vma=False,
    )
```
